256 devices in a mesh: gx: 8 (over y, core), gy: 32 (over z, x).
Axes of the slice: x: 4, y: 4, z: 8, core: 2. Of those that a mesh axis runs over, the one named last changes fastest.
Arguments:
- right_side: float32 [256, 512, 256], P('gx', 'gy'), may hold values from -8 to 8
- coefficient: float32 [256, 512, 256], P('gx', 'gy'), may hold values from 0.1 to 10
Outputs:
- solution_field: float32 [256, 512, 256], P('gx', 'gy')
- residual: float32 [256, 512, 256], P('gx', 'gy')
The draws below stay inside these ranges and needn't reach their ends.
All inputs are finite; a program needn't handle non-finite values.
Results may differ from the reference program's by a relative error of at most 0.0003.
Values sent between devices are 32-bit elements; how exact they have to be, the bound alone decides.
A program may use at most 128 MiB of HBM per device.

```python
import math
from functools import partial
import jax
import jax.numpy as jnp

NZ = 256
LEVELS = 5
PRE = 2
POST = 2
BOTTOM = 8
NX = 256
NY = 512


def draw_right_side(key, part):
    values = jax.random.normal(key, (NX, NY, NZ), jnp.float32)
    return jnp.clip(values, -8.0, 8.0)


def levels(stream_key, extent, shards, low, largest):
    level, own = 1.0, jax.random.fold_in(stream_key, 6)
    for dim, blocks in shards:
        heights = jnp.exp(jax.random.uniform(jax.random.fold_in(own, dim), (blocks,), jnp.float32, low / len(shards), largest / len(shards)))
        level = level * jnp.repeat(heights, extent[dim] // blocks).reshape([-1 if axis == dim else 1 for axis in range(len(extent))])
    return level


def setup_inputs(seed: int = 0) -> dict:
    key_of = jax.random.split(jax.random.key(seed), 3)
    right_side = draw_right_side(jax.random.fold_in(key_of[2], 71), 0)
    coefficient = jnp.clip(jnp.exp(math.log(10.0) - 4.6051702 * jax.random.uniform(key_of[1], (NX, NY, NZ), jnp.float32) ** levels(key_of[1], (NX, NY, NZ), ((0, 8), (1, 32)), -0.2, 0.2)), 0.1, 10.0)
    return dict(right_side=right_side, coefficient=coefficient)


SMOOTH_LO = 0.5
SMOOTH_HI = 2.0
COARSE_LO = 0.05
COARSE_HI = 2.0


def harmonic(own, other):
    return 2.0 * own * other / (own + other)


def face_weights(conduct, padded):
    lower_x = jnp.where(padded[:-2, 1:-1, :] > 0.0, padded[:-2, 1:-1, :], conduct)
    upper_x = jnp.where(padded[2:, 1:-1, :] > 0.0, padded[2:, 1:-1, :], conduct)
    lower_y = jnp.where(padded[1:-1, :-2, :] > 0.0, padded[1:-1, :-2, :], conduct)
    upper_y = jnp.where(padded[1:-1, 2:, :] > 0.0, padded[1:-1, 2:, :], conduct)
    edged = jnp.pad(conduct, ((0, 0), (0, 0), (1, 1)), mode="edge")
    lower_z = edged[:, :, :-2]
    upper_z = edged[:, :, 2:]
    faces = [harmonic(conduct, other) for other in (lower_x, upper_x, lower_y, upper_y, lower_z, upper_z)]
    total = faces[0] + faces[1] + faces[2] + faces[3] + faces[4] + faces[5]
    return tuple(faces) + (total,)


def stencil(field, padded, weights, scale):
    zpad = jnp.pad(field, ((0, 0), (0, 0), (1, 1)))
    beside = weights[0] * padded[:-2, 1:-1, :] + weights[1] * padded[2:, 1:-1, :]
    beside = beside + weights[2] * padded[1:-1, :-2, :] + weights[3] * padded[1:-1, 2:, :]
    beside = beside + weights[4] * zpad[:, :, :-2] + weights[5] * zpad[:, :, 2:]
    return scale * (weights[6] * field - beside)


def pad_plane(field):
    return jnp.pad(field, ((1, 1), (1, 1), (0, 0)))


def whole_operate(field, weights, scale):
    return stencil(field, pad_plane(field), weights, scale)


def chebyshev(source, start, sweeps, low_end, high_end, operate, inverse):
    theta_val = (high_end + low_end) / 2.0
    half_width = (high_end - low_end) / 2.0
    sigma_val = theta_val / half_width
    rho_now = 1.0 / sigma_val
    if start is None:
        update = inverse * source / theta_val
        iterate = update
    else:
        update = inverse * (source - operate(start)) / theta_val
        iterate = start + update
    for sweep_index in range(sweeps - 1):
        rho_next = 1.0 / (2.0 * sigma_val - rho_now)
        update = rho_next * rho_now * update + (2.0 * rho_next / half_width) * inverse * (source - operate(iterate))
        iterate = iterate + update
        rho_now = rho_next
    return iterate


def restrict(field):
    size_x, size_y, size_z = field.shape
    return jnp.mean(field.reshape(size_x // 2, 2, size_y // 2, 2, size_z // 2, 2), axis=(1, 3, 5))


def prolong(field):
    size_x, size_y, size_z = field.shape
    grown = jnp.broadcast_to(field[:, None, :, None, :, None], (size_x, 2, size_y, 2, size_z, 2))
    return grown.reshape(2 * size_x, 2 * size_y, 2 * size_z)


def cycle(level_index, source, conduct):
    weights = face_weights(conduct, pad_plane(conduct))
    scale = 0.25 ** level_index
    inverse = 1.0 / (scale * weights[6])
    operate = partial(whole_operate, weights=weights, scale=scale)
    if level_index == LEVELS - 1:
        return chebyshev(source, None, BOTTOM, COARSE_LO, COARSE_HI, operate, inverse)
    iterate = chebyshev(source, None, PRE, SMOOTH_LO, SMOOTH_HI, operate, inverse)
    coarse = restrict(source - operate(iterate))
    iterate = iterate + prolong(cycle(level_index + 1, coarse, restrict(conduct)))
    return chebyshev(source, iterate, POST, SMOOTH_LO, SMOOTH_HI, operate, inverse)


def reference(right_side, coefficient):
    solution_field = cycle(0, right_side, coefficient)
    weights = face_weights(coefficient, pad_plane(coefficient))
    residual = right_side - whole_operate(solution_field, weights, 1.0)
    return solution_field, residual
```

```python
import functools

import jax
import jax.numpy as jnp
from jax import lax
from jax.experimental import pallas as pl
from jax.experimental.pallas import tpu as pltpu
from jax.sharding import PartitionSpec as P

MESH = pl.DeviceIdType.MESH
F32 = jnp.float32

SMOOTH_LO, SMOOTH_HI = 0.5, 2.0
COARSE_LO, COARSE_HI = 0.05, 2.0
BOTTOM = 8

STEPS = ((0, 1), (0, -1), (1, 0), (-1, 0), (1, 1), (1, -1), (-1, 1), (-1, -1))


def coefficients(low, high, sweeps):
    theta = (high + low) / 2.0
    delta = (high - low) / 2.0
    sigma = theta / delta
    rho = 1.0 / sigma
    pairs = []
    for _ in range(sweeps - 1):
        rho_next = 1.0 / (2.0 * sigma - rho)
        pairs.append((rho_next * rho, 2.0 * rho_next / delta))
        rho = rho_next
    return theta, pairs


THETA, ((MOMENTUM, STEP),) = coefficients(SMOOTH_LO, SMOOTH_HI, 2)


def harmonic(own, other):
    return 2.0 * own * other / (own + other)


def roll(value, shift, axis):
    size = value.shape[axis]
    return pltpu.roll(value, shift % size, axis)


def iota(shape, dim):
    return lax.broadcasted_iota(jnp.int32, shape, dim)


def times(rows, matrix):
    return jnp.dot(rows, matrix, precision=lax.Precision.HIGHEST, preferred_element_type=F32)


def loop(start, stop, body):
    def step(index, carry):
        body(index)
        return carry

    lax.fori_loop(start, stop, step, 0)


class Exchange:
    def __init__(self, field, left, right, send, recv, halo, depth):
        self.field, self.left, self.right = field, left, right
        self.send, self.recv = send, recv
        self.halo, self.depth = halo, depth
        self.planes = field.shape[0] - 2 * halo
        self.rows = field.shape[1] - 8

    def copies(self, place):
        h, n, r, x = self.halo, self.planes, self.depth, self.rows
        found = []
        for number, (dx, dy) in enumerate(STEPS):
            if dx == 0:
                source_plane = h + n - r if dy > 0 else h
                target_plane = h - r if dy > 0 else h + n
                source = self.field.at[pl.ds(source_plane, r), pl.ds(0, x)]
                target = self.field.at[pl.ds(target_plane, r), pl.ds(0, x)]
            else:
                count = n if dy == 0 else r - 1
                source_plane = h if dy <= 0 else h + n - count
                target_plane = h if dy == 0 else (h - count if dy > 0 else h + n)
                source = self.field.at[pl.ds(source_plane, count), pl.ds(x - 8 if dx > 0 else 0, 8)]
                landing = self.left if dx > 0 else self.right
                target = landing.at[pl.ds(target_plane, count)]
            found.append(
                pltpu.make_async_remote_copy(
                    src_ref=source,
                    dst_ref=target,
                    send_sem=self.send.at[number],
                    recv_sem=self.recv.at[number],
                    device_id=place(dx, dy),
                    device_id_type=MESH,
                )
            )
        return found

    def start(self, place):
        self.started = self.copies(place)
        for copy in self.started:
            copy.start()

    def arrive(self, which):
        for number in which:
            self.started[number].wait_recv()

    def merge(self, start, stop):
        x = self.rows
        shape = (8, self.field.shape[2])

        def body(p):
            upper = iota(shape, 0) < 4
            self.field[p, x:, :] = jnp.where(upper, self.right[p], self.left[p])

        loop(start, stop, body)

    def sent(self):
        for copy in self.started:
            copy.wait_send()


class Level:
    def __init__(self, number, lanes, refs, gx, gy, counts):
        self.scale = 0.25**number
        self.lanes = lanes
        self.gx, self.gy = gx, gy
        self.count_x, self.count_y = counts
        (self.k, self.b, self.xh, self.x1, self.x2, self.wx, self.wy, self.wz, self.w, self.inv, self.z0, self.z1) = refs
        self.h = self.k.halo
        self.n = self.k.planes
        self.x = self.k.rows
        self.shape = (self.x + 8, 128 * ((lanes + 127) // 128))
        self.period = lanes

    def row_ok(self):
        row = iota(self.shape, 0)
        below = jnp.where(self.gx == 0, 1, 0)
        above = jnp.where(self.gx == self.count_x - 1, 1, 0)
        bad_low = jnp.where(row >= self.x + 4, below, 0)
        bad_high = jnp.where((row >= self.x) & (row < self.x + 4), above, 0)
        return (bad_low + bad_high) == 0

    def plane_ok(self, p):
        y = self.gy * self.n + p - self.h
        return (y >= 0) & (y < self.count_y * self.n)

    def mend(self, start, stop):
        field, x = self.k.field, self.x
        tile = (8, self.shape[1])

        @pl.when(self.gx == self.count_x - 1)
        def _():
            def body(p):
                own = roll(field[p, x - 8 : x, :], 1, 0)
                field[p, x:, :] = jnp.where(iota(tile, 0) == 0, own, field[p, x:, :])

            loop(start, stop, body)

        @pl.when(self.gx == 0)
        def _():
            def body(p):
                own = roll(field[p, 0:8, :], 7, 0)
                field[p, x:, :] = jnp.where(iota(tile, 0) == 7, own, field[p, x:, :])

            loop(start, stop, body)

    def mend_planes(self):
        field, h, n = self.k.field, self.h, self.n

        @pl.when(self.gy == 0)
        def _():
            field[h - 1] = field[h]

        @pl.when(self.gy == self.count_y - 1)
        def _():
            field[h + n] = field[h + n - 1]

    def lane(self):
        return iota(self.shape, 1) % self.period

    def faces(self, start, stop):
        k = self.k.field

        def body(p):
            own = k[p]
            self.wx[p] = harmonic(own, roll(own, -1, 0))
            along = harmonic(own, roll(own, -1, 1))
            self.wz[p] = jnp.where(self.lane() == self.period - 1, 0.0, along)

        loop(start, stop, body)

    def faces_y(self, start, stop):
        k = self.k.field

        def body(p):
            self.wy[p] = harmonic(k[p], k[p + 1])

        loop(start, stop, body)

    def totals(self, start, stop):
        k = self.k.field

        def body(p):
            wx, wz = self.wx[p], self.wz[p]
            lane = self.lane()
            edge = jnp.where((lane == 0) | (lane == self.period - 1), k[p], 0.0)
            total = wx + roll(wx, 1, 0) + self.wy[p] + self.wy[p - 1] + wz + roll(wz, 1, 1) + edge
            self.w[p] = total
            ok = self.row_ok() & self.plane_ok(p)
            self.inv[p] = jnp.where(ok, 1.0 / total, 0.0)

        loop(start, stop, body)

    def beside(self, field, p):
        own, wx, wz = field[p], self.wx[p], self.wz[p]
        found = wx * roll(own, -1, 0) + roll(wx * own, 1, 0)
        found = found + self.wy[p] * field[p + 1] + self.wy[p - 1] * field[p - 1]
        return found + wz * roll(own, -1, 1) + roll(wz * own, 1, 1)

    def first(self, start, stop):
        b = self.b.field

        def body(p):
            self.x1[p] = b[p] * self.inv[p] * (1.0 / (THETA * self.scale))

        loop(start, stop, body)

    def second(self):
        h, n, x = self.h, self.n, self.x

        def body(p):
            own = self.x1[p]
            factor = 1.0 + MOMENTUM + STEP * (THETA - 1.0)
            self.x2[p] = factor * own + STEP * (self.inv[p] * self.beside(self.x1, p))

        loop(h - 1, h + n + 1, body)

        def keep(p):
            self.xh.field[p, 0:x, :] = self.x2[p, 0:x, :]

        loop(h, h + n, keep)

    def residual(self, field, p):
        return self.b.field[p] - self.scale * (self.w[p] * field[p] - self.beside(field, p))

    def correct(self, p, grown):
        ok = self.row_ok() & self.plane_ok(p)
        self.z0[p] = jnp.where(ok, self.xh.field[p] + grown, 0.0)

    def third(self, start, stop):
        def body(p):
            own = self.z0[p]
            flow = self.inv[p] * self.beside(self.z0, p)
            self.z1[p] = (1.0 - 1.0 / THETA) * own + self.x1[p] + (1.0 / THETA) * flow

        loop(start, stop, body)

    def fourth(self, start, stop, target):
        def body(p):
            own = self.z1[p]
            flow = self.inv[p] * self.beside(self.z1, p)
            found = (1.0 + MOMENTUM - STEP) * own - MOMENTUM * self.z0[p]
            target[p] = found + (STEP * THETA) * self.x1[p] + STEP * flow

        loop(start, stop, body)


class Whole:
    def __init__(self, number, size_z, per_block, refs):
        self.scale = 0.25**number
        self.size_z, self.per_block = size_z, per_block
        self.k, self.b, self.x1, self.x2, self.wx, self.wy, self.wz, self.w, self.inv, self.z0, self.z1 = refs
        self.count = self.k.shape[0] - 2
        self.shape = self.k.shape[1:]
        self.period = size_z * per_block

    def lane(self):
        return iota(self.shape, 1) % self.period

    def blank(self):
        for ref in (self.k, self.x1, self.x2, self.wx, self.z0, self.z1):
            ref[0] = jnp.zeros(self.shape, F32)
            ref[self.count + 1] = jnp.zeros(self.shape, F32)

    def after(self, ref, g):
        inner = self.lane() < self.period - self.size_z
        return jnp.where(inner, roll(ref[g], -self.size_z, 1), roll(ref[g + 1], -self.size_z, 1))

    def before(self, own, previous):
        inner = self.lane() >= self.size_z
        return jnp.where(inner, roll(own, self.size_z, 1), roll(previous, self.size_z, 1))

    def weights(self):
        rows = self.shape[0]

        def faces(g):
            own = self.k[g]
            lane, row = self.lane(), iota(self.shape, 0)
            end = jnp.where(lane >= self.period - self.size_z, jnp.where(g == self.count, 1, 0), 0)
            self.wx[g] = jnp.where(end == 1, 0.0, harmonic(own, self.after(self.k, g)))
            self.wy[g] = jnp.where(row == rows - 1, 0.0, harmonic(own, roll(own, -1, 0)))
            self.wz[g] = jnp.where(lane % self.size_z == self.size_z - 1, 0.0, harmonic(own, roll(own, -1, 1)))

        loop(1, self.count + 1, faces)

        def totals(g):
            lane, row = self.lane(), iota(self.shape, 0)
            high = jnp.where(lane >= self.period - self.size_z, jnp.where(g == self.count, 1.0, 0.0), 0.0)
            low = jnp.where(lane < self.size_z, jnp.where(g == 1, 1.0, 0.0), 0.0)
            edge = high + low
            edge = edge + jnp.where((row == 0) | (row == rows - 1), 1.0, 0.0)
            z = lane % self.size_z
            edge = edge + jnp.where((z == 0) | (z == self.size_z - 1), 1.0, 0.0)
            wx, wy, wz = self.wx[g], self.wy[g], self.wz[g]
            total = wx + self.before(wx, self.wx[g - 1]) + wy + roll(wy, 1, 0) + wz + roll(wz, 1, 1)
            total = total + edge * self.k[g]
            self.w[g] = total
            self.inv[g] = 1.0 / total

        loop(1, self.count + 1, totals)

    def beside(self, field, g):
        own, wx, wy, wz = field[g], self.wx[g], self.wy[g], self.wz[g]
        found = wx * self.after(field, g) + self.before(wx * own, self.wx[g - 1] * field[g - 1])
        found = found + wy * roll(own, -1, 0) + roll(wy * own, 1, 0)
        return found + wz * roll(own, -1, 1) + roll(wz * own, 1, 1)

    def down(self):
        def first(g):
            self.x1[g] = self.b[g] * self.inv[g] * (1.0 / (THETA * self.scale))

        loop(1, self.count + 1, first)

        def second(g):
            factor = 1.0 + MOMENTUM + STEP * (THETA - 1.0)
            self.x2[g] = factor * self.x1[g] + STEP * (self.inv[g] * self.beside(self.x1, g))

        loop(1, self.count + 1, second)

    def residual(self, g):
        return self.b[g] - self.scale * (self.w[g] * self.x2[g] - self.beside(self.x2, g))

    def up(self, target):
        def third(g):
            own = self.z0[g]
            flow = self.inv[g] * self.beside(self.z0, g)
            self.z1[g] = (1.0 - 1.0 / THETA) * own + self.x1[g] + (1.0 / THETA) * flow

        loop(1, self.count + 1, third)

        def fourth(g):
            flow = self.inv[g] * self.beside(self.z1, g)
            found = (1.0 + MOMENTUM - STEP) * self.z1[g] - MOMENTUM * self.z0[g]
            target(g, found + (STEP * THETA) * self.x1[g] + STEP * flow)

        loop(1, self.count + 1, fourth)

    def bottom(self):
        theta, pairs = coefficients(COARSE_LO, COARSE_HI, BOTTOM)

        def first(g):
            scaled = self.b[g] * self.inv[g] * (1.0 / self.scale)
            self.x2[g] = scaled
            self.x1[g] = scaled * (1.0 / theta)
            self.z0[g] = scaled * (1.0 / theta)

        loop(1, self.count + 1, first)
        now, later = self.z0, self.z1
        for momentum, step in pairs:

            def sweep(g, now=now, later=later, momentum=momentum, step=step):
                own = now[g]
                flow = self.inv[g] * self.beside(now, g)
                update = momentum * self.x1[g] + step * (self.x2[g] - own + flow)
                self.x1[g] = update
                later[g] = own + update

            loop(1, self.count + 1, sweep)
            now, later = later, now
        return now


def shrink_lanes(lanes, kept):
    row, col = iota((lanes, 128), 0), iota((lanes, 128), 1)
    return jnp.where(row // 2 == col % kept, 0.125, 0.0).astype(F32)


def grow_lanes(kept, lanes):
    row, col = iota((128, lanes), 0), iota((128, lanes), 1)
    period = 2 * kept
    return jnp.where((col % period) // 2 == row, 1.0, 0.0).astype(F32)


def halve_rows(pair, scratch, rows):
    parts = []
    for part in range(pair.shape[1] // 128):
        scratch[part, 0:rows, :] = pair[:, part * 128 : (part + 1) * 128]
    for part in range(pair.shape[1] // 128):
        even = scratch[part, pl.ds(0, rows // 2, stride=2), :]
        odd = scratch[part, pl.ds(1, rows // 2, stride=2), :]
        parts.append(even + odd)
    return parts[0] if len(parts) == 1 else jnp.concatenate(parts, axis=1)


def restrict(read, target, fine_plane, coarse_plane, rows, lanes, kept, scratch):
    matrix = shrink_lanes(128 * ((lanes + 127) // 128), kept)
    if lanes < 128:
        matrix = jnp.where(iota(matrix.shape, 0) < lanes, matrix, 0.0)
    target_rows = rows // 2

    def body(j):
        pair = read(fine_plane + 2 * j) + read(fine_plane + 2 * j + 1)
        target[coarse_plane + j, 0:target_rows, :] = times(halve_rows(pair, scratch, rows), matrix)

    return body


def double_rows(value, scratch, rows):
    own = 2 * (rows - 8)
    parts = []
    for part in range(value.shape[1] // 128):
        piece = value[:, part * 128 : (part + 1) * 128]
        scratch[part, pl.ds(0, rows, stride=2), :] = piece
        scratch[part, pl.ds(1, rows, stride=2), :] = piece
    for part in range(value.shape[1] // 128):
        upper = iota((8, 128), 0) < 4
        low, high = scratch[part, own : own + 8, :], scratch[part, own + 8 : own + 16, :]
        tail = jnp.where(upper, low, high)
        parts.append(jnp.concatenate([scratch[part, 0:own, :], tail], axis=0))
    return parts[0] if len(parts) == 1 else jnp.concatenate(parts, axis=1)


def kernel(count_x, count_y, names, *refs):
    r = dict(zip(names, refs))
    gx, gy = lax.axis_index("gx"), lax.axis_index("gy")
    ring_x = 4
    ring_z = count_y // ring_x
    chip_x, chip_z = gy % ring_x, gy // ring_x

    def place(dx, dy):
        return ((gx + dx + count_x) % count_x, (gy + dy + count_y) % count_y)

    def along_x(d):
        return (gx, chip_z * ring_x + (chip_x + d) % ring_x)

    def along_z(d):
        return (gx, ((chip_z + d) % ring_z) * ring_x + chip_x)

    def along_gx(d):
        return ((gx + d) % count_x, gy)

    partners = [place(dx, dy) for dx, dy in STEPS]
    partners += [along_x(d) for d in range(1, ring_x)]
    partners += [along_z(d) for d in range(1, ring_z)]
    partners += [along_gx(d) for d in range(1, count_x)]

    load_k = pltpu.make_async_copy(r["coefficient"], r["k_in"], r["load"].at[0])
    load_b = pltpu.make_async_copy(r["right_side"], r["b_in"], r["load"].at[1])
    load_k.start()
    load_b.start()
    barrier = pltpu.get_barrier_semaphore()
    for partner in partners:
        pl.semaphore_signal(barrier, inc=1, device_id=partner, device_id_type=MESH)

    def exchange(name, number, halo, depth):
        tag = f"{name}{number}"
        return Exchange(r[tag], r[tag + "_l"], r[tag + "_r"], r[tag + "_send"], r[tag + "_recv"], halo, depth)

    levels = []
    for number, (lanes, halo, depth_k, depth_b, depth_x) in enumerate(SHAPES):
        fields = [
            exchange("k", number, halo, depth_k),
            exchange("b", number, halo, depth_b),
            exchange("xh", number, halo, depth_x),
        ]
        fields += [r[f"{name}{number}"] for name in LOCAL]
        levels.append(Level(number, lanes, fields, gx, gy, (count_x, count_y)))
    l0, l1, l2 = levels
    l3 = Whole(3, 32, 4, [r[f"{name}3"] for name in WHOLE])
    l4 = Whole(4, 16, 2, [r[f"{name}4"] for name in WHOLE])

    def turn(staged, target):
        for y in range(l0.n):
            for part in range(2):
                lanes = pl.ds(128 * part, 128)
                target[l0.h + y, 0 : l0.x, lanes] = staged[part, pl.ds(y, l0.x, stride=l0.n), :]

    load_k.wait()
    turn(r["k_in"], r["k0"])
    load_b.wait()
    turn(r["b_in"], r["b0"])
    pl.semaphore_wait(barrier, len(partners))
    l0.k.start(place)
    l0.b.start(place)

    half = r["half"]
    k0, k1, k2 = r["k0"], r["k1"], r["k2"]
    loop(0, l1.n, restrict(lambda p: k0[p, 0 : l0.x, :], k1, l0.h, l1.h, l0.x, 256, 128, half))
    l1.k.start(place)
    loop(0, l2.n, restrict(lambda p: k1[p, 0 : l1.x, :], k2, l1.h, l2.h, l1.x, 128, 64, half))
    l2.k.start(place)

    def small_block(read):
        row, col = iota((128, 128), 0), iota((128, 128), 1)
        matrix = jnp.where((row < 64) & (row // 2 == col % 32), 0.125, 0.0).astype(F32)
        tile = (8, 128)
        mine = iota(tile, 1) // 32 == iota(tile, 0) // 2
        found = jnp.zeros(tile, F32)
        for j in range(2):
            pair = read(l2.h + 2 * j) + read(l2.h + 2 * j + 1)
            spread = jnp.where(mine, times(pair, matrix), 0.0)
            line = jnp.sum(spread, axis=0, keepdims=True)
            found = jnp.where(iota(tile, 0) == 2 * chip_x + j, jnp.broadcast_to(line, tile), found)
        return found

    class Gather:
        def __init__(self, name, target):
            self.first, self.target = r[name + "_first"], target
            self.send, self.recv = r[name + "_send"], r[name + "_recv"]
            self.all = []

        def go(self, base, source, target, where, count):
            copies = []
            for d in range(1, count):
                copies.append(
                    pltpu.make_async_remote_copy(
                        src_ref=source,
                        dst_ref=target,
                        send_sem=self.send.at[base + d - 1],
                        recv_sem=self.recv.at[base + d - 1],
                        device_id=where(d),
                        device_id_type=MESH,
                    )
                )
            for copy in copies:
                copy.start()
            self.now = copies
            self.all += copies

        def along_x(self, tile):
            self.first[chip_x] = tile
            slot = self.first.at[chip_x]
            self.go(0, slot, slot, along_x, ring_x)

        def along_z(self):
            self.arrive()
            rows = pl.ds(pl.multiple_of(8 * chip_z, 8), 8)
            found = self.first[0]
            for slot in range(1, ring_x):
                found = found + self.first[slot]
            self.target[gx + 1, rows, :] = found
            part = self.target.at[gx + 1, rows]
            self.go(ring_x - 1, part, part, along_z, ring_z)

        def along_gx(self):
            self.arrive()
            part = self.target.at[gx + 1]
            self.go(ring_x + ring_z - 2, part, part, along_gx, count_x)

        def arrive(self):
            for copy in self.now:
                copy.wait_recv()

    l3.blank()
    l4.blank()
    gather_k, gather_b = Gather("gk", l3.k), Gather("gb", l3.b)
    gather_k.along_x(small_block(lambda p: k2[p, 0 : l2.x, :]))

    def ready(level):
        h, n, depth = level.h, level.n, level.k.depth
        level.k.arrive((2, 3))
        level.k.merge(h, h + n)
        level.mend(h, h + n)
        level.faces(h, h + n)
        level.faces_y(h, h + n - 1)
        level.totals(h + 1, h + n - 1)
        level.k.arrive((0, 1, 4, 5, 6, 7))
        low, high = h - depth + 1, h + n + depth - 1
        level.k.merge(low, h)
        level.k.merge(h + n, high)
        level.mend(low, h)
        level.mend(h + n, high)
        level.mend_planes()
        level.faces(low, h)
        level.faces(h + n, high)
        level.faces_y(h - depth, h)
        level.faces_y(h + n - 1, high)
        level.totals(low, h + 1)
        level.totals(h + n - 1, high)

    def descend(level):
        h, n, depth = level.h, level.n, level.b.depth
        level.b.arrive(range(8))
        level.b.merge(h - depth + 1, h + n + depth - 1)
        level.first(h - depth, h + n + depth)
        level.second()

    ready(l0)
    descend(l0)
    loop(
        0,
        l1.n,
        restrict(lambda p: l0.residual(l0.x2, p)[0 : l0.x, :], r["b1"], l0.h, l1.h, l0.x, 256, 128, half),
    )
    l1.b.start(place)
    l0.xh.start(place)
    gather_k.along_z()
    ready(l1)
    descend(l1)
    loop(
        0,
        l2.n,
        restrict(lambda p: l1.residual(l1.x2, p)[0 : l1.x, :], r["b2"], l1.h, l2.h, l1.x, 128, 64, half),
    )
    l2.b.start(place)
    l1.xh.start(place)
    gather_k.along_gx()
    ready(l2)
    descend(l2)
    gather_b.along_x(small_block(lambda p: l2.residual(l2.x2, p)[0 : l2.x, :]))
    l2.xh.start(place)

    def to_bottom(read, target):
        row, col = iota((128, 128), 0), iota((128, 128), 1)
        same_x = (row // 32) // 2 == (col % 32) // 16
        same_z = (row % 32) // 2 == col % 16
        matrix = jnp.where(same_x & same_z, 0.125, 0.0).astype(F32)

        def body(g):
            target[g] = times(halve_rows(read(g), half, 64), matrix)

        loop(1, count_x + 1, body)

    gather_k.arrive()
    l3.weights()
    to_bottom(lambda g: l3.k[g], l4.k)
    l4.weights()
    gather_b.along_z()
    gather_b.along_gx()
    gather_b.arrive()
    l3.down()
    to_bottom(l3.residual, l4.b)
    deepest = l4.bottom()

    row, col = iota((128, 128), 0), iota((128, 128), 1)
    same = ((col // 32) // 2 == (row % 32) // 16) & ((col % 32) // 2 == row % 16) & (row < 32)
    matrix_43 = jnp.where(same, 1.0, 0.0).astype(F32)

    def lift(g):
        grown = times(deepest[g], matrix_43)
        half[0, pl.ds(0, 32, stride=2), :] = grown
        half[0, pl.ds(1, 32, stride=2), :] = grown
        l3.z0[g] = l3.x2[g] + half[0, 0:64, :]

    loop(1, count_x + 1, lift)
    answer = r["answer"]

    def store(g, value):
        answer[g - 1, 8:72, :] = value

    l3.up(store)

    matrix_32 = jnp.where(iota((128, 128), 0) % 32 == (iota((128, 128), 1) % 64) // 2, 1.0, 0.0).astype(F32)
    lower = jnp.maximum(gx - 1, 0)
    upper = jnp.minimum(gx + 1, count_x - 1)
    l2.xh.arrive(range(8))
    l2.xh.merge(l2.h - 3, l2.h + l2.n + 3)
    tile = (8, 128)
    group = iota(tile, 1) // 32 == iota(tile, 0) // 2
    first_half = iota(tile, 0) < 4

    def lift_2(j):
        at = 6 + 2 * gy + j
        own = jnp.broadcast_to(answer[gx, pl.ds(at, 1), :], tile)
        high = jnp.broadcast_to(answer[upper, pl.ds(at, 1), :], tile)
        low = jnp.broadcast_to(answer[lower, pl.ds(at, 1), :], tile)
        halo = jnp.where(first_half, high, low)
        spread = jnp.concatenate([jnp.where(group, own, 0.0), jnp.where(group, halo, 0.0)], axis=0)
        grown = times(spread, matrix_32)
        l2.correct(2 * j, grown)
        l2.correct(2 * j + 1, grown)

    loop(0, 6, lift_2)
    l2.third(1, 11)
    l2.fourth(2, 10, r["z2"])

    matrix_21 = grow_lanes(64, 128)
    l1.xh.arrive(range(8))
    l1.xh.merge(l1.h - 3, l1.h + l1.n + 3)

    def lift_1(j):
        grown = double_rows(times(r["z2"][2 + j], matrix_21), half, 16)
        l1.correct(2 * j, grown)
        l1.correct(2 * j + 1, grown)

    loop(0, 8, lift_1)
    l1.third(1, 15)
    l1.fourth(2, 14, r["z1out"])

    matrix_10 = grow_lanes(128, 256)
    l0.xh.arrive(range(8))
    l0.xh.merge(l0.h - 2, l0.h + l0.n + 2)

    def lift_0(j):
        grown = double_rows(times(r["z1out"][2 + j], matrix_10), half, 24)

        @pl.when(j > 0)
        def _():
            l0.correct(2 * j - 1, grown)

        @pl.when(j < 11)
        def _():
            l0.correct(2 * j, grown)

    loop(0, 12, lift_0)
    l0.third(1, 21)
    l0.fourth(2, 20, l0.x2)

    def finish(y):
        p = l0.h + y
        left = l0.residual(l0.x2, p)
        for part in range(2):
            lanes = slice(128 * part, 128 * (part + 1))
            r["k_in"][part, pl.ds(y, l0.x, stride=l0.n), :] = l0.x2[p, 0 : l0.x, lanes]
            r["b_in"][part, pl.ds(y, l0.x, stride=l0.n), :] = left[0 : l0.x, lanes]

    for y in range(l0.n):
        finish(y)
    stores = []
    for number, (staged, target) in enumerate(((r["k_in"], r["solution"]), (r["b_in"], r["residual"]))):
        stores.append(pltpu.make_async_copy(staged, target, r["load"].at[2 + number]))
    for copy in stores:
        copy.start()
    for level in levels:
        for field in (level.k, level.b, level.xh):
            field.sent()
    for copy in gather_k.all + gather_b.all:
        copy.wait_send()
    for copy in stores:
        copy.wait()


SHAPES = ((256, 3, 3, 2, 3), (128, 4, 4, 3, 4), (64, 4, 4, 3, 4))
LOCAL = ("x1_", "x2_", "wx", "wy", "wz", "w", "inv", "z0_", "z1_")
WHOLE = ("k", "b", "x1_", "x2_", "wx", "wy", "wz", "w", "inv", "z0_", "z1_")


def per_device(count_x, count_y, right_side, coefficient):
    nx, ny, nz = right_side.shape
    vmem = lambda *shape: pltpu.VMEM(shape, F32)
    scratch = {
        "k_in": vmem(2, nx * ny, 128),
        "b_in": vmem(2, nx * ny, 128),
        "load": pltpu.SemaphoreType.DMA((4,)),
        "half": vmem(2, 64, 128),
    }
    for number, (lanes, halo, *_) in enumerate(SHAPES):
        rows, planes, width = nx >> number, ny >> number, max(128, lanes)
        full = (planes + 2 * halo, rows + 8, width)
        for name in ("k", "b", "xh"):
            tag = f"{name}{number}"
            scratch[tag] = vmem(*full)
            scratch[tag + "_l"] = vmem(full[0], 8, width)
            scratch[tag + "_r"] = vmem(full[0], 8, width)
            scratch[tag + "_send"] = pltpu.SemaphoreType.DMA((8,))
            scratch[tag + "_recv"] = pltpu.SemaphoreType.DMA((8,))
        for name in LOCAL:
            scratch[f"{name}{number}"] = vmem(*full)
    for number, rows in ((3, 2 * count_y), (4, count_y)):
        for name in WHOLE:
            scratch[f"{name}{number}"] = vmem(count_x + 2, rows, 128)
    for name in ("gk", "gb"):
        scratch[name + "_first"] = vmem(4, 8, 128)
        scratch[name + "_send"] = pltpu.SemaphoreType.DMA((3 + count_y // 4 - 1 + count_x - 1,))
        scratch[name + "_recv"] = pltpu.SemaphoreType.DMA((3 + count_y // 4 - 1 + count_x - 1,))
    scratch["answer"] = vmem(count_x, 2 * count_y + 16, 128)
    scratch["z2"] = vmem((ny >> 2) + 8, (nx >> 2) + 8, 128)
    scratch["z1out"] = vmem((ny >> 1) + 8, (nx >> 1) + 8, 128)

    split = lambda value: value.reshape(nx * ny, 2, 128).transpose(1, 0, 2)
    join = lambda value: value.transpose(1, 0, 2).reshape(nx, ny, nz)
    names = ["right_side", "coefficient", "solution", "residual"] + list(scratch)
    shape = jax.ShapeDtypeStruct((2, nx * ny, 128), F32)
    found = pl.pallas_call(
        functools.partial(kernel, count_x, count_y, names),
        out_shape=(shape, shape),
        in_specs=[pl.BlockSpec(memory_space=pl.ANY)] * 2,
        out_specs=(pl.BlockSpec(memory_space=pl.ANY),) * 2,
        scratch_shapes=list(scratch.values()),
        compiler_params=pltpu.CompilerParams(
            collective_id=0, has_side_effects=True, vmem_limit_bytes=56 << 20
        ),
        name="vcycle",
    )(split(right_side), split(coefficient))
    return tuple(join(value) for value in found)


def solution(mesh):
    spec = P("gx", "gy", None)
    step = functools.partial(per_device, mesh.shape["gx"], mesh.shape["gy"])
    return jax.shard_map(step, mesh=mesh, in_specs=(spec, spec), out_specs=(spec, spec), check_vma=False)
```

```python
import functools

import jax
import jax.numpy as jnp
from jax import lax
from jax.experimental import pallas as pl
from jax.experimental.pallas import tpu as pltpu
from jax.sharding import PartitionSpec as P

MESH = pl.DeviceIdType.MESH
F32 = jnp.float32

SMOOTH_LO, SMOOTH_HI = 0.5, 2.0
COARSE_LO, COARSE_HI = 0.05, 2.0
BOTTOM = 8

STEPS = ((0, 1), (0, -1), (1, 0), (-1, 0), (1, 1), (1, -1), (-1, 1), (-1, -1))


def coefficients(low, high, sweeps):
    theta = (high + low) / 2.0
    delta = (high - low) / 2.0
    sigma = theta / delta
    rho = 1.0 / sigma
    pairs = []
    for _ in range(sweeps - 1):
        rho_next = 1.0 / (2.0 * sigma - rho)
        pairs.append((rho_next * rho, 2.0 * rho_next / delta))
        rho = rho_next
    return theta, pairs


THETA, ((MOMENTUM, STEP),) = coefficients(SMOOTH_LO, SMOOTH_HI, 2)


def harmonic(own, other):
    return 2.0 * own * other / (own + other)


def roll(value, shift, axis):
    size = value.shape[axis]
    return pltpu.roll(value, shift % size, axis)


def iota(shape, dim):
    return lax.broadcasted_iota(jnp.int32, shape, dim)


def times(rows, matrix):
    high = rows.astype(jnp.bfloat16)
    rest = rows - high.astype(F32)
    middle = rest.astype(jnp.bfloat16)
    low = (rest - middle.astype(F32)).astype(jnp.bfloat16)
    found = [jnp.dot(term, matrix, preferred_element_type=F32) for term in (low, middle, high)]
    return (found[0] + found[1]) + found[2]


def loop(start, stop, body, unroll=1):
    count = (stop - start) // unroll

    def step(index, carry):
        for k in range(unroll):
            body(start + index * unroll + k)
        return carry

    if count > 1:
        lax.fori_loop(0, count, step, 0)
        start += count * unroll
    for index in range(start, stop):
        body(index)


class Exchange:
    def __init__(self, field, left, right, send, recv, halo, depth):
        self.field, self.left, self.right = field, left, right
        self.send, self.recv = send, recv
        self.halo, self.depth = halo, depth
        self.planes = field.shape[0] - 2 * halo
        self.rows = field.shape[1] - 8

    def copies(self, place):
        h, n, r, x = self.halo, self.planes, self.depth, self.rows
        found = []
        for number, (dx, dy) in enumerate(STEPS):
            if dx == 0:
                source_plane = h + n - r if dy > 0 else h
                target_plane = h - r if dy > 0 else h + n
                source = self.field.at[pl.ds(source_plane, r), pl.ds(0, x)]
                target = self.field.at[pl.ds(target_plane, r), pl.ds(0, x)]
            else:
                count = n if dy == 0 else r - 1
                source_plane = h if dy <= 0 else h + n - count
                target_plane = h if dy == 0 else (h - count if dy > 0 else h + n)
                source = self.field.at[pl.ds(source_plane, count), pl.ds(x - 8 if dx > 0 else 0, 8)]
                landing = self.left if dx > 0 else self.right
                target = landing.at[pl.ds(target_plane, count)]
            found.append(
                pltpu.make_async_remote_copy(
                    src_ref=source,
                    dst_ref=target,
                    send_sem=self.send.at[number],
                    recv_sem=self.recv.at[number],
                    device_id=place(dx, dy),
                    device_id_type=MESH,
                )
            )
        return found

    def start(self, place):
        self.started = self.copies(place)
        for copy in self.started:
            copy.start()

    def arrive(self, which):
        for number in which:
            self.started[number].wait_recv()

    def merge(self, start, stop):
        x = self.rows
        shape = (8, self.field.shape[2])

        def body(p):
            upper = iota(shape, 0) < 4
            self.field[p, x:, :] = jnp.where(upper, self.right[p], self.left[p])

        loop(start, stop, body, 4)

    def merge_mended(self, start, stop, at_low, at_high):
        x = self.rows
        shape = (8, self.field.shape[2])
        row = iota(shape, 0)
        take_high = jnp.where(row == 0, at_high, 0) == 1
        take_low = jnp.where(row == 7, at_low, 0) == 1
        upper = row < 4

        def body(p):
            tile = jnp.where(upper, self.right[p], self.left[p])
            tile = jnp.where(take_high, roll(self.field[p, x - 8 : x, :], 1, 0), tile)
            self.field[p, x:, :] = jnp.where(take_low, roll(self.field[p, 0:8, :], 7, 0), tile)

        loop(start, stop, body, 4)

    def sent(self):
        for copy in self.started:
            copy.wait_send()


class Level:
    def __init__(self, number, lanes, refs, gx, gy, counts):
        self.scale = 0.25**number
        self.lanes = lanes
        self.gx, self.gy = gx, gy
        self.count_x, self.count_y = counts
        (self.k, self.b, self.xh, self.x1, self.x2, self.wx, self.wy, self.wz, self.w, self.inv, self.z0, self.z1) = refs
        self.h = self.k.halo
        self.n = self.k.planes
        self.x = self.k.rows
        self.shape = (self.x + 8, 128 * ((lanes + 127) // 128))
        self.period = lanes
        self.unroll = 2 if number == 0 else 4

    def merge_k(self, start, stop):
        at_low = jnp.where(self.gx == 0, 1, 0)
        at_high = jnp.where(self.gx == self.count_x - 1, 1, 0)
        self.k.merge_mended(start, stop, at_low, at_high)

    def row_ok(self):
        row = iota(self.shape, 0)
        below = jnp.where(self.gx == 0, 1, 0)
        above = jnp.where(self.gx == self.count_x - 1, 1, 0)
        bad_low = jnp.where(row >= self.x + 4, below, 0)
        bad_high = jnp.where((row >= self.x) & (row < self.x + 4), above, 0)
        return (bad_low + bad_high) == 0

    def plane_ok(self, p):
        y = self.gy * self.n + p - self.h
        return (y >= 0) & (y < self.count_y * self.n)

    def mend_planes(self):
        field, h, n = self.k.field, self.h, self.n

        @pl.when(self.gy == 0)
        def _():
            field[h - 1] = field[h]

        @pl.when(self.gy == self.count_y - 1)
        def _():
            field[h + n] = field[h + n - 1]

    def lane(self):
        return iota(self.shape, 1) % self.period

    def faces(self, start, stop):
        k = self.k.field

        def body(p):
            own = k[p]
            self.wx[p] = harmonic(own, roll(own, -1, 0))
            along = harmonic(own, roll(own, -1, 1))
            self.wz[p] = jnp.where(self.lane() == self.period - 1, 0.0, along)

        loop(start, stop, body, self.unroll)

    def faces_y(self, start, stop):
        k = self.k.field

        def body(p):
            self.wy[p] = harmonic(k[p], k[p + 1])

        loop(start, stop, body, self.unroll)

    def totals(self, start, stop):
        k = self.k.field
        rows_ok = self.row_ok()

        def body(p):
            wx, wz = self.wx[p], self.wz[p]
            lane = self.lane()
            edge = jnp.where((lane == 0) | (lane == self.period - 1), k[p], 0.0)
            total = wx + roll(wx, 1, 0) + self.wy[p] + self.wy[p - 1] + wz + roll(wz, 1, 1) + edge
            self.w[p] = total
            ok = rows_ok & self.plane_ok(p)
            self.inv[p] = jnp.where(ok, 1.0 / total, 0.0)

        loop(start, stop, body, self.unroll)

    def beside(self, field, p):
        own, wx, wz = field[p], self.wx[p], self.wz[p]
        found = wx * roll(own, -1, 0) + roll(wx * own, 1, 0)
        found = found + self.wy[p] * field[p + 1] + self.wy[p - 1] * field[p - 1]
        return found + wz * roll(own, -1, 1) + roll(wz * own, 1, 1)

    def first(self, start, stop):
        b = self.b.field

        def body(p):
            self.x1[p] = b[p] * self.inv[p] * (1.0 / (THETA * self.scale))

        loop(start, stop, body, self.unroll)

    def second(self):
        h, n, x = self.h, self.n, self.x

        def value(p):
            own = self.x1[p]
            factor = 1.0 + MOMENTUM + STEP * (THETA - 1.0)
            return factor * own + STEP * (self.inv[p] * self.beside(self.x1, p))

        def inner(p):
            found = value(p)
            self.x2[p] = found
            self.xh.field[p, 0:x, :] = found[0:x, :]

        loop(h, h + n, inner, self.unroll)
        for p in (h - 1, h + n):
            self.x2[p] = value(p)

    def residual(self, field, p):
        return self.b.field[p] - self.scale * (self.w[p] * field[p] - self.beside(field, p))

    def correct(self, p, grown):
        ok = self.rows_ok & self.plane_ok(p)
        self.z0[p] = jnp.where(ok, self.xh.field[p] + grown, 0.0)

    def third(self, start, stop):
        def body(p):
            own = self.z0[p]
            flow = self.inv[p] * self.beside(self.z0, p)
            self.z1[p] = (1.0 - 1.0 / THETA) * own + self.x1[p] + (1.0 / THETA) * flow

        loop(start, stop, body, self.unroll)

    def fourth(self, start, stop, target):
        def body(p):
            own = self.z1[p]
            flow = self.inv[p] * self.beside(self.z1, p)
            found = (1.0 + MOMENTUM - STEP) * own - MOMENTUM * self.z0[p]
            target[p] = found + (STEP * THETA) * self.x1[p] + STEP * flow

        loop(start, stop, body, self.unroll)


LOW, HIGH = 8, 16


class Whole:
    def __init__(self, refs):
        self.scale = 0.25**3
        self.size_z = 32
        self.k, self.b, self.x1, self.x2, self.wx, self.wy, self.wz, self.w, self.inv = refs
        self.count = self.k.shape[0] - 2
        self.rows = self.k.shape[1] - LOW - HIGH
        self.shape = (self.rows, 128)

    def blank(self):
        for ref in (self.k, self.x1, self.x2, self.wx, self.wy, self.wz, self.inv):
            empty = jnp.zeros(ref.shape[1:], F32)
            ref[0] = empty
            ref[self.count + 1] = empty

            def body(g, ref=ref):
                ref[g, 0:LOW, :] = jnp.zeros((LOW, 128), F32)
                ref[g, LOW + self.rows :, :] = jnp.zeros((HIGH, 128), F32)

            loop(1, self.count + 1, body, 4)

    def at(self, ref, g):
        return ref[g, LOW : LOW + self.rows, :]

    def after(self, own, following):
        inner = iota(own.shape, 1) < 128 - self.size_z
        return jnp.where(inner, roll(own, -self.size_z, 1), roll(following, -self.size_z, 1))

    def before(self, own, previous):
        inner = iota(own.shape, 1) >= self.size_z
        return jnp.where(inner, roll(own, self.size_z, 1), roll(previous, self.size_z, 1))

    def weights(self):
        rows, inside = self.rows, slice(LOW, LOW + self.rows)

        def faces(g):
            own, following = self.at(self.k, g), self.at(self.k, g + 1)
            lane, row = iota(self.shape, 1), iota(self.shape, 0)
            end = jnp.where(lane >= 128 - self.size_z, jnp.where(g == self.count, 1, 0), 0)
            self.wx[g, inside, :] = jnp.where(end == 1, 0.0, harmonic(own, self.after(own, following)))
            self.wy[g, inside, :] = jnp.where(row == rows - 1, 0.0, harmonic(own, roll(own, -1, 0)))
            last = lane % self.size_z == self.size_z - 1
            self.wz[g, inside, :] = jnp.where(last, 0.0, harmonic(own, roll(own, -1, 1)))

        loop(1, self.count + 1, faces)

        def totals(g):
            lane, row = iota(self.shape, 1), iota(self.shape, 0)
            high = jnp.where(lane >= 128 - self.size_z, jnp.where(g == self.count, 1.0, 0.0), 0.0)
            low = jnp.where(lane < self.size_z, jnp.where(g == 1, 1.0, 0.0), 0.0)
            edge = high + low
            edge = edge + jnp.where((row == 0) | (row == rows - 1), 1.0, 0.0)
            z = lane % self.size_z
            edge = edge + jnp.where((z == 0) | (z == self.size_z - 1), 1.0, 0.0)
            wx, wy, wz = self.at(self.wx, g), self.at(self.wy, g), self.at(self.wz, g)
            total = wx + self.before(wx, self.at(self.wx, g - 1)) + wy + roll(wy, 1, 0) + wz + roll(wz, 1, 1)
            total = total + edge * self.at(self.k, g)
            self.w[g, inside, :] = total
            self.inv[g, inside, :] = 1.0 / total

        loop(1, self.count + 1, totals)

    def flow(self, fields, weights):
        previous, own, following = fields
        wx_previous, wx, wy, wz = weights
        found = wx * self.after(own, following) + self.before(wx * own, wx_previous * previous)
        found = found + wy * roll(own, -1, 0) + roll(wy * own, 1, 0)
        return found + wz * roll(own, -1, 1) + roll(wz * own, 1, 1)

    def beside(self, field, g):
        fields = [self.at(field, g + step) for step in (-1, 0, 1)]
        weights = [self.at(self.wx, g - 1)] + [self.at(ref, g) for ref in (self.wx, self.wy, self.wz)]
        return self.flow(fields, weights)

    def down(self, left):
        inside = slice(LOW, LOW + self.rows)

        def first(g):
            found = self.at(self.b, g) * self.at(self.inv, g) * (1.0 / (THETA * self.scale))
            self.x1[g, inside, :] = found

        loop(1, self.count + 1, first, 2)

        def second(g):
            factor = 1.0 + MOMENTUM + STEP * (THETA - 1.0)
            moved = self.at(self.inv, g) * self.beside(self.x1, g)
            self.x2[g, inside, :] = factor * self.at(self.x1, g) + STEP * moved

        loop(1, self.count + 1, second, 2)

        def residual(g):
            applied = self.at(self.w, g) * self.at(self.x2, g) - self.beside(self.x2, g)
            left[g - 1] = self.at(self.b, g) - self.scale * applied

        loop(1, self.count + 1, residual, 2)

    def up(self, gx, start, grown, held, answer):
        span = pl.ds(start, 24)
        z0, z1 = held
        planes = (0, 1, 2)
        part = lambda ref, c: ref[gx + c, span, :]
        for c in planes:
            z0[c + 1] = part(self.x2, c) + grown[c, span, :]

        def flow(field, c):
            fields = [field[c + step] for step in (0, 1, 2)]
            before = self.wx[jnp.maximum(gx + c - 1, 0), span, :]
            return part(self.inv, c) * self.flow(fields, [before, part(self.wx, c), part(self.wy, c), part(self.wz, c)])

        for c in planes:
            z1[c + 1] = (1.0 - 1.0 / THETA) * z0[c + 1] + part(self.x1, c) + (1.0 / THETA) * flow(z0, c)
        for c in planes:
            found = (1.0 + MOMENTUM - STEP) * z1[c + 1] - MOMENTUM * z0[c + 1]
            answer[c] = found + (STEP * THETA) * part(self.x1, c) + STEP * flow(z1, c)


class Deepest:
    def __init__(self, count):
        self.count = count
        self.scale = 0.25**4
        shape = (8, 128)
        self.lane, self.row = iota(shape, 1), iota(shape, 0)
        self.low_x = (self.lane % 32) < 16
        self.zero = jnp.zeros(shape, F32)

    def next_x(self, tiles):
        back, ahead = [roll(t, -16, 1) for t in tiles], [roll(t, 16, 1) for t in tiles] + [self.zero]
        return [jnp.where(self.low_x, back[g], ahead[g + 1]) for g in range(self.count)]

    def last_x(self, tiles):
        back, ahead = [self.zero] + [roll(t, -16, 1) for t in tiles], [roll(t, 16, 1) for t in tiles]
        return [jnp.where(self.low_x, back[g], ahead[g]) for g in range(self.count)]

    def next_y(self, tiles):
        moved = [roll(t, -1, 0) for t in tiles]
        return [jnp.where(self.row < 7, t, roll(t, -32, 1)) for t in moved]

    def last_y(self, tiles):
        moved = [roll(t, 1, 0) for t in tiles]
        return [jnp.where(self.row > 0, t, roll(t, 32, 1)) for t in moved]

    def next_z(self, tiles):
        return [roll(t, -1, 1) for t in tiles]

    def last_z(self, tiles):
        return [roll(t, 1, 1) for t in tiles]

    def weights(self, k, weight_refs, inv_ref):
        lane, row, span = self.lane, self.row, range(self.count)
        z = lane % 16
        end_y = (row == 7) & (lane >= 96)
        edge = jnp.where((z == 0) | (z == 15), 1.0, 0.0)
        edge = edge + jnp.where(end_y | ((row == 0) & (lane < 32)), 1.0, 0.0)
        faces_x = [harmonic(a, b) for a, b in zip(k, self.next_x(k))]
        faces_x[-1] = jnp.where(self.low_x, faces_x[-1], 0.0)
        faces_y = [jnp.where(end_y, 0.0, harmonic(a, b)) for a, b in zip(k, self.next_y(k))]
        faces_z = [jnp.where(z == 15, 0.0, harmonic(a, b)) for a, b in zip(k, self.next_z(k))]
        sets = [faces_x, self.last_x(faces_x), faces_y, self.last_y(faces_y), faces_z, self.last_z(faces_z)]
        for g in span:
            total = edge * k[g]
            if g == 0:
                total = total + jnp.where(self.low_x, k[g], 0.0)
            if g == self.count - 1:
                total = total + jnp.where(self.low_x, 0.0, k[g])
            for one in sets:
                total = total + one[g]
            inv = 1.0 / total
            inv_ref[g] = inv
            for number, one in enumerate(sets):
                weight_refs[number, g] = one[g] * inv

    def solve(self, b, weight_refs, inv_ref):
        theta, pairs = coefficients(COARSE_LO, COARSE_HI, BOTTOM)
        span = range(self.count)
        scaled = [b[g] * inv_ref[g] * (1.0 / self.scale) for g in span]
        update = [t * (1.0 / theta) for t in scaled]
        found = update
        for momentum, step in pairs:
            shifted = [
                self.next_x(found),
                self.last_x(found),
                self.next_y(found),
                self.last_y(found),
                self.next_z(found),
                self.last_z(found),
            ]
            following = []
            for g in span:
                flow = weight_refs[0, g] * shifted[0][g]
                for number in range(1, 6):
                    flow = flow + weight_refs[number, g] * shifted[number][g]
                following.append(momentum * update[g] + step * ((scaled[g] - found[g]) + flow))
            update = following
            found = [a + d for a, d in zip(found, update)]
        return found


def shrink_lanes(lanes, kept):
    row, col = iota((max(lanes, 128), 128), 0), iota((max(lanes, 128), 128), 1)
    return jnp.where((row // 2 == col % kept) & (row < lanes), 0.125, 0.0).astype(jnp.bfloat16)


def grow_lanes(kept, lanes):
    row, col = iota((128, lanes), 0), iota((128, lanes), 1)
    period = 2 * kept
    return jnp.where((col % period) // 2 == row, 1.0, 0.0).astype(jnp.bfloat16)


def restrict(read, target, count, fine_plane, coarse_plane, rows, matrix, half, sums):
    kept = rows // 2
    parts = matrix.shape[0] // 128

    def body(j):
        pair = read(fine_plane + 2 * j) + read(fine_plane + 2 * j + 1)
        slot = j % 2
        for part in range(parts):
            half[slot, part, 0:rows, :] = pair[:, part * 128 : (part + 1) * 128]
        for part in range(parts):
            even = half[slot, part, pl.ds(0, kept, stride=2), :]
            odd = half[slot, part, pl.ds(1, kept, stride=2), :]
            sums[pl.ds(pl.multiple_of(j * kept, 8), kept), 128 * part : 128 * (part + 1)] = even + odd

    loop(0, count, body, 2)
    means = times(sums[0 : count * kept, 0 : 128 * parts], matrix)
    target[coarse_plane : coarse_plane + count, 0:kept, :] = means.reshape(count, kept, 128)


def grow(source, planes, rows, matrix, doubled):
    start, stop = planes
    count, parts = stop - start, matrix.shape[1] // 128
    wide = times(source[start:stop].reshape(count * rows, 128), matrix)
    for j in range(count):
        for part in range(parts):
            piece = wide[j * rows : (j + 1) * rows, 128 * part : 128 * (part + 1)]
            doubled[j, part, pl.ds(0, rows, stride=2), :] = piece
            doubled[j, part, pl.ds(1, rows, stride=2), :] = piece


def grown_plane(doubled, j, rows, parts):
    own = 2 * (rows - 8)
    upper = iota((8, 128), 0) < 4
    found = []
    for part in range(parts):
        tail = jnp.where(upper, doubled[j, part, own : own + 8, :], doubled[j, part, own + 8 : own + 16, :])
        found.append(jnp.concatenate([doubled[j, part, 0:own, :], tail], axis=0))
    return found[0] if parts == 1 else jnp.concatenate(found, axis=1)


def kernel(count_x, count_y, names, *refs):
    r = dict(zip(names, refs))
    gx, gy = lax.axis_index("gx"), lax.axis_index("gy")
    ring_x = 4
    ring_z = count_y // ring_x
    chip_x, chip_z = gy % ring_x, gy // ring_x

    def place(dx, dy):
        return ((gx + dx + count_x) % count_x, (gy + dy + count_y) % count_y)

    def along_x(d):
        return (gx, chip_z * ring_x + (chip_x + d) % ring_x)

    def along_z(d):
        return (gx, ((chip_z + d) % ring_z) * ring_x + chip_x)

    def along_gx(d):
        return ((gx + d) % count_x, gy)

    partners = [place(dx, dy) for dx, dy in STEPS]
    partners += [along_x(d) for d in range(1, ring_x)]
    partners += [along_z(d) for d in range(1, ring_z)]
    partners += [along_gx(d) for d in range(1, count_x)]

    barrier = pltpu.get_barrier_semaphore()
    for partner in partners:
        pl.semaphore_signal(barrier, inc=1, device_id=partner, device_id_type=MESH)

    def halves(whole, staged, first, store):
        copies = []
        for part in range(2):
            wide = whole.at[:, pl.ds(128 * part, 128)]
            pair = (staged.at[part], wide) if store else (wide, staged.at[part])
            copies.append(pltpu.make_async_copy(*pair, r["load"].at[first + part]))
        return copies

    loads_k = halves(r["coefficient"], r["k_in"], 0, False)
    loads_b = halves(r["right_side"], r["b_in"], 2, False)
    for copy in loads_k + loads_b:
        copy.start()

    def exchange(name, number, halo, depth):
        tag = f"{name}{number}"
        return Exchange(r[tag], r[tag + "_l"], r[tag + "_r"], r[tag + "_send"], r[tag + "_recv"], halo, depth)

    levels = []
    for number, (lanes, halo, depth_k, depth_b, depth_x) in enumerate(SHAPES):
        fields = [
            exchange("k", number, halo, depth_k),
            exchange("b", number, halo, depth_b),
            exchange("xh", number, halo, depth_x),
        ]
        fields += [r[f"{name}{number}"] for name in LOCAL]
        levels.append(Level(number, lanes, fields, gx, gy, (count_x, count_y)))
    l0, l1, l2 = levels
    l3 = Whole([r[f"{name}3"] for name in WHOLE])
    l4 = Deepest(count_x)

    def turn(staged, target):
        for y in range(l0.n):
            for part in range(2):
                lanes = pl.ds(128 * part, 128)
                target[l0.h + y, 0 : l0.x, lanes] = staged[part, pl.ds(y, l0.x, stride=l0.n), :]

    for copy in loads_k:
        copy.wait()
    turn(r["k_in"], r["k0"])
    for copy in loads_b:
        copy.wait()
    turn(r["b_in"], r["b0"])
    pl.semaphore_wait(barrier, len(partners))
    l0.k.start(place)
    l0.b.start(place)

    half, sums, doubled = r["half"], r["sums"], r["doubled"]
    k0, k1, k2 = r["k0"], r["k1"], r["k2"]
    to_1, to_2 = shrink_lanes(256, 128), shrink_lanes(128, 64)
    restrict(lambda p: k0[p, 0 : l0.x, :], k1, l1.n, l0.h, l1.h, l0.x, to_1, half, sums)
    l1.k.start(place)
    restrict(lambda p: k1[p, 0 : l1.x, :], k2, l2.n, l1.h, l2.h, l1.x, to_2, half, sums)
    l2.k.start(place)

    def small_block(read):
        row, col = iota((128, 128), 0), iota((128, 128), 1)
        matrix = jnp.where((row < 64) & (row // 2 == col % 32), 0.125, 0.0).astype(jnp.bfloat16)
        tile = (8, 128)
        mine = iota(tile, 1) // 32 == iota(tile, 0) // 2
        pairs = [read(l2.h + 2 * j) + read(l2.h + 2 * j + 1) for j in range(2)]
        means = times(jnp.concatenate(pairs, axis=0), matrix)
        found = jnp.zeros(tile, F32)
        for j in range(2):
            spread = jnp.where(mine, means[8 * j : 8 * j + 8], 0.0)
            line = jnp.sum(spread, axis=0, keepdims=True)
            found = jnp.where(iota(tile, 0) == 2 * chip_x + j, jnp.broadcast_to(line, tile), found)
        return found

    class Gather:
        def __init__(self, name, target):
            self.first, self.target = r[name + "_first"], target
            self.send, self.recv = r[name + "_send"], r[name + "_recv"]
            self.all = []

        def go(self, base, source, target, where, count):
            copies = []
            for d in range(1, count):
                copies.append(
                    pltpu.make_async_remote_copy(
                        src_ref=source,
                        dst_ref=target,
                        send_sem=self.send.at[base + d - 1],
                        recv_sem=self.recv.at[base + d - 1],
                        device_id=where(d),
                        device_id_type=MESH,
                    )
                )
            for copy in copies:
                copy.start()
            self.now = copies
            self.all += copies

        def along_x(self, tile):
            self.first[chip_x] = tile
            slot = self.first.at[chip_x]
            self.go(0, slot, slot, along_x, ring_x)

        def along_z(self):
            self.arrive()
            rows = pl.ds(pl.multiple_of(8 * chip_z + LOW, 8), 8)
            found = self.first[0]
            for slot in range(1, ring_x):
                found = found + self.first[slot]
            self.target[gx + 1, rows, :] = found
            part = self.target.at[gx + 1, rows]
            self.go(ring_x - 1, part, part, along_z, ring_z)

        def along_gx(self):
            self.arrive()
            part = self.target.at[gx + 1, pl.ds(LOW, 8 * ring_z)]
            self.go(ring_x + ring_z - 2, part, part, along_gx, count_x)

        def arrive(self):
            for copy in self.now:
                copy.wait_recv()

    gather_k, gather_b = Gather("gk", l3.k), Gather("gb", l3.b)
    gather_k.along_x(small_block(lambda p: k2[p, 0 : l2.x, :]))
    l3.blank()
    z0_3, z1_3 = r["z0_3"], r["z1_3"]
    for held in (z0_3, z1_3):
        held[0] = jnp.zeros((24, 128), F32)
        held[4] = jnp.zeros((24, 128), F32)
    grown3 = r["grown3"]
    for c in range(3):
        grown3[c, 0:LOW, :] = jnp.zeros((LOW, 128), F32)
        grown3[c, LOW + 8 * ring_z :, :] = jnp.zeros((HIGH, 128), F32)

    def ready(level):
        h, n, depth = level.h, level.n, level.k.depth
        level.k.arrive((2, 3))
        level.merge_k(h, h + n)
        level.faces(h, h + n)
        level.faces_y(h, h + n - 1)
        level.totals(h + 1, h + n - 1)
        level.k.arrive((0, 1, 4, 5, 6, 7))
        low, high = h - depth + 1, h + n + depth - 1
        level.merge_k(low, h)
        level.merge_k(h + n, high)
        level.mend_planes()
        level.faces(low, h)
        level.faces(h + n, high)
        level.faces_y(h - depth, h)
        level.faces_y(h + n - 1, high)
        level.totals(low, h + 1)
        level.totals(h + n - 1, high)

    def descend(level):
        h, n, depth = level.h, level.n, level.b.depth
        level.b.arrive(range(8))
        level.b.merge(h - depth + 1, h + n + depth - 1)
        level.first(h - depth, h + n + depth)
        level.second()

    def source_below(level, target, matrix):
        below = levels[levels.index(level) + 1]
        read = lambda p: level.residual(level.x2, p)[0 : level.x, :]
        restrict(read, target, below.n, level.h, below.h, level.x, matrix, half, sums)

    ready(l0)
    descend(l0)
    source_below(l0, r["b1"], shrink_lanes(256, 128))
    l1.b.start(place)
    l0.xh.start(place)
    gather_k.along_z()
    ready(l1)
    descend(l1)
    source_below(l1, r["b2"], shrink_lanes(128, 64))
    l2.b.start(place)
    l1.xh.start(place)
    gather_k.along_gx()
    ready(l2)
    descend(l2)
    gather_b.along_x(small_block(lambda p: l2.residual(l2.x2, p)[0 : l2.x, :]))
    l2.xh.start(place)

    def to_bottom(source, low):
        row, col = iota((128, 128), 0), iota((128, 128), 1)
        same_x = (row // 32) // 2 == (col % 32) // 16
        same_z = (row % 32) // 2 == col % 16
        matrix = jnp.where(same_x & same_z, 0.125, 0.0).astype(jnp.bfloat16)
        kept = 4 * ring_z
        pieces = []
        for g in range(count_x):
            even = source[g, pl.ds(low, kept, stride=2), :]
            odd = source[g, pl.ds(low + 1, kept, stride=2), :]
            pieces.append(even + odd)
        means = times(jnp.concatenate(pieces, axis=0), matrix)
        group = iota((8, 128), 1) // 32
        tiles = []
        for g in range(count_x):
            found = means[g * kept : g * kept + 8]
            for q in range(1, 4):
                found = jnp.where(group == q, means[g * kept + 8 * q : g * kept + 8 * q + 8], found)
            tiles.append(found)
        return tiles

    gather_k.arrive()
    l3.weights()
    l4.weights(to_bottom(l3.k.at[pl.ds(1, count_x)], LOW), r["w4"], r["inv4"])
    gather_b.along_z()
    gather_b.along_gx()
    gather_b.arrive()
    l3.down(r["left3"])
    deepest = l4.solve(to_bottom(r["left3"], 0), r["w4"], r["inv4"])
    tiles4 = r["tiles4"]
    tiles4[0] = l4.zero
    tiles4[count_x + 1] = l4.zero
    for g in range(count_x):
        tiles4[g + 1] = deepest[g]

    row, col = iota((128, 128), 0), iota((128, 128), 1)
    same = ((row % 32) // 16 == (col // 32) // 2) & (row % 16 == (col % 32) // 2)
    matrix_43 = jnp.where(same, 1.0, 0.0).astype(jnp.bfloat16)
    group = iota((8, 128), 1) // 32
    spread = [jnp.where(group == q, tiles4[gx + c], 0.0) for c in range(3) for q in range(4)]
    wide = times(jnp.concatenate(spread, axis=0), matrix_43)
    for c in range(3):
        piece = wide[32 * c : 32 * c + 32]
        grown3[c, pl.ds(LOW, 32, stride=2), :] = piece
        grown3[c, pl.ds(LOW + 1, 32, stride=2), :] = piece
    start = 8 * ((2 * gy + 4) // 8)
    answer = r["answer"]
    l3.up(gx, pl.multiple_of(start, 8), grown3, (z0_3, z1_3), answer)

    matrix_32 = jnp.where(iota((128, 128), 0) % 32 == (iota((128, 128), 1) % 64) // 2, 1.0, 0.0).astype(jnp.bfloat16)
    l2.xh.arrive(range(8))
    l2.xh.merge(l2.h - 3, l2.h + l2.n + 3)
    tile = (8, 128)
    own_group = iota(tile, 1) // 32 == iota(tile, 0) // 2
    first_half = iota(tile, 0) < 4
    spread = []
    for j in range(6):
        at = 6 + 2 * gy + j - start
        lower, own, upper = [jnp.broadcast_to(answer[c, pl.ds(at, 1), :], tile) for c in range(3)]
        spread.append(jnp.where(own_group, own, 0.0))
        spread.append(jnp.where(own_group, jnp.where(first_half, upper, lower), 0.0))
    wide = times(jnp.concatenate(spread, axis=0), matrix_32)
    l2.rows_ok = l2.row_ok()
    for p in range(12):
        l2.correct(p, wide[16 * (p // 2) : 16 * (p // 2) + 16])
    l2.third(1, 11)
    l2.fourth(2, 10, r["z2"])

    grow(r["z2"], (2, 10), 16, grow_lanes(64, 128), doubled)
    l1.xh.arrive(range(8))
    l1.xh.merge(l1.h - 3, l1.h + l1.n + 3)
    l1.rows_ok = l1.row_ok()

    def lift_1(j):
        grown = grown_plane(doubled, j, 16, 1)
        l1.correct(2 * j, grown)
        l1.correct(2 * j + 1, grown)

    loop(0, 8, lift_1, 2)
    l1.third(1, 15)
    l1.fourth(2, 14, r["z1out"])

    grow(r["z1out"], (2, 14), 24, grow_lanes(128, 256), doubled)
    l0.xh.arrive(range(8))
    l0.xh.merge(l0.h - 2, l0.h + l0.n + 2)
    l0.rows_ok = l0.row_ok()
    l0.correct(0, grown_plane(doubled, 0, 24, 2))

    def lift_0(j):
        grown = grown_plane(doubled, j, 24, 2)
        l0.correct(2 * j - 1, grown)
        l0.correct(2 * j, grown)

    loop(1, 11, lift_0)
    l0.correct(21, grown_plane(doubled, 11, 24, 2))
    l0.third(1, 21)
    l0.fourth(2, 20, l0.x2)

    def finish(y):
        p = l0.h + y
        left = l0.residual(l0.x2, p)
        for part in range(2):
            lanes = slice(128 * part, 128 * (part + 1))
            r["k_in"][part, pl.ds(y, l0.x, stride=l0.n), :] = l0.x2[p, 0 : l0.x, lanes]
            r["b_in"][part, pl.ds(y, l0.x, stride=l0.n), :] = left[0 : l0.x, lanes]

    loop(0, l0.n, finish, 2)
    stores = halves(r["solution"], r["k_in"], 4, True) + halves(r["residual"], r["b_in"], 6, True)
    for copy in stores:
        copy.start()
    for level in levels:
        for field in (level.k, level.b, level.xh):
            field.sent()
    for copy in gather_k.all + gather_b.all:
        copy.wait_send()
    for copy in stores:
        copy.wait()


SHAPES = ((256, 3, 3, 2, 3), (128, 4, 4, 3, 4), (64, 4, 4, 3, 4))
LOCAL = ("x1_", "x2_", "wx", "wy", "wz", "w", "inv", "z0_", "z1_")
WHOLE = ("k", "b", "x1_", "x2_", "wx", "wy", "wz", "w", "inv")


def per_device(count_x, count_y, right_side, coefficient):
    nx, ny, nz = right_side.shape
    vmem = lambda *shape: pltpu.VMEM(shape, F32)
    rows3 = 2 * count_y
    scratch = {
        "k_in": vmem(2, nx * ny, 128),
        "b_in": vmem(2, nx * ny, 128),
        "load": pltpu.SemaphoreType.DMA((8,)),
        "half": vmem(2, 2, nx, 128),
        "sums": vmem(nx * ny // 4, nz),
        "doubled": vmem(ny // 2 + 4, 2, nx + 16, 128),
        "z0_3": vmem(5, 24, 128),
        "z1_3": vmem(5, 24, 128),
        "left3": vmem(count_x, rows3, 128),
        "w4": vmem(6, count_x, 8, 128),
        "inv4": vmem(count_x, 8, 128),
        "tiles4": vmem(count_x + 2, 8, 128),
        "grown3": vmem(3, LOW + rows3 + HIGH, 128),
        "answer": vmem(3, 24, 128),
        "z2": vmem((ny >> 2) + 8, (nx >> 2) + 8, 128),
        "z1out": vmem((ny >> 1) + 8, (nx >> 1) + 8, 128),
    }
    for number, (lanes, halo, *_) in enumerate(SHAPES):
        rows, planes, width = nx >> number, ny >> number, max(128, lanes)
        full = (planes + 2 * halo, rows + 8, width)
        for name in ("k", "b", "xh"):
            tag = f"{name}{number}"
            scratch[tag] = vmem(*full)
            scratch[tag + "_l"] = vmem(full[0], 8, width)
            scratch[tag + "_r"] = vmem(full[0], 8, width)
            scratch[tag + "_send"] = pltpu.SemaphoreType.DMA((8,))
            scratch[tag + "_recv"] = pltpu.SemaphoreType.DMA((8,))
        for name in LOCAL:
            scratch[f"{name}{number}"] = vmem(*full)
    for name in WHOLE:
        scratch[f"{name}3"] = vmem(count_x + 2, LOW + rows3 + HIGH, 128)
    for name in ("gk", "gb"):
        scratch[name + "_first"] = vmem(4, 8, 128)
        scratch[name + "_send"] = pltpu.SemaphoreType.DMA((3 + count_y // 4 - 1 + count_x - 1,))
        scratch[name + "_recv"] = pltpu.SemaphoreType.DMA((3 + count_y // 4 - 1 + count_x - 1,))

    names = ["right_side", "coefficient", "solution", "residual"] + list(scratch)
    shape = jax.ShapeDtypeStruct((nx * ny, nz), F32)
    found = pl.pallas_call(
        functools.partial(kernel, count_x, count_y, names),
        out_shape=(shape, shape),
        in_specs=[pl.BlockSpec(memory_space=pl.ANY)] * 2,
        out_specs=(pl.BlockSpec(memory_space=pl.ANY),) * 2,
        scratch_shapes=list(scratch.values()),
        compiler_params=pltpu.CompilerParams(
            collective_id=0, has_side_effects=True, vmem_limit_bytes=56 << 20
        ),
        name="vcycle",
    )(right_side.reshape(nx * ny, nz), coefficient.reshape(nx * ny, nz))
    return tuple(value.reshape(nx, ny, nz) for value in found)


def solution(mesh):
    spec = P("gx", "gy", None)
    step = functools.partial(per_device, mesh.shape["gx"], mesh.shape["gy"])
    return jax.shard_map(step, mesh=mesh, in_specs=(spec, spec), out_specs=(spec, spec), check_vma=False)
```

```python
import functools

import jax
import jax.numpy as jnp
from jax import lax
from jax.experimental import pallas as pl
from jax.experimental.pallas import tpu as pltpu
from jax.sharding import PartitionSpec as P

MESH = pl.DeviceIdType.MESH
F32 = jnp.float32

SMOOTH_LO, SMOOTH_HI = 0.5, 2.0
COARSE_LO, COARSE_HI = 0.05, 2.0
BOTTOM = 8

STEPS = ((1, 1), (1, -1), (-1, 1), (-1, -1), (0, 1), (0, -1), (1, 0), (-1, 0))
ALONG_GX, ALONG_GY = (6, 7), (0, 1, 2, 3, 4, 5)


def coefficients(low, high, sweeps):
    theta = (high + low) / 2.0
    delta = (high - low) / 2.0
    sigma = theta / delta
    rho = 1.0 / sigma
    pairs = []
    for _ in range(sweeps - 1):
        rho_next = 1.0 / (2.0 * sigma - rho)
        pairs.append((rho_next * rho, 2.0 * rho_next / delta))
        rho = rho_next
    return theta, pairs


THETA, ((MOMENTUM, STEP),) = coefficients(SMOOTH_LO, SMOOTH_HI, 2)


def harmonic(own, other):
    return 2.0 * own * other / (own + other)


def roll(value, shift, axis):
    size = value.shape[axis]
    return pltpu.roll(value, shift % size, axis)


def iota(shape, dim):
    return lax.broadcasted_iota(jnp.int32, shape, dim)


def times(rows, matrix):
    high = rows.astype(jnp.bfloat16)
    rest = rows - high.astype(F32)
    middle = rest.astype(jnp.bfloat16)
    low = (rest - middle.astype(F32)).astype(jnp.bfloat16)
    found = [jnp.dot(term, matrix, preferred_element_type=F32) for term in (low, middle, high)]
    return (found[0] + found[1]) + found[2]


def loop(start, stop, body, unroll=1):
    count = (stop - start) // unroll

    def step(index, carry):
        for k in range(unroll):
            body(start + index * unroll + k)
        return carry

    if count > 1:
        lax.fori_loop(0, count, step, 0)
        start += count * unroll
    for index in range(start, stop):
        body(index)


class Exchange:
    def __init__(self, field, landing, send, recv, halo, depth, corner):
        self.field, self.wide = field, landing is None
        self.left, self.right = (None, None) if self.wide else landing
        self.send, self.recv = send, recv
        self.halo, self.depth, self.corner = halo, depth, corner
        self.planes = field.shape[0] - 2 * halo
        self.rows = field.shape[1] - (16 if self.wide else 8)

    def copies(self, place):
        h, n, r, x = self.halo, self.planes, self.depth, self.rows
        found = []
        for number, (dx, dy) in enumerate(STEPS):
            if dx == 0:
                source_plane = h + n - r if dy > 0 else h
                target_plane = h - r if dy > 0 else h + n
                source = self.field.at[pl.ds(source_plane, r), pl.ds(0, x)]
                target = self.field.at[pl.ds(target_plane, r), pl.ds(0, x)]
            else:
                count = n if dy == 0 else self.corner
                source_plane = h if dy <= 0 else h + n - count
                target_plane = h if dy == 0 else (h - count if dy > 0 else h + n)
                source = self.field.at[pl.ds(source_plane, count), pl.ds(x - 8 if dx > 0 else 0, 8)]
                if self.wide:
                    target = self.field.at[pl.ds(target_plane, count), pl.ds(x + 8 if dx > 0 else x, 8)]
                else:
                    landing = self.left if dx > 0 else self.right
                    target = landing.at[pl.ds(target_plane, count)]
            found.append(
                pltpu.make_async_remote_copy(
                    src_ref=source,
                    dst_ref=target,
                    send_sem=self.send.at[number],
                    recv_sem=self.recv.at[number],
                    device_id=place(dx, dy),
                    device_id_type=MESH,
                )
            )
        return found

    def start(self, place):
        self.started = self.copies(place)
        for copy in self.started:
            copy.start()

    def arrive(self, which):
        for number in which:
            self.started[number].wait_recv()

    def merge(self, start, stop):
        if self.wide:
            return
        x = self.rows
        shape = (8, self.field.shape[2])

        def body(p):
            upper = iota(shape, 0) < 4
            self.field[p, x:, :] = jnp.where(upper, self.right[p], self.left[p])

        loop(start, stop, body, 4)

    def merge_mended(self, start, stop, at_low, at_high):
        x = self.rows
        shape = (8, self.field.shape[2])
        row = iota(shape, 0)
        take_high = jnp.where(row == 0, at_high, 0) == 1
        take_low = jnp.where(row == 7, at_low, 0) == 1
        upper = row < 4

        def ends(p):
            high, low = self.field[p, x : x + 8, :], self.field[p, x + 8 :, :]
            self.field[p, x : x + 8, :] = jnp.where(take_high, roll(self.field[p, x - 8 : x, :], 1, 0), high)
            self.field[p, x + 8 :, :] = jnp.where(take_low, roll(self.field[p, 0:8, :], 7, 0), low)

        if self.wide:
            loop(start, stop, ends, 4)
            return

        def body(p):
            tile = jnp.where(upper, self.right[p], self.left[p])
            tile = jnp.where(take_high, roll(self.field[p, x - 8 : x, :], 1, 0), tile)
            self.field[p, x:, :] = jnp.where(take_low, roll(self.field[p, 0:8, :], 7, 0), tile)

        loop(start, stop, body, 4)

    def sent(self):
        for copy in self.started:
            copy.wait_send()


class Level:
    def __init__(self, number, lanes, refs, gx, gy, counts):
        self.scale = 0.25**number
        self.lanes = lanes
        self.gx, self.gy = gx, gy
        self.count_x, self.count_y = counts
        (self.k, self.b, self.xh, self.x1, self.x2, self.wx, self.wy, self.wz, self.w, self.inv, self.z0, self.z1) = refs
        self.h = self.k.halo
        self.n = self.k.planes
        self.x = self.k.rows
        self.shape = self.k.field.shape[1:]
        self.period = lanes
        self.unroll = 2 if number == 0 else 4

    def merge_k(self, start, stop):
        at_low = jnp.where(self.gx == 0, 1, 0)
        at_high = jnp.where(self.gx == self.count_x - 1, 1, 0)
        self.k.merge_mended(start, stop, at_low, at_high)

    def row_ok(self):
        row = iota(self.shape, 0)
        below = jnp.where(self.gx == 0, 1, 0)
        above = jnp.where(self.gx == self.count_x - 1, 1, 0)
        middle = (self.x + self.shape[0]) // 2
        bad_low = jnp.where(row >= middle, below, 0)
        bad_high = jnp.where((row >= self.x) & (row < middle), above, 0)
        return (bad_low + bad_high) == 0

    def plane_ok(self, p):
        y = self.gy * self.n + p - self.h
        return (y >= 0) & (y < self.count_y * self.n)

    def mend_planes(self):
        field, h, n = self.k.field, self.h, self.n

        @pl.when(self.gy == 0)
        def _():
            field[h - 1] = field[h]

        @pl.when(self.gy == self.count_y - 1)
        def _():
            field[h + n] = field[h + n - 1]

    def lane(self):
        return iota(self.shape, 1) % self.period

    def faces(self, start, stop):
        k = self.k.field

        def body(p):
            own = k[p]
            self.wx[p] = harmonic(own, roll(own, -1, 0))
            along = harmonic(own, roll(own, -1, 1))
            self.wz[p] = jnp.where(self.lane() == self.period - 1, 0.0, along)

        loop(start, stop, body, self.unroll)

    def faces_y(self, start, stop):
        k = self.k.field

        def body(p):
            self.wy[p] = harmonic(k[p], k[p + 1])

        loop(start, stop, body, self.unroll)

    def totals(self, start, stop):
        k = self.k.field
        rows_ok = self.row_ok()

        def body(p):
            wx, wz = self.wx[p], self.wz[p]
            lane = self.lane()
            edge = jnp.where((lane == 0) | (lane == self.period - 1), k[p], 0.0)
            total = wx + roll(wx, 1, 0) + self.wy[p] + self.wy[p - 1] + wz + roll(wz, 1, 1) + edge
            self.w[p] = total
            ok = rows_ok & self.plane_ok(p)
            self.inv[p] = jnp.where(ok, 1.0 / total, 0.0)

        loop(start, stop, body, self.unroll)

    def beside(self, field, p):
        own, wx, wz = field[p], self.wx[p], self.wz[p]
        found = wx * roll(own, -1, 0) + roll(wx * own, 1, 0)
        found = found + self.wy[p] * field[p + 1] + self.wy[p - 1] * field[p - 1]
        return found + wz * roll(own, -1, 1) + roll(wz * own, 1, 1)

    def first(self, start, stop):
        def body(p):
            self.x1[p] = self.b[p] * self.inv[p] * (1.0 / (THETA * self.scale))

        loop(start, stop, body, self.unroll)

    def second(self, margin):
        h, n, x = self.h, self.n, self.x

        def value(p):
            own = self.x1[p]
            factor = 1.0 + MOMENTUM + STEP * (THETA - 1.0)
            return factor * own + STEP * (self.inv[p] * self.beside(self.x1, p))

        def plain(p):
            self.x2[p] = value(p)

        def kept(p):
            found = value(p)
            self.x2[p] = found
            self.xh.field[p, 0:x, 0 : found.shape[1]] = found[0:x, :]

        if self.xh is None:
            loop(h - margin, h + n + margin, plain, self.unroll)
            return
        loop(h, h + n, kept, self.unroll)
        for p in list(range(h - margin, h)) + list(range(h + n, h + n + margin)):
            plain(p)

    def residual(self, field, p):
        return self.b[p] - self.scale * (self.w[p] * field[p] - self.beside(field, p))

    def correct(self, p, grown):
        ok = self.rows_ok & self.plane_ok(p)
        base = self.x2[p] if self.xh is None else self.xh.field[p, :, 0 : self.shape[1]]
        self.z0[p] = jnp.where(ok, base + grown, 0.0)

    def third(self, start, stop):
        def body(p):
            own = self.z0[p]
            flow = self.inv[p] * self.beside(self.z0, p)
            self.z1[p] = (1.0 - 1.0 / THETA) * own + self.x1[p] + (1.0 / THETA) * flow

        loop(start, stop, body, self.unroll)

    def fourth(self, start, stop, target):
        def body(p):
            own = self.z1[p]
            flow = self.inv[p] * self.beside(self.z1, p)
            found = (1.0 + MOMENTUM - STEP) * own - MOMENTUM * self.z0[p]
            target[p] = found + (STEP * THETA) * self.x1[p] + STEP * flow

        loop(start, stop, body, self.unroll)


LOW, HIGH = 8, 16


class Whole:
    def __init__(self, refs):
        self.scale = 0.25**3
        self.size_z = 32
        self.k, self.b, self.x1, self.x2, self.wx, self.wy, self.wz, self.w, self.inv = refs
        self.count = self.k.shape[0] - 2
        self.rows = self.k.shape[1] - LOW - HIGH
        self.shape = (self.rows, 128)

    def blank(self):
        for ref in (self.k, self.x1, self.x2, self.wx, self.wy, self.wz, self.inv):
            empty = jnp.zeros(ref.shape[1:], F32)
            ref[0] = empty
            ref[self.count + 1] = empty

            def body(g, ref=ref):
                ref[g, 0:LOW, :] = jnp.zeros((LOW, 128), F32)
                ref[g, LOW + self.rows :, :] = jnp.zeros((HIGH, 128), F32)

            loop(1, self.count + 1, body, 4)

    def at(self, ref, g):
        return ref[g, LOW : LOW + self.rows, :]

    def after(self, own, following):
        inner = iota(own.shape, 1) < 128 - self.size_z
        return jnp.where(inner, roll(own, -self.size_z, 1), roll(following, -self.size_z, 1))

    def before(self, own, previous):
        inner = iota(own.shape, 1) >= self.size_z
        return jnp.where(inner, roll(own, self.size_z, 1), roll(previous, self.size_z, 1))

    def weights(self):
        rows, inside = self.rows, slice(LOW, LOW + self.rows)

        def faces(g):
            own, following = self.at(self.k, g), self.at(self.k, g + 1)
            lane, row = iota(self.shape, 1), iota(self.shape, 0)
            end = jnp.where(lane >= 128 - self.size_z, jnp.where(g == self.count, 1, 0), 0)
            self.wx[g, inside, :] = jnp.where(end == 1, 0.0, harmonic(own, self.after(own, following)))
            self.wy[g, inside, :] = jnp.where(row == rows - 1, 0.0, harmonic(own, roll(own, -1, 0)))
            last = lane % self.size_z == self.size_z - 1
            self.wz[g, inside, :] = jnp.where(last, 0.0, harmonic(own, roll(own, -1, 1)))

        loop(1, self.count + 1, faces)

        def totals(g):
            lane, row = iota(self.shape, 1), iota(self.shape, 0)
            high = jnp.where(lane >= 128 - self.size_z, jnp.where(g == self.count, 1.0, 0.0), 0.0)
            low = jnp.where(lane < self.size_z, jnp.where(g == 1, 1.0, 0.0), 0.0)
            edge = high + low
            edge = edge + jnp.where((row == 0) | (row == rows - 1), 1.0, 0.0)
            z = lane % self.size_z
            edge = edge + jnp.where((z == 0) | (z == self.size_z - 1), 1.0, 0.0)
            wx, wy, wz = self.at(self.wx, g), self.at(self.wy, g), self.at(self.wz, g)
            total = wx + self.before(wx, self.at(self.wx, g - 1)) + wy + roll(wy, 1, 0) + wz + roll(wz, 1, 1)
            total = total + edge * self.at(self.k, g)
            self.w[g, inside, :] = total
            self.inv[g, inside, :] = 1.0 / total

        loop(1, self.count + 1, totals)

    def flow(self, fields, weights):
        previous, own, following = fields
        wx_previous, wx, wy, wz = weights
        found = wx * self.after(own, following) + self.before(wx * own, wx_previous * previous)
        found = found + wy * roll(own, -1, 0) + roll(wy * own, 1, 0)
        return found + wz * roll(own, -1, 1) + roll(wz * own, 1, 1)

    def beside(self, field, g):
        fields = [self.at(field, g + step) for step in (-1, 0, 1)]
        weights = [self.at(self.wx, g - 1)] + [self.at(ref, g) for ref in (self.wx, self.wy, self.wz)]
        return self.flow(fields, weights)

    def down(self, left):
        inside = slice(LOW, LOW + self.rows)

        def first(g):
            found = self.at(self.b, g) * self.at(self.inv, g) * (1.0 / (THETA * self.scale))
            self.x1[g, inside, :] = found

        loop(1, self.count + 1, first, 2)

        def second(g):
            factor = 1.0 + MOMENTUM + STEP * (THETA - 1.0)
            moved = self.at(self.inv, g) * self.beside(self.x1, g)
            self.x2[g, inside, :] = factor * self.at(self.x1, g) + STEP * moved

        loop(1, self.count + 1, second, 2)

        def residual(g):
            applied = self.at(self.w, g) * self.at(self.x2, g) - self.beside(self.x2, g)
            left[g - 1] = self.at(self.b, g) - self.scale * applied

        loop(1, self.count + 1, residual, 2)

    def up(self, gx, start, grown, held, answer):
        span = pl.ds(start, 24)
        z0, z1 = held
        planes = (0, 1, 2)
        part = lambda ref, c: ref[gx + c, span, :]
        for c in planes:
            z0[c + 1] = part(self.x2, c) + grown[c, span, :]

        def flow(field, c):
            fields = [field[c + step] for step in (0, 1, 2)]
            before = self.wx[jnp.maximum(gx + c - 1, 0), span, :]
            return part(self.inv, c) * self.flow(fields, [before, part(self.wx, c), part(self.wy, c), part(self.wz, c)])

        for c in planes:
            z1[c + 1] = (1.0 - 1.0 / THETA) * z0[c + 1] + part(self.x1, c) + (1.0 / THETA) * flow(z0, c)
        for c in planes:
            found = (1.0 + MOMENTUM - STEP) * z1[c + 1] - MOMENTUM * z0[c + 1]
            answer[c] = found + (STEP * THETA) * part(self.x1, c) + STEP * flow(z1, c)


class Deepest:
    def __init__(self, count):
        self.count = count
        self.scale = 0.25**4
        shape = (8, 128)
        self.lane, self.row = iota(shape, 1), iota(shape, 0)
        self.low_x = (self.lane % 32) < 16
        self.zero = jnp.zeros(shape, F32)

    def next_x(self, tiles):
        back, ahead = [roll(t, -16, 1) for t in tiles], [roll(t, 16, 1) for t in tiles] + [self.zero]
        return [jnp.where(self.low_x, back[g], ahead[g + 1]) for g in range(self.count)]

    def last_x(self, tiles):
        back, ahead = [self.zero] + [roll(t, -16, 1) for t in tiles], [roll(t, 16, 1) for t in tiles]
        return [jnp.where(self.low_x, back[g], ahead[g]) for g in range(self.count)]

    def next_y(self, tiles):
        moved = [roll(t, -1, 0) for t in tiles]
        return [jnp.where(self.row < 7, t, roll(t, -32, 1)) for t in moved]

    def last_y(self, tiles):
        moved = [roll(t, 1, 0) for t in tiles]
        return [jnp.where(self.row > 0, t, roll(t, 32, 1)) for t in moved]

    def next_z(self, tiles):
        return [roll(t, -1, 1) for t in tiles]

    def last_z(self, tiles):
        return [roll(t, 1, 1) for t in tiles]

    def weights(self, k, weight_refs, inv_ref):
        lane, row, span = self.lane, self.row, range(self.count)
        z = lane % 16
        end_y = (row == 7) & (lane >= 96)
        edge = jnp.where((z == 0) | (z == 15), 1.0, 0.0)
        edge = edge + jnp.where(end_y | ((row == 0) & (lane < 32)), 1.0, 0.0)
        faces_x = [harmonic(a, b) for a, b in zip(k, self.next_x(k))]
        faces_x[-1] = jnp.where(self.low_x, faces_x[-1], 0.0)
        faces_y = [jnp.where(end_y, 0.0, harmonic(a, b)) for a, b in zip(k, self.next_y(k))]
        faces_z = [jnp.where(z == 15, 0.0, harmonic(a, b)) for a, b in zip(k, self.next_z(k))]
        sets = [faces_x, self.last_x(faces_x), faces_y, self.last_y(faces_y), faces_z, self.last_z(faces_z)]
        for g in span:
            total = edge * k[g]
            if g == 0:
                total = total + jnp.where(self.low_x, k[g], 0.0)
            if g == self.count - 1:
                total = total + jnp.where(self.low_x, 0.0, k[g])
            for one in sets:
                total = total + one[g]
            inv = 1.0 / total
            inv_ref[g] = inv
            for number, one in enumerate(sets):
                weight_refs[number, g] = one[g] * inv

    def solve(self, b, weight_refs, inv_ref):
        theta, pairs = coefficients(COARSE_LO, COARSE_HI, BOTTOM)
        span = range(self.count)
        scaled = [b[g] * inv_ref[g] * (1.0 / self.scale) for g in span]
        update = [t * (1.0 / theta) for t in scaled]
        found = update
        for momentum, step in pairs:
            shifted = [
                self.next_x(found),
                self.last_x(found),
                self.next_y(found),
                self.last_y(found),
                self.next_z(found),
                self.last_z(found),
            ]
            following = []
            for g in span:
                flow = weight_refs[0, g] * shifted[0][g]
                for number in range(1, 6):
                    flow = flow + weight_refs[number, g] * shifted[number][g]
                following.append(momentum * update[g] + step * ((scaled[g] - found[g]) + flow))
            update = following
            found = [a + d for a, d in zip(found, update)]
        return found


def shrink_lanes(lanes, kept):
    row, col = iota((max(lanes, 128), 128), 0), iota((max(lanes, 128), 128), 1)
    return jnp.where((row // 2 == col % kept) & (row < lanes), 0.125, 0.0).astype(jnp.bfloat16)


def grow_lanes(kept, lanes):
    row, col = iota((128, lanes), 0), iota((128, lanes), 1)
    period = 2 * kept
    return jnp.where((col % period) // 2 == row, 1.0, 0.0).astype(jnp.bfloat16)


def restrict(read, target, count, fine_plane, coarse_plane, rows, matrix, half, sums):
    kept = rows // 2
    parts = matrix.shape[0] // 128

    def body(j):
        pair = read(fine_plane + 2 * j) + read(fine_plane + 2 * j + 1)
        slot = j % 2
        for part in range(parts):
            half[slot, part, 0:rows, :] = pair[:, part * 128 : (part + 1) * 128]
        for part in range(parts):
            even = half[slot, part, pl.ds(0, kept, stride=2), :]
            odd = half[slot, part, pl.ds(1, kept, stride=2), :]
            sums[pl.ds(pl.multiple_of(j * kept, 8), kept), 128 * part : 128 * (part + 1)] = even + odd

    loop(0, count, body, 2)
    means = times(sums[0 : count * kept, 0 : 128 * parts], matrix)
    target[coarse_plane : coarse_plane + count, 0:kept, :] = means.reshape(count, kept, 128)


def grow(source, planes, rows, matrix, doubled):
    start, stop = planes
    count, parts = stop - start, matrix.shape[1] // 128
    wide = times(source[start:stop].reshape(count * rows, 128), matrix)
    for j in range(count):
        for part in range(parts):
            piece = wide[j * rows : (j + 1) * rows, 128 * part : 128 * (part + 1)]
            doubled[j, part, pl.ds(0, rows, stride=2), :] = piece
            doubled[j, part, pl.ds(1, rows, stride=2), :] = piece


def grown_plane(doubled, j, rows, parts):
    own = 2 * (rows - 16)
    upper = iota((8, 128), 0) < 4
    found = []
    for part in range(parts):
        tail = jnp.where(upper, doubled[j, part, own : own + 8, :], doubled[j, part, own + 24 : own + 32, :])
        found.append(jnp.concatenate([doubled[j, part, 0:own, :], tail], axis=0))
    return found[0] if parts == 1 else jnp.concatenate(found, axis=1)


def kernel(count_x, count_y, names, *refs):
    r = dict(zip(names, refs))
    gx, gy = lax.axis_index("gx"), lax.axis_index("gy")
    ring_x = 4
    ring_z = count_y // ring_x
    chip_x, chip_z = gy % ring_x, gy // ring_x

    def place(dx, dy):
        return ((gx + dx + count_x) % count_x, (gy + dy + count_y) % count_y)

    def along_x(d):
        return (gx, chip_z * ring_x + (chip_x + d) % ring_x)

    def along_z(d):
        return (gx, ((chip_z + d) % ring_z) * ring_x + chip_x)

    def along_gx(d):
        return ((gx + d) % count_x, gy)

    z_steps = [d for d in range(1, ring_z) if min(d, ring_z - d) <= 3]
    partners = [place(dx, dy) for dx, dy in STEPS]
    partners += [along_x(d) for d in range(1, ring_x)]
    partners += [along_z(d) for d in z_steps]
    partners += [along_gx(d) for d in range(1, count_x)]

    def halves(whole, staged, first, store):
        copies = []
        for part in range(2):
            wide = whole.at[:, pl.ds(128 * part, 128)]
            pair = (staged.at[part], wide) if store else (wide, staged.at[part])
            copies.append(pltpu.make_async_copy(*pair, r["load"].at[first + part]))
        return copies

    loads_k = halves(r["coefficient"], r["k_in"], 0, False)
    loads_b = halves(r["right_side"], r["b_in"], 2, False)
    for copy in loads_k + loads_b:
        copy.start()
    barrier = pltpu.get_barrier_semaphore()
    for partner in partners:
        pl.semaphore_signal(barrier, inc=1, device_id=partner, device_id_type=MESH)

    def exchange(name, number, halo, depth):
        tag = f"{name}{number}"
        if not depth:
            return None
        landing = (r[tag + "_l"], r[tag + "_r"]) if tag + "_l" in r else None
        corner = depth if number == 2 else depth - 1
        return Exchange(r[tag], landing, r[tag + "_send"], r[tag + "_recv"], halo, depth, corner)

    levels, sources = [], []
    for number, (lanes, halo, depth_k, depth_b, depth_x) in enumerate(SHAPES):
        sources.append(exchange("b", number, halo, depth_b))
        fields = [exchange("k", number, halo, depth_k), r[f"b{number}"], exchange("xh", number, halo, depth_x)]
        fields += [r[f"{name}{number}"] for name in LOCAL]
        levels.append(Level(number, lanes, fields, gx, gy, (count_x, count_y)))
    l0, l1, l2 = levels
    l3 = Whole([r[f"{name}3"] for name in WHOLE])
    l4 = Deepest(count_x)

    def turn(staged, target):
        for y in range(l0.n):
            for part in range(2):
                lanes = pl.ds(128 * part, 128)
                target[l0.h + y, 0 : l0.x, lanes] = staged[part, pl.ds(y, l0.x, stride=l0.n), :]

    for copy in loads_k:
        copy.wait()
    turn(r["k_in"], r["k0"])
    for copy in loads_b:
        copy.wait()
    turn(r["b_in"], r["b0"])
    pl.semaphore_wait(barrier, len(partners))
    l0.k.start(place)
    sources[0].start(place)

    half, sums, doubled = r["half"], r["sums"], r["doubled"]
    k0, k1, k2 = r["k0"], r["k1"], r["k2"]
    to_1, to_2 = shrink_lanes(256, 128), shrink_lanes(128, 64)
    restrict(lambda p: k0[p, 0 : l0.x, :], k1, l1.n, l0.h, l1.h, l0.x, to_1, half, sums)
    l1.k.start(place)
    restrict(lambda p: k1[p, 0 : l1.x, :], k2, l2.n, l1.h, l2.h, l1.x, to_2, half, sums)
    l2.k.start(place)

    def small_block(read):
        row, col = iota((128, 128), 0), iota((128, 128), 1)
        matrix = jnp.where((row < 64) & (row // 2 == col % 32), 0.125, 0.0).astype(jnp.bfloat16)
        tile = (8, 128)
        mine = iota(tile, 1) // 32 == iota(tile, 0) // 2
        pairs = [read(l2.h + 2 * j) + read(l2.h + 2 * j + 1) for j in range(2)]
        means = times(jnp.concatenate(pairs, axis=0), matrix)
        found = jnp.zeros(tile, F32)
        for j in range(2):
            spread = jnp.where(mine, means[8 * j : 8 * j + 8], 0.0)
            line = jnp.sum(spread, axis=0, keepdims=True)
            found = jnp.where(iota(tile, 0) == 2 * chip_x + j, jnp.broadcast_to(line, tile), found)
        return found

    class Gather:
        def __init__(self, name, target):
            self.first, self.target = r[name + "_first"], target
            self.send, self.recv = r[name + "_send"], r[name + "_recv"]
            self.all = []

        def go(self, base, source, target, where, steps):
            copies = []
            for d in steps:
                copies.append(
                    pltpu.make_async_remote_copy(
                        src_ref=source,
                        dst_ref=target,
                        send_sem=self.send.at[base + d - 1],
                        recv_sem=self.recv.at[base + d - 1],
                        device_id=where(d),
                        device_id_type=MESH,
                    )
                )
            for copy in copies:
                copy.start()
            self.now = copies
            self.all += copies

        def along_x(self, tile):
            self.first[chip_x] = tile
            slot = self.first.at[chip_x]
            self.go(0, slot, slot, along_x, range(1, ring_x))

        def along_z(self):
            self.arrive()
            rows = pl.ds(pl.multiple_of(8 * chip_z + LOW, 8), 8)
            found = self.first[0]
            for slot in range(1, ring_x):
                found = found + self.first[slot]
            self.target[gx + 1, rows, :] = found
            part = self.target.at[gx + 1, rows]
            self.go(ring_x - 1, part, part, along_z, z_steps)

        def along_gx(self):
            self.arrive()
            part = self.target.at[gx + 1, pl.ds(LOW, 8 * ring_z)]
            self.go(ring_x + ring_z - 2, part, part, along_gx, range(1, count_x))

        def arrive(self):
            for copy in self.now:
                copy.wait_recv()

    gather_k, gather_b = Gather("gk", l3.k), Gather("gb", l3.b)
    gather_k.along_x(small_block(lambda p: k2[p, 0 : l2.x, :]))
    l3.blank()
    for d in range(1, ring_z):
        if d not in z_steps:
            unused = pl.ds(pl.multiple_of(8 * ((chip_z + d) % ring_z) + LOW, 8), 8)
            l3.k[gx + 1, unused, :] = jnp.ones((8, 128), F32)
            l3.b[gx + 1, unused, :] = jnp.zeros((8, 128), F32)
    z0_3, z1_3 = r["z0_3"], r["z1_3"]
    for held in (z0_3, z1_3):
        held[0] = jnp.zeros((24, 128), F32)
        held[4] = jnp.zeros((24, 128), F32)
    grown3 = r["grown3"]
    for c in range(3):
        grown3[c, 0:LOW, :] = jnp.zeros((LOW, 128), F32)
        grown3[c, LOW + 8 * ring_z :, :] = jnp.zeros((HIGH, 128), F32)

    def ready(level):
        h, n, depth = level.h, level.n, level.k.depth
        level.k.arrive(ALONG_GX)
        level.merge_k(h, h + n)
        level.faces(h, h + n)
        level.faces_y(h, h + n - 1)
        level.totals(h + 1, h + n - 1)
        level.k.arrive(ALONG_GY)
        low, high = h - depth + 1, h + n + depth - 1
        level.merge_k(h - level.k.corner, h)
        level.merge_k(h + n, h + n + level.k.corner)
        level.mend_planes()
        level.faces(low, h)
        level.faces(h + n, high)
        level.faces_y(h - depth, h)
        level.faces_y(h + n - 1, high)
        level.totals(low, h + 1)
        level.totals(h + n - 1, high)

    def descend(level, source, depth):
        h, n = level.h, level.n
        if source is not None:
            source.arrive(range(8))
            source.merge(h - depth + 1, h + n + depth - 1)
        level.first(h - depth, h + n + depth)
        level.second(depth - 1)

    def source_below(level, target, margin, rows, matrix):
        below = levels[levels.index(level) + 1]
        read = lambda p: level.residual(level.x2, p)[0:rows, :]
        count, fine = below.n + 2 * margin, level.h - 2 * margin
        restrict(read, target, count, fine, below.h - margin, rows, matrix, half, sums)

    ready(l0)
    descend(l0, sources[0], 2)
    source_below(l0, r["b1"], 0, l0.x, shrink_lanes(256, 128))
    sources[1].start(place)
    l0.xh.start(place)
    gather_k.along_z()
    ready(l1)
    descend(l1, sources[1], 6)
    source_below(l1, r["b2"], 2, l1.x + 16, shrink_lanes(128, 64))
    gather_k.along_gx()
    ready(l2)
    descend(l2, None, 2)
    gather_b.along_x(small_block(lambda p: l2.residual(l2.x2, p)[0 : l2.x, :]))
    for p in range(l2.h, l2.h + l2.n):
        l2.xh.field[p, 0 : l2.x, 128:] = l2.x1[p, 0 : l2.x, :]
    l2.xh.start(place)

    def to_bottom(source, low):
        row, col = iota((128, 128), 0), iota((128, 128), 1)
        same_x = (row // 32) // 2 == (col % 32) // 16
        same_z = (row % 32) // 2 == col % 16
        matrix = jnp.where(same_x & same_z, 0.125, 0.0).astype(jnp.bfloat16)
        kept = 4 * ring_z
        pieces = []
        for g in range(count_x):
            even = source[g, pl.ds(low, kept, stride=2), :]
            odd = source[g, pl.ds(low + 1, kept, stride=2), :]
            pieces.append(even + odd)
        means = times(jnp.concatenate(pieces, axis=0), matrix)
        group = iota((8, 128), 1) // 32
        tiles = []
        for g in range(count_x):
            found = means[g * kept : g * kept + 8]
            for q in range(1, 4):
                found = jnp.where(group == q, means[g * kept + 8 * q : g * kept + 8 * q + 8], found)
            tiles.append(found)
        return tiles

    gather_k.arrive()
    l3.weights()
    l4.weights(to_bottom(l3.k.at[pl.ds(1, count_x)], LOW), r["w4"], r["inv4"])
    gather_b.along_z()
    gather_b.along_gx()
    for field in [level.k for level in levels] + sources[:2] + [l0.xh, l2.xh]:
        field.sent()
    for copy in gather_k.all:
        copy.wait_send()
    gather_b.arrive()
    l3.down(r["left3"])
    deepest = l4.solve(to_bottom(r["left3"], 0), r["w4"], r["inv4"])
    tiles4 = r["tiles4"]
    tiles4[0] = l4.zero
    tiles4[count_x + 1] = l4.zero
    for g in range(count_x):
        tiles4[g + 1] = deepest[g]

    row, col = iota((128, 128), 0), iota((128, 128), 1)
    same = ((row % 32) // 16 == (col // 32) // 2) & (row % 16 == (col % 32) // 2)
    matrix_43 = jnp.where(same, 1.0, 0.0).astype(jnp.bfloat16)
    group = iota((8, 128), 1) // 32
    spread = [jnp.where(group == q, tiles4[gx + c], 0.0) for c in range(3) for q in range(4)]
    wide = times(jnp.concatenate(spread, axis=0), matrix_43)
    for c in range(3):
        piece = wide[32 * c : 32 * c + 32]
        grown3[c, pl.ds(LOW, 32, stride=2), :] = piece
        grown3[c, pl.ds(LOW + 1, 32, stride=2), :] = piece
    start = 8 * ((2 * gy + 4) // 8)
    answer = r["answer"]
    l3.up(gx, pl.multiple_of(start, 8), grown3, (z0_3, z1_3), answer)

    matrix_32 = jnp.where(iota((128, 128), 0) % 32 == (iota((128, 128), 1) % 64) // 2, 1.0, 0.0).astype(jnp.bfloat16)
    l2.xh.arrive(range(8))
    l2.xh.merge(0, 2 * l2.h + l2.n)
    tile = (8, 128)
    own_group = iota(tile, 1) // 32 == iota(tile, 0) // 2
    first_half = iota(tile, 0) < 4
    spread = []
    for j in range(6):
        at = 6 + 2 * gy + j - start
        lower, own, upper = [jnp.broadcast_to(answer[c, pl.ds(at, 1), :], tile) for c in range(3)]
        spread.append(jnp.where(own_group, own, 0.0))
        spread.append(jnp.where(own_group, jnp.where(first_half, upper, lower), 0.0))
    wide = times(jnp.concatenate(spread, axis=0), matrix_32)
    l2.rows_ok = l2.row_ok()
    for p in range(1, 11):
        l2.x1[p] = jnp.where(l2.rows_ok & l2.plane_ok(p), l2.xh.field[p, :, 128:], 0.0)
    for p in range(12):
        l2.correct(p, wide[16 * (p // 2) : 16 * (p // 2) + 16])
    l2.third(1, 11)
    l2.fourth(2, 10, r["z2"])

    grow(r["z2"], (2, 10), 16, grow_lanes(64, 128), doubled)
    l1.rows_ok = l1.row_ok()

    def lift_1(j):
        grown = doubled[j, 0, 0 : l1.x + 16, :]
        l1.correct(l1.h - 4 + 2 * j, grown)
        l1.correct(l1.h - 3 + 2 * j, grown)

    loop(0, 8, lift_1, 2)
    l1.third(l1.h - 3, l1.h + l1.n + 3)
    l1.fourth(l1.h - 2, l1.h + l1.n + 2, r["z1out"])

    grow(r["z1out"], (l1.h - 2, l1.h + l1.n + 2), 32, grow_lanes(128, 256), doubled)
    l0.xh.arrive(range(8))
    l0.xh.merge(l0.h - 2, l0.h + l0.n + 2)
    l0.rows_ok = l0.row_ok()
    l0.correct(0, grown_plane(doubled, 0, 32, 2))

    def lift_0(j):
        grown = grown_plane(doubled, j, 32, 2)
        l0.correct(2 * j - 1, grown)
        l0.correct(2 * j, grown)

    loop(1, 11, lift_0)
    l0.correct(21, grown_plane(doubled, 11, 32, 2))
    l0.third(1, 21)
    l0.fourth(2, 20, l0.x2)

    def finish(y):
        p = l0.h + y
        left = l0.residual(l0.x2, p)
        for part in range(2):
            lanes = slice(128 * part, 128 * (part + 1))
            r["k_in"][part, pl.ds(y, l0.x, stride=l0.n), :] = l0.x2[p, 0 : l0.x, lanes]
            r["b_in"][part, pl.ds(y, l0.x, stride=l0.n), :] = left[0 : l0.x, lanes]

    loop(0, l0.n, finish, 2)
    stores = halves(r["solution"], r["k_in"], 4, True) + halves(r["residual"], r["b_in"], 6, True)
    for copy in stores:
        copy.start()
    for copy in gather_b.all:
        copy.wait_send()
    for copy in stores:
        copy.wait()


SHAPES = ((256, 3, 3, 2, 3), (128, 7, 7, 6, 0), (64, 4, 4, 0, 4))
LOCAL = ("x1_", "x2_", "wx", "wy", "wz", "w", "inv", "z0_", "z1_")
WHOLE = ("k", "b", "x1_", "x2_", "wx", "wy", "wz", "w", "inv")


def per_device(count_x, count_y, right_side, coefficient):
    nx, ny, nz = right_side.shape
    vmem = lambda *shape: pltpu.VMEM(shape, F32)
    rows3 = 2 * count_y
    scratch = {
        "k_in": vmem(2, nx * ny, 128),
        "b_in": vmem(2, nx * ny, 128),
        "load": pltpu.SemaphoreType.DMA((8,)),
        "half": vmem(2, 2, nx, 128),
        "sums": vmem(nx * ny // 4, nz),
        "doubled": vmem(ny // 2 + 4, 2, nx + 32, 128),
        "z0_3": vmem(5, 24, 128),
        "z1_3": vmem(5, 24, 128),
        "left3": vmem(count_x, rows3, 128),
        "w4": vmem(6, count_x, 8, 128),
        "inv4": vmem(count_x, 8, 128),
        "tiles4": vmem(count_x + 2, 8, 128),
        "grown3": vmem(3, LOW + rows3 + HIGH, 128),
        "answer": vmem(3, 24, 128),
        "z2": vmem((ny >> 2) + 8, (nx >> 2) + 8, 128),
        "z1out": vmem((ny >> 1) + 14, (nx >> 1) + 16, 128),
    }
    for number, (lanes, halo, *depths) in enumerate(SHAPES):
        rows, planes, width = nx >> number, ny >> number, max(128, lanes)
        wide = number == 1
        full = (planes + 2 * halo, rows + (16 if wide else 8), width)
        scratch[f"b{number}"] = vmem(*full)
        for name, depth in zip(("k", "b", "xh"), depths):
            if not depth:
                continue
            tag = f"{name}{number}"
            lanes_sent = 2 * width if tag == "xh2" else width
            scratch[tag] = vmem(*full[:2], lanes_sent)
            if not wide:
                scratch[tag + "_l"] = vmem(full[0], 8, lanes_sent)
                scratch[tag + "_r"] = vmem(full[0], 8, lanes_sent)
            scratch[tag + "_send"] = pltpu.SemaphoreType.DMA((8,))
            scratch[tag + "_recv"] = pltpu.SemaphoreType.DMA((8,))
        for name in LOCAL:
            scratch[f"{name}{number}"] = vmem(*full)
    for name in WHOLE:
        scratch[f"{name}3"] = vmem(count_x + 2, LOW + rows3 + HIGH, 128)
    for name in ("gk", "gb"):
        scratch[name + "_first"] = vmem(4, 8, 128)
        scratch[name + "_send"] = pltpu.SemaphoreType.DMA((3 + count_y // 4 - 1 + count_x - 1,))
        scratch[name + "_recv"] = pltpu.SemaphoreType.DMA((3 + count_y // 4 - 1 + count_x - 1,))

    names = ["right_side", "coefficient", "solution", "residual"] + list(scratch)
    shape = jax.ShapeDtypeStruct((nx * ny, nz), F32)
    found = pl.pallas_call(
        functools.partial(kernel, count_x, count_y, names),
        out_shape=(shape, shape),
        in_specs=[pl.BlockSpec(memory_space=pl.ANY)] * 2,
        out_specs=(pl.BlockSpec(memory_space=pl.ANY),) * 2,
        scratch_shapes=list(scratch.values()),
        compiler_params=pltpu.CompilerParams(
            collective_id=0, has_side_effects=True, vmem_limit_bytes=56 << 20
        ),
        name="vcycle",
    )(right_side.reshape(nx * ny, nz), coefficient.reshape(nx * ny, nz))
    return tuple(value.reshape(nx, ny, nz) for value in found)


def solution(mesh):
    spec = P("gx", "gy", None)
    step = functools.partial(per_device, mesh.shape["gx"], mesh.shape["gy"])
    return jax.shard_map(step, mesh=mesh, in_specs=(spec, spec), out_specs=(spec, spec), check_vma=False)
```

```python
import functools

import jax
import jax.numpy as jnp
from jax import lax
from jax.experimental import pallas as pl
from jax.experimental.pallas import tpu as pltpu
from jax.sharding import PartitionSpec as P

MESH = pl.DeviceIdType.MESH
F32 = jnp.float32

SMOOTH_LO, SMOOTH_HI = 0.5, 2.0
COARSE_LO, COARSE_HI = 0.05, 2.0
BOTTOM = 8

STEPS = ((1, 1), (1, -1), (-1, 1), (-1, -1), (0, 1), (0, -1), (1, 0), (-1, 0))
ALONG_GX, ALONG_GY = (6, 7), (0, 1, 2, 3, 4, 5)


def coefficients(low, high, sweeps):
    theta = (high + low) / 2.0
    delta = (high - low) / 2.0
    sigma = theta / delta
    rho = 1.0 / sigma
    pairs = []
    for _ in range(sweeps - 1):
        rho_next = 1.0 / (2.0 * sigma - rho)
        pairs.append((rho_next * rho, 2.0 * rho_next / delta))
        rho = rho_next
    return theta, pairs


THETA, ((MOMENTUM, STEP),) = coefficients(SMOOTH_LO, SMOOTH_HI, 2)


def harmonic(own, other):
    return 2.0 * own * other / (own + other)


def roll(value, shift, axis):
    size = value.shape[axis]
    return pltpu.roll(value, shift % size, axis)


def iota(shape, dim):
    return lax.broadcasted_iota(jnp.int32, shape, dim)


def times(rows, matrix):
    high = rows.astype(jnp.bfloat16)
    rest = rows - high.astype(F32)
    middle = rest.astype(jnp.bfloat16)
    low = (rest - middle.astype(F32)).astype(jnp.bfloat16)
    found = [jnp.dot(term, matrix, preferred_element_type=F32) for term in (low, middle, high)]
    return (found[0] + found[1]) + found[2]


def loop(start, stop, body, unroll=1):
    count = (stop - start) // unroll

    def step(index, carry):
        for k in range(unroll):
            body(start + index * unroll + k)
        return carry

    if count > 1:
        lax.fori_loop(0, count, step, 0)
        start += count * unroll
    for index in range(start, stop):
        body(index)


class Exchange:
    def __init__(self, field, landing, send, recv, halo, depth, corner, skip=0):
        self.skip = skip
        self.field, self.wide = field, landing is None
        self.left, self.right = (None, None) if self.wide else landing
        self.send, self.recv = send, recv
        self.halo, self.depth, self.corner = halo, depth, corner
        self.planes = field.shape[0] - 2 * halo
        self.rows = field.shape[1] - (16 if self.wide else 8)

    def copies(self, place):
        h, n, r, x = self.halo, self.planes, self.depth, self.rows
        found, self.tiles = [], 0
        for number, (dx, dy) in enumerate(STEPS):
            if dx == 0:
                count, skip = r - self.skip, self.skip
                source_plane = h + n - r if dy > 0 else h + skip
                target_plane = h - r if dy > 0 else h + n + skip
                source = self.field.at[pl.ds(source_plane, count), pl.ds(0, x)]
                target = self.field.at[pl.ds(target_plane, count), pl.ds(0, x)]
            else:
                count = n if dy == 0 else self.corner
                source_plane = h if dy <= 0 else h + n - count
                target_plane = h if dy == 0 else (h - count if dy > 0 else h + n)
                source = self.field.at[pl.ds(source_plane, count), pl.ds(x - 8 if dx > 0 else 0, 8)]
                if self.wide:
                    target = self.field.at[pl.ds(target_plane, count), pl.ds(x + 8 if dx > 0 else x, 8)]
                else:
                    landing = self.left if dx > 0 else self.right
                    target = landing.at[pl.ds(target_plane, count)]
            self.tiles += source.shape[0] * source.shape[1] * source.shape[2] // 1024
            found.append(
                pltpu.make_async_remote_copy(
                    src_ref=source,
                    dst_ref=target,
                    send_sem=self.send.at[0],
                    recv_sem=self.recv.at[number],
                    device_id=place(dx, dy),
                    device_id_type=MESH,
                )
            )
        return found

    def start(self, place):
        self.started = self.copies(place)
        for copy in self.started:
            copy.start()

    def arrive(self, which):
        for number in which:
            self.started[number].wait_recv()

    def merge(self, start, stop):
        if self.wide:
            return
        x = self.rows
        shape = (8, self.field.shape[2])

        def body(p):
            upper = iota(shape, 0) < 4
            self.field[p, x:, :] = jnp.where(upper, self.right[p], self.left[p])

        loop(start, stop, body, 4)

    def merge_mended(self, start, stop, at_low, at_high):
        x = self.rows
        shape = (8, self.field.shape[2])
        row = iota(shape, 0)
        take_high = jnp.where(row == 0, at_high, 0) == 1
        take_low = jnp.where(row == 7, at_low, 0) == 1
        upper = row < 4

        def ends(p):
            high, low = self.field[p, x : x + 8, :], self.field[p, x + 8 :, :]
            self.field[p, x : x + 8, :] = jnp.where(take_high, roll(self.field[p, x - 8 : x, :], 1, 0), high)
            self.field[p, x + 8 :, :] = jnp.where(take_low, roll(self.field[p, 0:8, :], 7, 0), low)

        if self.wide:
            loop(start, stop, ends, 4)
            return

        def body(p):
            tile = jnp.where(upper, self.right[p], self.left[p])
            tile = jnp.where(take_high, roll(self.field[p, x - 8 : x, :], 1, 0), tile)
            self.field[p, x:, :] = jnp.where(take_low, roll(self.field[p, 0:8, :], 7, 0), tile)

        loop(start, stop, body, 4)

    def sent(self, idle):
        whole = idle.at[pl.ds(0, self.tiles)]
        pltpu.make_async_copy(whole, whole, self.send.at[0]).wait()


class Level:
    def __init__(self, number, lanes, refs, gx, gy, counts):
        self.scale = 0.25**number
        self.lanes = lanes
        self.gx, self.gy = gx, gy
        self.count_x, self.count_y = counts
        (self.k, self.b, self.xh, self.x1, self.x2, self.wx, self.wy, self.wz, self.w, self.inv, self.z0, self.z1) = refs
        self.h = self.k.halo
        self.n = self.k.planes
        self.x = self.k.rows
        self.shape = self.k.field.shape[1:]
        self.period = lanes
        self.unroll = 2 if number == 0 else 4

    def merge_k(self, start, stop):
        at_low = jnp.where(self.gx == 0, 1, 0)
        at_high = jnp.where(self.gx == self.count_x - 1, 1, 0)
        self.k.merge_mended(start, stop, at_low, at_high)

    def row_ok(self):
        row = iota(self.shape, 0)
        below = jnp.where(self.gx == 0, 1, 0)
        above = jnp.where(self.gx == self.count_x - 1, 1, 0)
        middle = (self.x + self.shape[0]) // 2
        bad_low = jnp.where(row >= middle, below, 0)
        bad_high = jnp.where((row >= self.x) & (row < middle), above, 0)
        return (bad_low + bad_high) == 0

    def plane_ok(self, p):
        y = self.gy * self.n + p - self.h
        return (y >= 0) & (y < self.count_y * self.n)

    def mend_planes(self):
        field, h, n = self.k.field, self.h, self.n

        @pl.when(self.gy == 0)
        def _():
            field[h - 1] = field[h]

        @pl.when(self.gy == self.count_y - 1)
        def _():
            field[h + n] = field[h + n - 1]

    def lane(self):
        return iota(self.shape, 1) % self.period

    def faces(self, start, stop):
        k = self.k.field

        def body(p):
            own = k[p]
            self.wx[p] = harmonic(own, roll(own, -1, 0))
            along = harmonic(own, roll(own, -1, 1))
            self.wz[p] = jnp.where(self.lane() == self.period - 1, 0.0, along)

        loop(start, stop, body, self.unroll)

    def faces_inside(self):
        k, h, n, x = self.k.field, self.h, self.n, self.x
        last = self.lane()[0:x] == self.period - 1

        def body(p):
            own = k[p, 0:x, :]
            self.wx[p, 0:x, :] = harmonic(own, roll(own, -1, 0))
            self.wz[p, 0:x, :] = jnp.where(last, 0.0, harmonic(own, roll(own, -1, 1)))

        def along(p):
            self.wy[p, 0:x, :] = harmonic(k[p, 0:x, :], k[p + 1, 0:x, :])

        loop(h, h + n, body, self.unroll)
        loop(h, h + n - 1, along, self.unroll)

    def faces_edge(self):
        k, h, n, x = self.k.field, self.h, self.n, self.x
        last = self.lane()[0:8] == self.period - 1
        inner = iota((8, self.shape[1]), 0) < 7
        after = lambda own, following: jnp.where(inner, roll(own, -1, 0), roll(following, -1, 0))

        def body(p):
            first, end, halo = k[p, 0:8, :], k[p, x - 8 : x, :], k[p, x:, :]
            self.wx[p, x - 8 : x, :] = harmonic(end, after(end, halo))
            self.wx[p, x:, :] = harmonic(halo, after(halo, first))
            self.wz[p, x:, :] = jnp.where(last, 0.0, harmonic(halo, roll(halo, -1, 1)))

        def along(p):
            self.wy[p, x:, :] = harmonic(k[p, x:, :], k[p + 1, x:, :])

        loop(h, h + n, body, 4)
        loop(h, h + n - 1, along, 4)

    def faces_y(self, start, stop):
        k = self.k.field

        def body(p):
            self.wy[p] = harmonic(k[p], k[p + 1])

        loop(start, stop, body, self.unroll)

    def totals(self, start, stop):
        k = self.k.field
        rows_ok = self.row_ok()

        def body(p):
            wx, wz = self.wx[p], self.wz[p]
            lane = self.lane()
            edge = jnp.where((lane == 0) | (lane == self.period - 1), k[p], 0.0)
            total = wx + roll(wx, 1, 0) + self.wy[p] + self.wy[p - 1] + wz + roll(wz, 1, 1) + edge
            self.w[p] = total
            ok = rows_ok & self.plane_ok(p)
            self.inv[p] = jnp.where(ok, 1.0 / total, 0.0)

        loop(start, stop, body, self.unroll)

    def beside(self, field, p):
        own, wx, wz = field[p], self.wx[p], self.wz[p]
        found = wx * roll(own, -1, 0) + roll(wx * own, 1, 0)
        found = found + self.wy[p] * field[p + 1] + self.wy[p - 1] * field[p - 1]
        return found + wz * roll(own, -1, 1) + roll(wz * own, 1, 1)

    def first(self, start, stop):
        def body(p):
            self.x1[p] = self.b[p] * self.inv[p] * (1.0 / (THETA * self.scale))

        loop(start, stop, body, self.unroll)

    def second(self, margin):
        h, n, x = self.h, self.n, self.x

        def value(p):
            own = self.x1[p]
            factor = 1.0 + MOMENTUM + STEP * (THETA - 1.0)
            return factor * own + STEP * (self.inv[p] * self.beside(self.x1, p))

        def plain(p):
            self.x2[p] = value(p)

        def kept(p):
            found = value(p)
            self.x2[p] = found
            if self.lanes < 128:
                first = iota(found.shape, 1) < self.lanes
                found = jnp.where(first, found, self.x1[p])
            self.xh.field[p, 0:x, :] = found[0:x, :]

        if self.xh is None:
            loop(h - margin, h + n + margin, plain, self.unroll)
            return
        loop(h, h + n, kept, self.unroll)
        for p in list(range(h - margin, h)) + list(range(h + n, h + n + margin)):
            plain(p) if self.xh.skip == 0 else kept(p)

    def residual(self, field, p):
        return self.b[p] - self.scale * (self.w[p] * field[p] - self.beside(field, p))

    def correct(self, p, grown):
        ok = self.rows_ok & self.plane_ok(p)
        base = self.x2[p] if self.xh is None or self.lanes < 128 else self.xh.field[p]
        self.z0[p] = jnp.where(ok, base + grown, 0.0)

    def third(self, start, stop):
        def body(p):
            own = self.z0[p]
            flow = self.inv[p] * self.beside(self.z0, p)
            self.z1[p] = (1.0 - 1.0 / THETA) * own + self.x1[p] + (1.0 / THETA) * flow

        loop(start, stop, body, self.unroll)

    def fourth(self, start, stop, target):
        def body(p):
            own = self.z1[p]
            flow = self.inv[p] * self.beside(self.z1, p)
            found = (1.0 + MOMENTUM - STEP) * own - MOMENTUM * self.z0[p]
            target[p] = found + (STEP * THETA) * self.x1[p] + STEP * flow

        loop(start, stop, body, self.unroll)


LOW, HIGH = 8, 16


class Whole:
    def __init__(self, refs):
        self.scale = 0.25**3
        self.size_z = 32
        self.k, self.b, self.x1, self.x2, self.wx, self.wy, self.wz, self.w, self.inv = refs
        self.count = self.k.shape[0] - 2
        self.rows = self.k.shape[1] - LOW - HIGH
        self.shape = (self.rows, 128)

    def blank(self):
        for ref in (self.k, self.x1, self.x2, self.wx, self.wy, self.wz, self.inv):
            empty = jnp.zeros(ref.shape[1:], F32)
            ref[0] = empty
            ref[self.count + 1] = empty

            def body(g, ref=ref):
                ref[g, 0:LOW, :] = jnp.zeros((LOW, 128), F32)
                ref[g, LOW + self.rows :, :] = jnp.zeros((HIGH, 128), F32)

            loop(1, self.count + 1, body, 4)

    def at(self, ref, g):
        return ref[g, LOW : LOW + self.rows, :]

    def after(self, own, following):
        inner = iota(own.shape, 1) < 128 - self.size_z
        return jnp.where(inner, roll(own, -self.size_z, 1), roll(following, -self.size_z, 1))

    def before(self, own, previous):
        inner = iota(own.shape, 1) >= self.size_z
        return jnp.where(inner, roll(own, self.size_z, 1), roll(previous, self.size_z, 1))

    def weights(self):
        rows, inside = self.rows, slice(LOW, LOW + self.rows)

        def faces(g):
            own, following = self.at(self.k, g), self.at(self.k, g + 1)
            lane, row = iota(self.shape, 1), iota(self.shape, 0)
            end = jnp.where(lane >= 128 - self.size_z, jnp.where(g == self.count, 1, 0), 0)
            self.wx[g, inside, :] = jnp.where(end == 1, 0.0, harmonic(own, self.after(own, following)))
            self.wy[g, inside, :] = jnp.where(row == rows - 1, 0.0, harmonic(own, roll(own, -1, 0)))
            last = lane % self.size_z == self.size_z - 1
            self.wz[g, inside, :] = jnp.where(last, 0.0, harmonic(own, roll(own, -1, 1)))

        loop(1, self.count + 1, faces)

        def totals(g):
            lane, row = iota(self.shape, 1), iota(self.shape, 0)
            high = jnp.where(lane >= 128 - self.size_z, jnp.where(g == self.count, 1.0, 0.0), 0.0)
            low = jnp.where(lane < self.size_z, jnp.where(g == 1, 1.0, 0.0), 0.0)
            edge = high + low
            edge = edge + jnp.where((row == 0) | (row == rows - 1), 1.0, 0.0)
            z = lane % self.size_z
            edge = edge + jnp.where((z == 0) | (z == self.size_z - 1), 1.0, 0.0)
            wx, wy, wz = self.at(self.wx, g), self.at(self.wy, g), self.at(self.wz, g)
            total = wx + self.before(wx, self.at(self.wx, g - 1)) + wy + roll(wy, 1, 0) + wz + roll(wz, 1, 1)
            total = total + edge * self.at(self.k, g)
            self.w[g, inside, :] = total
            self.inv[g, inside, :] = 1.0 / total

        loop(1, self.count + 1, totals)

    def flow(self, fields, weights):
        previous, own, following = fields
        wx_previous, wx, wy, wz = weights
        found = wx * self.after(own, following) + self.before(wx * own, wx_previous * previous)
        found = found + wy * roll(own, -1, 0) + roll(wy * own, 1, 0)
        return found + wz * roll(own, -1, 1) + roll(wz * own, 1, 1)

    def beside(self, field, g):
        fields = [self.at(field, g + step) for step in (-1, 0, 1)]
        weights = [self.at(self.wx, g - 1)] + [self.at(ref, g) for ref in (self.wx, self.wy, self.wz)]
        return self.flow(fields, weights)

    def down(self, left):
        inside = slice(LOW, LOW + self.rows)

        def first(g):
            found = self.at(self.b, g) * self.at(self.inv, g) * (1.0 / (THETA * self.scale))
            self.x1[g, inside, :] = found

        loop(1, self.count + 1, first, 2)

        def second(g):
            factor = 1.0 + MOMENTUM + STEP * (THETA - 1.0)
            moved = self.at(self.inv, g) * self.beside(self.x1, g)
            self.x2[g, inside, :] = factor * self.at(self.x1, g) + STEP * moved

        loop(1, self.count + 1, second, 2)

        def residual(g):
            applied = self.at(self.w, g) * self.at(self.x2, g) - self.beside(self.x2, g)
            left[g - 1] = self.at(self.b, g) - self.scale * applied

        loop(1, self.count + 1, residual, 2)

    def up(self, gx, start, grown, held, answer):
        span = pl.ds(start, 24)
        z0, z1 = held
        planes = (0, 1, 2)
        part = lambda ref, c: ref[gx + c, span, :]
        for c in planes:
            z0[c + 1] = part(self.x2, c) + grown[c, span, :]

        def flow(field, c):
            fields = [field[c + step] for step in (0, 1, 2)]
            before = self.wx[jnp.maximum(gx + c - 1, 0), span, :]
            return part(self.inv, c) * self.flow(fields, [before, part(self.wx, c), part(self.wy, c), part(self.wz, c)])

        for c in planes:
            z1[c + 1] = (1.0 - 1.0 / THETA) * z0[c + 1] + part(self.x1, c) + (1.0 / THETA) * flow(z0, c)
        for c in planes:
            found = (1.0 + MOMENTUM - STEP) * z1[c + 1] - MOMENTUM * z0[c + 1]
            answer[c] = found + (STEP * THETA) * part(self.x1, c) + STEP * flow(z1, c)


class Deepest:
    def __init__(self, count):
        self.count = count
        self.scale = 0.25**4
        shape = (8, 128)
        self.lane, self.row = iota(shape, 1), iota(shape, 0)
        self.low_x = (self.lane % 32) < 16
        self.zero = jnp.zeros(shape, F32)

    def next_x(self, tiles):
        back, ahead = [roll(t, -16, 1) for t in tiles], [roll(t, 16, 1) for t in tiles] + [self.zero]
        return [jnp.where(self.low_x, back[g], ahead[g + 1]) for g in range(self.count)]

    def last_x(self, tiles):
        back, ahead = [self.zero] + [roll(t, -16, 1) for t in tiles], [roll(t, 16, 1) for t in tiles]
        return [jnp.where(self.low_x, back[g], ahead[g]) for g in range(self.count)]

    def next_y(self, tiles):
        moved = [roll(t, -1, 0) for t in tiles]
        return [jnp.where(self.row < 7, t, roll(t, -32, 1)) for t in moved]

    def last_y(self, tiles):
        moved = [roll(t, 1, 0) for t in tiles]
        return [jnp.where(self.row > 0, t, roll(t, 32, 1)) for t in moved]

    def next_z(self, tiles):
        return [roll(t, -1, 1) for t in tiles]

    def last_z(self, tiles):
        return [roll(t, 1, 1) for t in tiles]

    def weights(self, k, weight_refs, inv_ref):
        lane, row, span = self.lane, self.row, range(self.count)
        z = lane % 16
        end_y = (row == 7) & (lane >= 96)
        edge = jnp.where((z == 0) | (z == 15), 1.0, 0.0)
        edge = edge + jnp.where(end_y | ((row == 0) & (lane < 32)), 1.0, 0.0)
        faces_x = [harmonic(a, b) for a, b in zip(k, self.next_x(k))]
        faces_x[-1] = jnp.where(self.low_x, faces_x[-1], 0.0)
        faces_y = [jnp.where(end_y, 0.0, harmonic(a, b)) for a, b in zip(k, self.next_y(k))]
        faces_z = [jnp.where(z == 15, 0.0, harmonic(a, b)) for a, b in zip(k, self.next_z(k))]
        sets = [faces_x, self.last_x(faces_x), faces_y, self.last_y(faces_y), faces_z, self.last_z(faces_z)]
        for g in span:
            total = edge * k[g]
            if g == 0:
                total = total + jnp.where(self.low_x, k[g], 0.0)
            if g == self.count - 1:
                total = total + jnp.where(self.low_x, 0.0, k[g])
            for one in sets:
                total = total + one[g]
            inv = 1.0 / total
            inv_ref[g] = inv
            for number, one in enumerate(sets):
                weight_refs[number, g] = one[g] * inv

    def solve(self, b, weight_refs, inv_ref):
        theta, pairs = coefficients(COARSE_LO, COARSE_HI, BOTTOM)
        span = range(self.count)
        scaled = [b[g] * inv_ref[g] * (1.0 / self.scale) for g in span]
        update = [t * (1.0 / theta) for t in scaled]
        found = update
        for momentum, step in pairs:
            shifted = [
                self.next_x(found),
                self.last_x(found),
                self.next_y(found),
                self.last_y(found),
                self.next_z(found),
                self.last_z(found),
            ]
            following = []
            for g in span:
                flow = weight_refs[0, g] * shifted[0][g]
                for number in range(1, 6):
                    flow = flow + weight_refs[number, g] * shifted[number][g]
                following.append(momentum * update[g] + step * ((scaled[g] - found[g]) + flow))
            update = following
            found = [a + d for a, d in zip(found, update)]
        return found


def shrink_lanes(lanes, kept):
    row, col = iota((max(lanes, 128), 128), 0), iota((max(lanes, 128), 128), 1)
    return jnp.where((row // 2 == col % kept) & (row < lanes), 0.125, 0.0).astype(jnp.bfloat16)


def grow_lanes(kept, lanes):
    row, col = iota((128, lanes), 0), iota((128, lanes), 1)
    period = 2 * kept
    return jnp.where((col % period) // 2 == row, 1.0, 0.0).astype(jnp.bfloat16)


def restrict(read, target, count, fine_plane, coarse_plane, rows, matrix, half, sums):
    kept = rows // 2
    parts = matrix.shape[0] // 128

    def body(j):
        pair = read(fine_plane + 2 * j) + read(fine_plane + 2 * j + 1)
        slot = j % 2
        for part in range(parts):
            half[slot, part, 0:rows, :] = pair[:, part * 128 : (part + 1) * 128]
        for part in range(parts):
            even = half[slot, part, pl.ds(0, kept, stride=2), :]
            odd = half[slot, part, pl.ds(1, kept, stride=2), :]
            sums[pl.ds(pl.multiple_of(j * kept, 8), kept), 128 * part : 128 * (part + 1)] = even + odd

    loop(0, count, body, 2)
    means = times(sums[0 : count * kept, 0 : 128 * parts], matrix)
    target[coarse_plane : coarse_plane + count, 0:kept, :] = means.reshape(count, kept, 128)


def grow(source, planes, rows, matrix, doubled):
    start, stop = planes
    count, parts = stop - start, matrix.shape[1] // 128
    wide = times(source[start:stop].reshape(count * rows, 128), matrix)
    for j in range(count):
        for part in range(parts):
            piece = wide[j * rows : (j + 1) * rows, 128 * part : 128 * (part + 1)]
            doubled[j, part, pl.ds(0, rows, stride=2), :] = piece
            doubled[j, part, pl.ds(1, rows, stride=2), :] = piece


def grown_plane(doubled, j, rows, parts):
    own = 2 * (rows - 16)
    upper = iota((8, 128), 0) < 4
    found = []
    for part in range(parts):
        tail = jnp.where(upper, doubled[j, part, own : own + 8, :], doubled[j, part, own + 24 : own + 32, :])
        found.append(jnp.concatenate([doubled[j, part, 0:own, :], tail], axis=0))
    return found[0] if parts == 1 else jnp.concatenate(found, axis=1)


def kernel(count_x, count_y, names, *refs):
    r = dict(zip(names, refs))
    gx, gy = lax.axis_index("gx"), lax.axis_index("gy")
    ring_x = 4
    ring_z = count_y // ring_x
    chip_x, chip_z = gy % ring_x, gy // ring_x

    def place(dx, dy):
        return ((gx + dx + count_x) % count_x, (gy + dy + count_y) % count_y)

    def along_x(d):
        return (gx, chip_z * ring_x + (chip_x + d) % ring_x)

    def along_z(d):
        return (gx, ((chip_z + d) % ring_z) * ring_x + chip_x)

    def along_gx(d):
        return ((gx + d) % count_x, gy)

    z_steps = [d for d in range(1, ring_z) if min(d, ring_z - d) <= 3]
    partners = [place(dx, dy) for dx, dy in STEPS]
    partners += [along_x(d) for d in range(1, ring_x)]
    partners += [along_z(d) for d in z_steps]
    partners += [along_gx(d) for d in range(1, count_x)]

    def halves(whole, staged, first, store):
        copies = []
        for part in range(2):
            wide = whole.at[:, pl.ds(128 * part, 128)]
            pair = (staged.at[part], wide) if store else (wide, staged.at[part])
            copies.append(pltpu.make_async_copy(*pair, r["load"].at[first + part]))
        return copies

    loads_k = halves(r["coefficient"], r["k_in"], 0, False)
    loads_b = halves(r["right_side"], r["b_in"], 2, False)
    for copy in loads_k + loads_b:
        copy.start()
    barrier = pltpu.get_barrier_semaphore()
    for partner in partners:
        pl.semaphore_signal(barrier, inc=1, device_id=partner, device_id_type=MESH)

    def exchange(name, number, halo, depth):
        tag = f"{name}{number}"
        if not depth:
            return None
        landing = (r[tag + "_l"], r[tag + "_r"]) if tag + "_l" in r else None
        corner = depth if number == 2 else depth - 1
        return Exchange(r[tag], landing, r[tag + "_send"], r[tag + "_recv"], halo, depth, corner, 1 if tag == "xh0" else 0)

    levels, sources = [], []
    for number, (lanes, halo, depth_k, depth_b, depth_x) in enumerate(SHAPES):
        sources.append(exchange("b", number, halo, depth_b))
        fields = [exchange("k", number, halo, depth_k), r[f"b{number}"], exchange("xh", number, halo, depth_x)]
        fields += [r[f"{name}{number}"] for name in LOCAL]
        levels.append(Level(number, lanes, fields, gx, gy, (count_x, count_y)))
    l0, l1, l2 = levels
    l3 = Whole([r[f"{name}3"] for name in WHOLE])
    l4 = Deepest(count_x)

    def turn(staged, target):
        for y in range(l0.n):
            for part in range(2):
                lanes = pl.ds(128 * part, 128)
                target[l0.h + y, 0 : l0.x, lanes] = staged[part, pl.ds(y, l0.x, stride=l0.n), :]

    for copy in loads_k:
        copy.wait()
    turn(r["k_in"], r["k0"])
    for copy in loads_b:
        copy.wait()
    turn(r["b_in"], r["b0"])
    pl.semaphore_wait(barrier, len(partners))
    l0.k.start(place)
    sources[0].start(place)

    half, sums, doubled = r["half"], r["sums"], r["doubled"]
    k0, k1, k2 = r["k0"], r["k1"], r["k2"]
    to_1, to_2 = shrink_lanes(256, 128), shrink_lanes(128, 64)
    restrict(lambda p: k0[p, 0 : l0.x, :], k1, l1.n, l0.h, l1.h, l0.x, to_1, half, sums)
    l1.k.start(place)
    restrict(lambda p: k1[p, 0 : l1.x, :], k2, l2.n, l1.h, l2.h, l1.x, to_2, half, sums)

    def small_block(read):
        row, col = iota((128, 128), 0), iota((128, 128), 1)
        matrix = jnp.where((row < 64) & (row // 2 == col % 32), 0.125, 0.0).astype(jnp.bfloat16)
        tile = (8, 128)
        mine = iota(tile, 1) // 32 == iota(tile, 0) // 2
        pairs = [read(l2.h + 2 * j) + read(l2.h + 2 * j + 1) for j in range(2)]
        means = times(jnp.concatenate(pairs, axis=0), matrix)
        found = jnp.zeros(tile, F32)
        for j in range(2):
            spread = jnp.where(mine, means[8 * j : 8 * j + 8], 0.0)
            line = jnp.sum(spread, axis=0, keepdims=True)
            found = jnp.where(iota(tile, 0) == 2 * chip_x + j, jnp.broadcast_to(line, tile), found)
        return found

    class Gather:
        def __init__(self, name, target, eager):
            self.first, self.target, self.eager = r[name + "_first"], target, eager
            self.send, self.recv = r[name + "_send"], r[name + "_recv"]
            self.tiles_sent, self.tiles_last = 0, 0

        def go(self, sems, source, target, where, steps):
            copies = []
            for d in steps:
                copies.append(
                    pltpu.make_async_remote_copy(
                        src_ref=source,
                        dst_ref=target,
                        send_sem=self.send.at[0],
                        recv_sem=self.recv.at[sems(d)],
                        device_id=where(d),
                        device_id_type=MESH,
                    )
                )
            for copy in copies:
                copy.start()
            self.tiles_sent += len(copies) * (source.shape[0] // 8)
            return copies

        def along_x(self, tile):
            self.first[chip_x] = tile
            slot = self.first.at[chip_x]
            self.near = self.go(lambda d: d, slot, slot, along_x, range(1, ring_x))

        def part(self, d):
            rows = pl.ds(pl.multiple_of(8 * ((chip_z + ring_z - d) % ring_z) + LOW, 8), 8)
            return self.target.at[gx + 1, rows]

        def pass_on(self, part):
            self.go(lambda d: 0, part, part, along_gx, range(1, count_x))
            self.tiles_last += (count_x - 1) * (part.shape[0] // 8)

        def along_z(self):
            for copy in self.near:
                copy.wait_recv()
            found = self.first[0]
            for slot in range(1, ring_x):
                found = found + self.first[slot]
            tile = self.part(0)
            tile[...] = found
            self.far = self.go(lambda d: ring_x - 1 + d, tile, tile, along_z, z_steps)
            if self.eager:
                self.pass_on(tile)

        def along_gx(self):
            for d, copy in sorted(zip(z_steps, self.far), key=lambda pair: min(pair[0], ring_z - pair[0])):
                copy.wait_recv()
                if self.eager:
                    self.pass_on(self.part(d))
            if not self.eager:
                self.pass_on(self.target.at[gx + 1, pl.ds(LOW, 8 * ring_z)])

        def arrive(self):
            whole = r["idle"].at[pl.ds(0, self.tiles_last)]
            pltpu.make_async_copy(whole, whole, self.recv.at[0]).wait()

        def sent(self):
            whole = r["idle"].at[pl.ds(0, self.tiles_sent)]
            pltpu.make_async_copy(whole, whole, self.send.at[0]).wait()

    gather_k, gather_b = Gather("gk", l3.k, False), Gather("gb", l3.b, True)
    gather_k.along_x(small_block(lambda p: k2[p, 0 : l2.x, :]))
    l3.blank()
    for d in range(1, ring_z):
        if d not in z_steps:
            unused = pl.ds(pl.multiple_of(8 * ((chip_z + d) % ring_z) + LOW, 8), 8)
            l3.k[gx + 1, unused, :] = jnp.ones((8, 128), F32)
            for g in range(1, count_x + 1):
                l3.b[g, unused, :] = jnp.zeros((8, 128), F32)
    z0_3, z1_3 = r["z0_3"], r["z1_3"]
    for held in (z0_3, z1_3):
        held[0] = jnp.zeros((24, 128), F32)
        held[4] = jnp.zeros((24, 128), F32)
    grown3 = r["grown3"]
    for c in range(3):
        grown3[c, 0:LOW, :] = jnp.zeros((LOW, 128), F32)
        grown3[c, LOW + 8 * ring_z :, :] = jnp.zeros((HIGH, 128), F32)

    def ready(level, between=None):
        h, n, depth = level.h, level.n, level.k.depth
        if level.k.wide:
            level.k.arrive(ALONG_GX)
            level.merge_k(h, h + n)
            level.faces(h, h + n)
            level.faces_y(h, h + n - 1)
        else:
            level.faces_inside()
            level.k.arrive(ALONG_GX)
            level.merge_k(h, h + n)
            level.faces_edge()
        level.totals(h + 1, h + n - 1)
        if between is not None:
            between()
        level.k.arrive(ALONG_GY)
        low, high = h - depth + 1, h + n + depth - 1
        level.merge_k(h - level.k.corner, h)
        level.merge_k(h + n, h + n + level.k.corner)
        level.mend_planes()
        level.faces(low, h)
        level.faces(h + n, high)
        level.faces_y(h - depth, h)
        level.faces_y(h + n - 1, high)
        level.totals(low, h + 1)
        level.totals(h + n - 1, high)

    def descend(level, source, depth):
        h, n = level.h, level.n
        if source is not None:
            source.arrive(range(8))
            source.merge(h - depth + 1, h + n + depth - 1)
        level.first(h - depth, h + n + depth)
        level.second(depth - 1)

    def source_below(level, target, margin, rows, matrix):
        below = levels[levels.index(level) + 1]
        read = lambda p: level.residual(level.x2, p)[0:rows, :]
        count, fine = below.n + 2 * margin, level.h - 2 * margin
        restrict(read, target, count, fine, below.h - margin, rows, matrix, half, sums)

    ready(l0, gather_k.along_z)
    descend(l0, sources[0], 2)
    source_below(l0, r["b1"], 0, l0.x, shrink_lanes(256, 128))
    sources[1].start(place)
    gather_k.along_gx()
    l2.k.start(place)
    ready(l1)
    descend(l1, sources[1], 6)
    source_below(l1, r["b2"], 2, l1.x + 16, shrink_lanes(128, 64))
    ready(l2)
    descend(l2, None, 2)
    gather_b.along_x(small_block(lambda p: l2.residual(l2.x2, p)[0 : l2.x, :]))
    def to_bottom(source, low):
        row, col = iota((128, 128), 0), iota((128, 128), 1)
        same_x = (row // 32) // 2 == (col % 32) // 16
        same_z = (row % 32) // 2 == col % 16
        matrix = jnp.where(same_x & same_z, 0.125, 0.0).astype(jnp.bfloat16)
        kept = 4 * ring_z
        pieces = []
        for g in range(count_x):
            even = source[g, pl.ds(low, kept, stride=2), :]
            odd = source[g, pl.ds(low + 1, kept, stride=2), :]
            pieces.append(even + odd)
        means = times(jnp.concatenate(pieces, axis=0), matrix)
        group = iota((8, 128), 1) // 32
        tiles = []
        for g in range(count_x):
            found = means[g * kept : g * kept + 8]
            for q in range(1, 4):
                found = jnp.where(group == q, means[g * kept + 8 * q : g * kept + 8 * q + 8], found)
            tiles.append(found)
        return tiles

    gather_k.arrive()
    l3.weights()
    gather_b.along_z()
    l4.weights(to_bottom(l3.k.at[pl.ds(1, count_x)], LOW), r["w4"], r["inv4"])
    gather_b.along_gx()
    l2.xh.start(place)
    l0.xh.start(place)
    for field in [level.k for level in levels] + sources[:2]:
        field.sent(r["idle"])
    gather_k.sent()
    gather_b.arrive()
    l3.down(r["left3"])
    deepest = l4.solve(to_bottom(r["left3"], 0), r["w4"], r["inv4"])
    tiles4 = r["tiles4"]
    tiles4[0] = l4.zero
    tiles4[count_x + 1] = l4.zero
    for g in range(count_x):
        tiles4[g + 1] = deepest[g]

    row, col = iota((128, 128), 0), iota((128, 128), 1)
    same = ((row % 32) // 16 == (col // 32) // 2) & (row % 16 == (col % 32) // 2)
    matrix_43 = jnp.where(same, 1.0, 0.0).astype(jnp.bfloat16)
    group = iota((8, 128), 1) // 32
    spread = [jnp.where(group == q, tiles4[gx + c], 0.0) for c in range(3) for q in range(4)]
    wide = times(jnp.concatenate(spread, axis=0), matrix_43)
    for c in range(3):
        piece = wide[32 * c : 32 * c + 32]
        grown3[c, pl.ds(LOW, 32, stride=2), :] = piece
        grown3[c, pl.ds(LOW + 1, 32, stride=2), :] = piece
    start = 8 * ((2 * gy + 4) // 8)
    answer = r["answer"]
    l3.up(gx, pl.multiple_of(start, 8), grown3, (z0_3, z1_3), answer)

    matrix_32 = jnp.where(iota((128, 128), 0) % 32 == (iota((128, 128), 1) % 64) // 2, 1.0, 0.0).astype(jnp.bfloat16)
    l2.xh.arrive(range(8))
    l2.xh.merge(0, 2 * l2.h + l2.n)
    tile = (8, 128)
    own_group = iota(tile, 1) // 32 == iota(tile, 0) // 2
    first_half = iota(tile, 0) < 4
    spread = []
    for j in range(6):
        at = 6 + 2 * gy + j - start
        lower, own, upper = [jnp.broadcast_to(answer[c, pl.ds(at, 1), :], tile) for c in range(3)]
        spread.append(jnp.where(own_group, own, 0.0))
        spread.append(jnp.where(own_group, jnp.where(first_half, upper, lower), 0.0))
    wide = times(jnp.concatenate(spread, axis=0), matrix_32)
    l2.rows_ok = l2.row_ok()
    low_lanes = iota(l2.shape, 1) < 64
    for p in range(12):
        both = l2.xh.field[p]
        turned = roll(both, 64, 1)
        l2.x1[p] = jnp.where(l2.rows_ok & l2.plane_ok(p), jnp.where(low_lanes, turned, both), 0.0)
        l2.x2[p] = jnp.where(low_lanes, both, turned)
        l2.correct(p, wide[16 * (p // 2) : 16 * (p // 2) + 16])
    l2.third(1, 11)
    l2.fourth(2, 10, r["z2"])

    grow(r["z2"], (2, 10), 16, grow_lanes(64, 128), doubled)
    l1.rows_ok = l1.row_ok()

    def lift_1(j):
        grown = doubled[j, 0, 0 : l1.x + 16, :]
        l1.correct(l1.h - 4 + 2 * j, grown)
        l1.correct(l1.h - 3 + 2 * j, grown)

    loop(0, 8, lift_1, 2)
    l1.third(l1.h - 3, l1.h + l1.n + 3)
    l1.fourth(l1.h - 2, l1.h + l1.n + 2, r["z1out"])

    grow(r["z1out"], (l1.h - 2, l1.h + l1.n + 2), 32, grow_lanes(128, 256), doubled)
    l0.xh.arrive(range(8))
    l0.xh.merge(l0.h - 2, l0.h + l0.n + 2)
    l0.rows_ok = l0.row_ok()
    l0.correct(0, grown_plane(doubled, 0, 32, 2))

    def lift_0(j):
        grown = grown_plane(doubled, j, 32, 2)
        l0.correct(2 * j - 1, grown)
        l0.correct(2 * j, grown)

    loop(1, 11, lift_0)
    l0.correct(21, grown_plane(doubled, 11, 32, 2))
    l0.third(1, 21)
    l0.fourth(2, 20, l0.x2)

    def turn_back(staged, y, value):
        for part in range(2):
            lanes = slice(128 * part, 128 * (part + 1))
            staged[part, pl.ds(y, l0.x, stride=l0.n), :] = value[0 : l0.x, lanes]

    loop(0, l0.n, lambda y: turn_back(r["k_in"], y, l0.x2[l0.h + y]), 4)
    stores = halves(r["solution"], r["k_in"], 4, True)
    for copy in stores:
        copy.start()
    loop(0, l0.n, lambda y: turn_back(r["b_in"], y, l0.residual(l0.x2, l0.h + y)), 2)
    for copy in halves(r["residual"], r["b_in"], 6, True):
        copy.start()
        stores.append(copy)
    gather_b.sent()
    l2.xh.sent(r["idle"])
    l0.xh.sent(r["idle"])
    for copy in stores:
        copy.wait()


SHAPES = ((256, 3, 3, 2, 3), (128, 7, 7, 6, 0), (64, 4, 4, 0, 4))
LOCAL = ("x1_", "x2_", "wx", "wy", "wz", "w", "inv", "z0_", "z1_")
WHOLE = ("k", "b", "x1_", "x2_", "wx", "wy", "wz", "w", "inv")


def per_device(count_x, count_y, right_side, coefficient):
    nx, ny, nz = right_side.shape
    vmem = lambda *shape: pltpu.VMEM(shape, F32)
    rows3 = 2 * count_y
    scratch = {
        "k_in": vmem(2, nx * ny, 128),
        "b_in": vmem(2, nx * ny, 128),
        "load": pltpu.SemaphoreType.DMA((8,)),
        "half": vmem(2, 2, nx, 128),
        "idle": vmem(256, 8, 128),
        "sums": vmem(nx * ny // 4, nz),
        "doubled": vmem(ny // 2 + 4, 2, nx + 32, 128),
        "z0_3": vmem(5, 24, 128),
        "z1_3": vmem(5, 24, 128),
        "left3": vmem(count_x, rows3, 128),
        "w4": vmem(6, count_x, 8, 128),
        "inv4": vmem(count_x, 8, 128),
        "tiles4": vmem(count_x + 2, 8, 128),
        "grown3": vmem(3, LOW + rows3 + HIGH, 128),
        "answer": vmem(3, 24, 128),
        "z2": vmem((ny >> 2) + 8, (nx >> 2) + 8, 128),
        "z1out": vmem((ny >> 1) + 14, (nx >> 1) + 16, 128),
    }
    for number, (lanes, halo, *depths) in enumerate(SHAPES):
        rows, planes, width = nx >> number, ny >> number, max(128, lanes)
        wide = number == 1
        full = (planes + 2 * halo, rows + (16 if wide else 8), width)
        scratch[f"b{number}"] = vmem(*full)
        for name, depth in zip(("k", "b", "xh"), depths):
            if not depth:
                continue
            tag = f"{name}{number}"
            scratch[tag] = vmem(*full)
            if not wide:
                scratch[tag + "_l"] = vmem(full[0], 8, width)
                scratch[tag + "_r"] = vmem(full[0], 8, width)
            scratch[tag + "_send"] = pltpu.SemaphoreType.DMA((1,))
            scratch[tag + "_recv"] = pltpu.SemaphoreType.DMA((8,))
        for name in LOCAL:
            scratch[f"{name}{number}"] = vmem(*full)
    for name in WHOLE:
        scratch[f"{name}3"] = vmem(count_x + 2, LOW + rows3 + HIGH, 128)
    for name in ("gk", "gb"):
        scratch[name + "_first"] = vmem(4, 8, 128)
        scratch[name + "_send"] = pltpu.SemaphoreType.DMA((1,))
        scratch[name + "_recv"] = pltpu.SemaphoreType.DMA((4 + count_y // 4,))

    names = ["right_side", "coefficient", "solution", "residual"] + list(scratch)
    shape = jax.ShapeDtypeStruct((nx * ny, nz), F32)
    found = pl.pallas_call(
        functools.partial(kernel, count_x, count_y, names),
        out_shape=(shape, shape),
        in_specs=[pl.BlockSpec(memory_space=pl.ANY)] * 2,
        out_specs=(pl.BlockSpec(memory_space=pl.ANY),) * 2,
        scratch_shapes=list(scratch.values()),
        compiler_params=pltpu.CompilerParams(
            collective_id=0, has_side_effects=True, vmem_limit_bytes=56 << 20
        ),
        name="vcycle",
    )(right_side.reshape(nx * ny, nz), coefficient.reshape(nx * ny, nz))
    return tuple(value.reshape(nx, ny, nz) for value in found)


def solution(mesh):
    spec = P("gx", "gy", None)
    step = functools.partial(per_device, mesh.shape["gx"], mesh.shape["gy"])
    return jax.shard_map(step, mesh=mesh, in_specs=(spec, spec), out_specs=(spec, spec), check_vma=False)
```

```python
import functools

import jax
import jax.numpy as jnp
from jax import lax
from jax.experimental import pallas as pl
from jax.experimental.pallas import tpu as pltpu
from jax.sharding import PartitionSpec as P

MESH = pl.DeviceIdType.MESH
F32 = jnp.float32

SMOOTH_LO, SMOOTH_HI = 0.5, 2.0
COARSE_LO, COARSE_HI = 0.05, 2.0
BOTTOM = 8

STEPS = ((1, 1), (1, -1), (-1, 1), (-1, -1), (0, 1), (0, -1), (1, 0), (-1, 0))
ALONG_GX, ALONG_GY = (6, 7), (0, 1, 2, 3, 4, 5)


def coefficients(low, high, sweeps):
    theta = (high + low) / 2.0
    delta = (high - low) / 2.0
    sigma = theta / delta
    rho = 1.0 / sigma
    pairs = []
    for _ in range(sweeps - 1):
        rho_next = 1.0 / (2.0 * sigma - rho)
        pairs.append((rho_next * rho, 2.0 * rho_next / delta))
        rho = rho_next
    return theta, pairs


THETA, ((MOMENTUM, STEP),) = coefficients(SMOOTH_LO, SMOOTH_HI, 2)


def harmonic(own, other):
    return 2.0 * own * other / (own + other)


def roll(value, shift, axis):
    size = value.shape[axis]
    return pltpu.roll(value, shift % size, axis)


def iota(shape, dim):
    return lax.broadcasted_iota(jnp.int32, shape, dim)


def times(rows, matrix):
    high = rows.astype(jnp.bfloat16)
    rest = rows - high.astype(F32)
    middle = rest.astype(jnp.bfloat16)
    low = (rest - middle.astype(F32)).astype(jnp.bfloat16)
    found = [jnp.dot(term, matrix, preferred_element_type=F32) for term in (low, middle, high)]
    return (found[0] + found[1]) + found[2]


def loop(start, stop, body, unroll=1):
    count = (stop - start) // unroll

    def step(index, carry):
        for k in range(unroll):
            body(start + index * unroll + k)
        return carry

    if count > 1:
        lax.fori_loop(0, count, step, 0)
        start += count * unroll
    for index in range(start, stop):
        body(index)


class Exchange:
    def __init__(self, field, landing, send, recv, halo, depth, corner, skip=0):
        self.skip = skip
        self.field, self.wide = field, landing is None
        self.left, self.right = (None, None) if self.wide else landing
        self.send, self.recv = send, recv
        self.halo, self.depth, self.corner = halo, depth, corner
        self.planes = field.shape[0] - 2 * halo
        self.rows = field.shape[1] - (16 if self.wide else 8)

    def copies(self, place):
        h, n, r, x = self.halo, self.planes, self.depth, self.rows
        found, self.tiles = [], 0
        for number, (dx, dy) in enumerate(STEPS):
            if dx == 0:
                count, skip = r - self.skip, self.skip
                source_plane = h + n - r if dy > 0 else h + skip
                target_plane = h - r if dy > 0 else h + n + skip
                source = self.field.at[pl.ds(source_plane, count), pl.ds(0, x)]
                target = self.field.at[pl.ds(target_plane, count), pl.ds(0, x)]
            else:
                count = n if dy == 0 else self.corner
                source_plane = h if dy <= 0 else h + n - count
                target_plane = h if dy == 0 else (h - count if dy > 0 else h + n)
                source = self.field.at[pl.ds(source_plane, count), pl.ds(x - 8 if dx > 0 else 0, 8)]
                if self.wide:
                    target = self.field.at[pl.ds(target_plane, count), pl.ds(x + 8 if dx > 0 else x, 8)]
                else:
                    landing = self.left if dx > 0 else self.right
                    target = landing.at[pl.ds(target_plane, count)]
            self.tiles += source.shape[0] * source.shape[1] * source.shape[2] // 1024
            found.append(
                pltpu.make_async_remote_copy(
                    src_ref=source,
                    dst_ref=target,
                    send_sem=self.send.at[0],
                    recv_sem=self.recv.at[number],
                    device_id=place(dx, dy),
                    device_id_type=MESH,
                )
            )
        return found

    def start(self, place):
        self.started = self.copies(place)
        for copy in self.started:
            copy.start()

    def arrive(self, which):
        for number in which:
            self.started[number].wait_recv()

    def merge(self, start, stop):
        if self.wide:
            return
        x = self.rows
        shape = (8, self.field.shape[2])

        def body(p):
            upper = iota(shape, 0) < 4
            self.field[p, x:, :] = jnp.where(upper, self.right[p], self.left[p])

        loop(start, stop, body, 4)

    def merge_mended(self, start, stop, at_low, at_high):
        x = self.rows
        shape = (8, self.field.shape[2])
        row = iota(shape, 0)
        take_high = jnp.where(row == 0, at_high, 0) == 1
        take_low = jnp.where(row == 7, at_low, 0) == 1
        upper = row < 4

        def ends(p):
            high, low = self.field[p, x : x + 8, :], self.field[p, x + 8 :, :]
            self.field[p, x : x + 8, :] = jnp.where(take_high, roll(self.field[p, x - 8 : x, :], 1, 0), high)
            self.field[p, x + 8 :, :] = jnp.where(take_low, roll(self.field[p, 0:8, :], 7, 0), low)

        if self.wide:
            loop(start, stop, ends, 4)
            return

        def body(p):
            tile = jnp.where(upper, self.right[p], self.left[p])
            tile = jnp.where(take_high, roll(self.field[p, x - 8 : x, :], 1, 0), tile)
            self.field[p, x:, :] = jnp.where(take_low, roll(self.field[p, 0:8, :], 7, 0), tile)

        loop(start, stop, body, 4)

    def sent(self, idle):
        whole = idle.at[pl.ds(0, self.tiles)]
        pltpu.make_async_copy(whole, whole, self.send.at[0]).wait()


class Level:
    def __init__(self, number, lanes, refs, gx, gy, counts):
        self.scale = 0.25**number
        self.lanes = lanes
        self.gx, self.gy = gx, gy
        self.count_x, self.count_y = counts
        (self.k, self.b, self.xh, self.x1, self.x2, self.wx, self.wy, self.wz, self.w, self.inv, self.z0, self.z1) = refs
        self.h = self.k.halo
        self.n = self.k.planes
        self.x = self.k.rows
        self.shape = self.k.field.shape[1:]
        self.period = lanes
        self.unroll = 2 if number == 0 else 4

    def merge_k(self, start, stop):
        at_low = jnp.where(self.gx == 0, 1, 0)
        at_high = jnp.where(self.gx == self.count_x - 1, 1, 0)
        self.k.merge_mended(start, stop, at_low, at_high)

    def row_ok(self):
        row = iota(self.shape, 0)
        below = jnp.where(self.gx == 0, 1, 0)
        above = jnp.where(self.gx == self.count_x - 1, 1, 0)
        middle = (self.x + self.shape[0]) // 2
        bad_low = jnp.where(row >= middle, below, 0)
        bad_high = jnp.where((row >= self.x) & (row < middle), above, 0)
        return (bad_low + bad_high) == 0

    def plane_ok(self, p):
        y = self.gy * self.n + p - self.h
        return (y >= 0) & (y < self.count_y * self.n)

    def mend_planes(self):
        field, h, n = self.k.field, self.h, self.n

        @pl.when(self.gy == 0)
        def _():
            field[h - 1] = field[h]

        @pl.when(self.gy == self.count_y - 1)
        def _():
            field[h + n] = field[h + n - 1]

    def lane(self):
        return iota(self.shape, 1) % self.period

    def faces(self, start, stop):
        k = self.k.field

        def body(p):
            own = k[p]
            self.wx[p] = harmonic(own, roll(own, -1, 0))
            along = harmonic(own, roll(own, -1, 1))
            self.wz[p] = jnp.where(self.lane() == self.period - 1, 0.0, along)

        loop(start, stop, body, self.unroll)

    def faces_inside(self):
        k, h, n, x = self.k.field, self.h, self.n, self.x
        last = self.lane()[0:x] == self.period - 1

        def body(p):
            own = k[p, 0:x, :]
            self.wx[p, 0:x, :] = harmonic(own, roll(own, -1, 0))
            self.wz[p, 0:x, :] = jnp.where(last, 0.0, harmonic(own, roll(own, -1, 1)))

        def along(p):
            self.wy[p, 0:x, :] = harmonic(k[p, 0:x, :], k[p + 1, 0:x, :])

        loop(h, h + n, body, self.unroll)
        loop(h, h + n - 1, along, self.unroll)

    def faces_edge(self):
        k, h, n, x = self.k.field, self.h, self.n, self.x
        last = self.lane()[0:8] == self.period - 1
        inner = iota((8, self.shape[1]), 0) < 7
        after = lambda own, following: jnp.where(inner, roll(own, -1, 0), roll(following, -1, 0))

        def body(p):
            first, end, halo = k[p, 0:8, :], k[p, x - 8 : x, :], k[p, x:, :]
            self.wx[p, x - 8 : x, :] = harmonic(end, after(end, halo))
            self.wx[p, x:, :] = harmonic(halo, after(halo, first))
            self.wz[p, x:, :] = jnp.where(last, 0.0, harmonic(halo, roll(halo, -1, 1)))

        def along(p):
            self.wy[p, x:, :] = harmonic(k[p, x:, :], k[p + 1, x:, :])

        loop(h, h + n, body, 4)
        loop(h, h + n - 1, along, 4)

    def faces_y(self, start, stop):
        k = self.k.field

        def body(p):
            self.wy[p] = harmonic(k[p], k[p + 1])

        loop(start, stop, body, self.unroll)

    def totals(self, start, stop):
        k = self.k.field
        rows_ok = self.row_ok()

        def body(p):
            wx, wz = self.wx[p], self.wz[p]
            lane = self.lane()
            edge = jnp.where((lane == 0) | (lane == self.period - 1), k[p], 0.0)
            total = wx + roll(wx, 1, 0) + self.wy[p] + self.wy[p - 1] + wz + roll(wz, 1, 1) + edge
            self.w[p] = total
            ok = rows_ok & self.plane_ok(p)
            self.inv[p] = jnp.where(ok, 1.0 / total, 0.0)

        loop(start, stop, body, self.unroll)

    def beside(self, field, p):
        own, wx, wz = field[p], self.wx[p], self.wz[p]
        found = wx * roll(own, -1, 0) + roll(wx * own, 1, 0)
        found = found + self.wy[p] * field[p + 1] + self.wy[p - 1] * field[p - 1]
        return found + wz * roll(own, -1, 1) + roll(wz * own, 1, 1)

    def first(self, start, stop):
        def body(p):
            self.x1[p] = self.b[p] * self.inv[p] * (1.0 / (THETA * self.scale))

        loop(start, stop, body, self.unroll)

    def second(self, margin):
        h, n, x = self.h, self.n, self.x

        def value(p):
            own = self.x1[p]
            factor = 1.0 + MOMENTUM + STEP * (THETA - 1.0)
            return factor * own + STEP * (self.inv[p] * self.beside(self.x1, p))

        def plain(p):
            self.x2[p] = value(p)

        def kept(p):
            found = value(p)
            self.x2[p] = found
            if self.lanes < 128:
                first = iota(found.shape, 1) < self.lanes
                found = jnp.where(first, found, self.x1[p])
            self.xh.field[p, 0:x, :] = found[0:x, :]

        if self.xh is None:
            loop(h - margin, h + n + margin, plain, self.unroll)
            return
        loop(h, h + n, kept, self.unroll)
        for p in list(range(h - margin, h)) + list(range(h + n, h + n + margin)):
            plain(p) if self.xh.skip == 0 else kept(p)

    def residual(self, field, p):
        return self.b[p] - self.scale * (self.w[p] * field[p] - self.beside(field, p))

    def correct(self, p, grown):
        ok = self.rows_ok & self.plane_ok(p)
        base = self.x2[p] if self.xh is None or self.lanes < 128 else self.xh.field[p]
        self.z0[p] = jnp.where(ok, base + grown, 0.0)

    def third(self, start, stop):
        def body(p):
            own = self.z0[p]
            flow = self.inv[p] * self.beside(self.z0, p)
            self.z1[p] = (1.0 - 1.0 / THETA) * own + self.x1[p] + (1.0 / THETA) * flow

        loop(start, stop, body, self.unroll)

    def fourth(self, start, stop, target):
        def body(p):
            own = self.z1[p]
            flow = self.inv[p] * self.beside(self.z1, p)
            found = (1.0 + MOMENTUM - STEP) * own - MOMENTUM * self.z0[p]
            target[p] = found + (STEP * THETA) * self.x1[p] + STEP * flow

        loop(start, stop, body, self.unroll)


LOW, HIGH = 8, 16


class Whole:
    def __init__(self, refs):
        self.scale = 0.25**3
        self.size_z = 32
        self.k, self.b, self.x1, self.x2, self.wx, self.wy, self.wz, self.w, self.inv = refs
        self.count = self.k.shape[0] - 2
        self.rows = self.k.shape[1] - LOW - HIGH
        self.shape = (self.rows, 128)

    def blank(self):
        for ref in (self.k, self.x1, self.x2, self.wx, self.wy, self.wz, self.inv):
            empty = jnp.zeros(ref.shape[1:], F32)
            ref[0] = empty
            ref[self.count + 1] = empty

            def body(g, ref=ref):
                ref[g, 0:LOW, :] = jnp.zeros((LOW, 128), F32)
                ref[g, LOW + self.rows :, :] = jnp.zeros((HIGH, 128), F32)

            loop(1, self.count + 1, body, 4)

    def at(self, ref, g):
        return ref[g, LOW : LOW + self.rows, :]

    def after(self, own, following):
        inner = iota(own.shape, 1) < 128 - self.size_z
        return jnp.where(inner, roll(own, -self.size_z, 1), roll(following, -self.size_z, 1))

    def before(self, own, previous):
        inner = iota(own.shape, 1) >= self.size_z
        return jnp.where(inner, roll(own, self.size_z, 1), roll(previous, self.size_z, 1))

    def weights(self):
        rows, inside = self.rows, slice(LOW, LOW + self.rows)

        def faces(g):
            own, following = self.at(self.k, g), self.at(self.k, g + 1)
            lane, row = iota(self.shape, 1), iota(self.shape, 0)
            end = jnp.where(lane >= 128 - self.size_z, jnp.where(g == self.count, 1, 0), 0)
            self.wx[g, inside, :] = jnp.where(end == 1, 0.0, harmonic(own, self.after(own, following)))
            self.wy[g, inside, :] = jnp.where(row == rows - 1, 0.0, harmonic(own, roll(own, -1, 0)))
            last = lane % self.size_z == self.size_z - 1
            self.wz[g, inside, :] = jnp.where(last, 0.0, harmonic(own, roll(own, -1, 1)))

        loop(1, self.count + 1, faces)

        def totals(g):
            lane, row = iota(self.shape, 1), iota(self.shape, 0)
            high = jnp.where(lane >= 128 - self.size_z, jnp.where(g == self.count, 1.0, 0.0), 0.0)
            low = jnp.where(lane < self.size_z, jnp.where(g == 1, 1.0, 0.0), 0.0)
            edge = high + low
            edge = edge + jnp.where((row == 0) | (row == rows - 1), 1.0, 0.0)
            z = lane % self.size_z
            edge = edge + jnp.where((z == 0) | (z == self.size_z - 1), 1.0, 0.0)
            wx, wy, wz = self.at(self.wx, g), self.at(self.wy, g), self.at(self.wz, g)
            total = wx + self.before(wx, self.at(self.wx, g - 1)) + wy + roll(wy, 1, 0) + wz + roll(wz, 1, 1)
            total = total + edge * self.at(self.k, g)
            self.w[g, inside, :] = total
            self.inv[g, inside, :] = 1.0 / total

        loop(1, self.count + 1, totals)

    def flow(self, fields, weights):
        previous, own, following = fields
        wx_previous, wx, wy, wz = weights
        found = wx * self.after(own, following) + self.before(wx * own, wx_previous * previous)
        found = found + wy * roll(own, -1, 0) + roll(wy * own, 1, 0)
        return found + wz * roll(own, -1, 1) + roll(wz * own, 1, 1)

    def beside(self, field, g):
        fields = [self.at(field, g + step) for step in (-1, 0, 1)]
        weights = [self.at(self.wx, g - 1)] + [self.at(ref, g) for ref in (self.wx, self.wy, self.wz)]
        return self.flow(fields, weights)

    def down(self, left):
        inside = slice(LOW, LOW + self.rows)

        def first(g):
            found = self.at(self.b, g) * self.at(self.inv, g) * (1.0 / (THETA * self.scale))
            self.x1[g, inside, :] = found

        loop(1, self.count + 1, first, 2)

        def second(g):
            factor = 1.0 + MOMENTUM + STEP * (THETA - 1.0)
            moved = self.at(self.inv, g) * self.beside(self.x1, g)
            self.x2[g, inside, :] = factor * self.at(self.x1, g) + STEP * moved

        loop(1, self.count + 1, second, 2)

        def residual(g):
            applied = self.at(self.w, g) * self.at(self.x2, g) - self.beside(self.x2, g)
            left[g - 1] = self.at(self.b, g) - self.scale * applied

        loop(1, self.count + 1, residual, 2)

    def up(self, gx, start, grown, held, answer):
        span = pl.ds(start, 24)
        z0, z1 = held
        planes = (0, 1, 2)
        part = lambda ref, c: ref[gx + c, span, :]
        for c in planes:
            z0[c + 1] = part(self.x2, c) + grown[c, span, :]

        def flow(field, c):
            fields = [field[c + step] for step in (0, 1, 2)]
            before = self.wx[jnp.maximum(gx + c - 1, 0), span, :]
            return part(self.inv, c) * self.flow(fields, [before, part(self.wx, c), part(self.wy, c), part(self.wz, c)])

        for c in planes:
            z1[c + 1] = (1.0 - 1.0 / THETA) * z0[c + 1] + part(self.x1, c) + (1.0 / THETA) * flow(z0, c)
        for c in planes:
            found = (1.0 + MOMENTUM - STEP) * z1[c + 1] - MOMENTUM * z0[c + 1]
            answer[c] = found + (STEP * THETA) * part(self.x1, c) + STEP * flow(z1, c)


class Deepest:
    def __init__(self, count):
        self.count = count
        self.scale = 0.25**4
        shape = (8, 128)
        self.lane, self.row = iota(shape, 1), iota(shape, 0)
        self.low_x = (self.lane % 32) < 16
        self.zero = jnp.zeros(shape, F32)

    def next_x(self, tiles):
        back, ahead = [roll(t, -16, 1) for t in tiles], [roll(t, 16, 1) for t in tiles] + [self.zero]
        return [jnp.where(self.low_x, back[g], ahead[g + 1]) for g in range(self.count)]

    def last_x(self, tiles):
        back, ahead = [self.zero] + [roll(t, -16, 1) for t in tiles], [roll(t, 16, 1) for t in tiles]
        return [jnp.where(self.low_x, back[g], ahead[g]) for g in range(self.count)]

    def next_y(self, tiles):
        moved = [roll(t, -1, 0) for t in tiles]
        return [jnp.where(self.row < 7, t, roll(t, -32, 1)) for t in moved]

    def last_y(self, tiles):
        moved = [roll(t, 1, 0) for t in tiles]
        return [jnp.where(self.row > 0, t, roll(t, 32, 1)) for t in moved]

    def next_z(self, tiles):
        return [roll(t, -1, 1) for t in tiles]

    def last_z(self, tiles):
        return [roll(t, 1, 1) for t in tiles]

    def weights(self, k, weight_refs, inv_ref):
        lane, row, span = self.lane, self.row, range(self.count)
        z = lane % 16
        end_y = (row == 7) & (lane >= 96)
        edge = jnp.where((z == 0) | (z == 15), 1.0, 0.0)
        edge = edge + jnp.where(end_y | ((row == 0) & (lane < 32)), 1.0, 0.0)
        faces_x = [harmonic(a, b) for a, b in zip(k, self.next_x(k))]
        faces_x[-1] = jnp.where(self.low_x, faces_x[-1], 0.0)
        faces_y = [jnp.where(end_y, 0.0, harmonic(a, b)) for a, b in zip(k, self.next_y(k))]
        faces_z = [jnp.where(z == 15, 0.0, harmonic(a, b)) for a, b in zip(k, self.next_z(k))]
        sets = [faces_x, self.last_x(faces_x), faces_y, self.last_y(faces_y), faces_z, self.last_z(faces_z)]
        for g in span:
            total = edge * k[g]
            if g == 0:
                total = total + jnp.where(self.low_x, k[g], 0.0)
            if g == self.count - 1:
                total = total + jnp.where(self.low_x, 0.0, k[g])
            for one in sets:
                total = total + one[g]
            inv = 1.0 / total
            inv_ref[g] = inv
            for number, one in enumerate(sets):
                weight_refs[number, g] = one[g] * inv

    def solve(self, b, weight_refs, inv_ref):
        theta, pairs = coefficients(COARSE_LO, COARSE_HI, BOTTOM)
        span = range(self.count)
        scaled = [b[g] * inv_ref[g] * (1.0 / self.scale) for g in span]
        update = [t * (1.0 / theta) for t in scaled]
        found = update
        for momentum, step in pairs:
            shifted = [
                self.next_x(found),
                self.last_x(found),
                self.next_y(found),
                self.last_y(found),
                self.next_z(found),
                self.last_z(found),
            ]
            following = []
            for g in span:
                flow = weight_refs[0, g] * shifted[0][g]
                for number in range(1, 6):
                    flow = flow + weight_refs[number, g] * shifted[number][g]
                following.append(momentum * update[g] + step * ((scaled[g] - found[g]) + flow))
            update = following
            found = [a + d for a, d in zip(found, update)]
        return found


def shrink_lanes(lanes, kept):
    row, col = iota((max(lanes, 128), 128), 0), iota((max(lanes, 128), 128), 1)
    return jnp.where((row // 2 == col % kept) & (row < lanes), 0.125, 0.0).astype(jnp.bfloat16)


def grow_lanes(kept, lanes):
    row, col = iota((128, lanes), 0), iota((128, lanes), 1)
    period = 2 * kept
    return jnp.where((col % period) // 2 == row, 1.0, 0.0).astype(jnp.bfloat16)


def restrict(read, target, count, fine_plane, coarse_plane, rows, matrix, half, sums):
    kept = rows // 2
    parts = matrix.shape[0] // 128

    def body(j):
        pair = read(fine_plane + 2 * j) + read(fine_plane + 2 * j + 1)
        slot = j % 2
        for part in range(parts):
            half[slot, part, 0:rows, :] = pair[:, part * 128 : (part + 1) * 128]
        for part in range(parts):
            even = half[slot, part, pl.ds(0, kept, stride=2), :]
            odd = half[slot, part, pl.ds(1, kept, stride=2), :]
            sums[pl.ds(pl.multiple_of(j * kept, 8), kept), 128 * part : 128 * (part + 1)] = even + odd

    loop(0, count, body, 2)
    means = times(sums[0 : count * kept, 0 : 128 * parts], matrix[...])
    target[coarse_plane : coarse_plane + count, 0:kept, :] = means.reshape(count, kept, 128)


def grow(source, planes, rows, matrix, doubled):
    start, stop = planes
    count, parts = stop - start, matrix.shape[1] // 128
    wide = times(source[start:stop].reshape(count * rows, 128), matrix[...])
    for j in range(count):
        for part in range(parts):
            piece = wide[j * rows : (j + 1) * rows, 128 * part : 128 * (part + 1)]
            doubled[j, part, pl.ds(0, rows, stride=2), :] = piece
            doubled[j, part, pl.ds(1, rows, stride=2), :] = piece


def grown_plane(doubled, j, rows, parts):
    own = 2 * (rows - 16)
    upper = iota((8, 128), 0) < 4
    found = []
    for part in range(parts):
        tail = jnp.where(upper, doubled[j, part, own : own + 8, :], doubled[j, part, own + 24 : own + 32, :])
        found.append(jnp.concatenate([doubled[j, part, 0:own, :], tail], axis=0))
    return found[0] if parts == 1 else jnp.concatenate(found, axis=1)


def kernel(count_x, count_y, names, *refs):
    r = dict(zip(names, refs))
    gx, gy = lax.axis_index("gx"), lax.axis_index("gy")
    ring_x = 4
    ring_z = count_y // ring_x
    chip_x, chip_z = gy % ring_x, gy // ring_x

    def place(dx, dy):
        return ((gx + dx + count_x) % count_x, (gy + dy + count_y) % count_y)

    def along_x(d):
        return (gx, chip_z * ring_x + (chip_x + d) % ring_x)

    def along_z(d):
        return (gx, ((chip_z + d) % ring_z) * ring_x + chip_x)

    def along_gx(d):
        return ((gx + d) % count_x, gy)

    z_steps = [d for d in range(1, ring_z) if min(d, ring_z - d) <= 3]
    partners = [place(dx, dy) for dx, dy in STEPS]
    partners += [along_x(d) for d in range(1, ring_x)]
    partners += [along_z(d) for d in z_steps]
    partners += [along_gx(d) for d in range(1, count_x)]

    def halves(whole, staged, first, store):
        copies = []
        for part in range(2):
            wide = whole.at[:, pl.ds(128 * part, 128)]
            pair = (staged.at[part], wide) if store else (wide, staged.at[part])
            copies.append(pltpu.make_async_copy(*pair, r["load"].at[first + part]))
        return copies

    loads_k = halves(r["coefficient"], r["k_in"], 0, False)
    loads_b = halves(r["right_side"], r["b_in"], 2, False)
    for copy in loads_k + loads_b:
        copy.start()
    barrier = pltpu.get_barrier_semaphore()
    for partner in partners:
        pl.semaphore_signal(barrier, inc=1, device_id=partner, device_id_type=MESH)

    def exchange(name, number, halo, depth):
        tag = f"{name}{number}"
        if not depth:
            return None
        landing = (r[tag + "_l"], r[tag + "_r"]) if tag + "_l" in r else None
        corner = depth if number == 2 else depth - 1
        return Exchange(r[tag], landing, r[tag + "_send"], r[tag + "_recv"], halo, depth, corner, 1 if tag == "xh0" else 0)

    levels, sources = [], []
    for number, (lanes, halo, depth_k, depth_b, depth_x) in enumerate(SHAPES):
        sources.append(exchange("b", number, halo, depth_b))
        fields = [exchange("k", number, halo, depth_k), r[f"b{number}"], exchange("xh", number, halo, depth_x)]
        fields += [r[f"{name}{number}"] for name in LOCAL]
        levels.append(Level(number, lanes, fields, gx, gy, (count_x, count_y)))
    l0, l1, l2 = levels
    l3 = Whole([r[f"{name}3"] for name in WHOLE])
    l4 = Deepest(count_x)

    def turn(staged, target):
        for y in range(l0.n):
            for part in range(2):
                lanes = pl.ds(128 * part, 128)
                target[l0.h + y, 0 : l0.x, lanes] = staged[part, pl.ds(y, l0.x, stride=l0.n), :]

    square = (128, 128)
    row, col = iota(square, 0), iota(square, 1)
    same_x, same_z = (row // 32) // 2 == (col % 32) // 16, (row % 32) // 2 == col % 16
    back = ((row % 32) // 16 == (col // 32) // 2) & (row % 16 == (col % 32) // 2)
    one = lambda where, value: jnp.where(where, value, 0.0).astype(jnp.bfloat16)
    r["to_1"][...] = shrink_lanes(256, 128)
    r["to_2"][...] = shrink_lanes(128, 64)
    r["to_3"][...] = one((row < 64) & (row // 2 == col % 32), 0.125)
    r["to_4"][...] = one(same_x & same_z, 0.125)
    r["from_4"][...] = one(back, 1.0)
    r["from_3"][...] = one(row % 32 == (col % 64) // 2, 1.0)
    r["from_2"][...] = grow_lanes(64, 128)
    r["from_1"][...] = grow_lanes(128, 256)

    for copy in loads_k:
        copy.wait()
    turn(r["k_in"], r["k0"])
    for copy in loads_b:
        copy.wait()
    turn(r["b_in"], r["b0"])
    pl.semaphore_wait(barrier, len(partners))
    l0.k.start(place)
    sources[0].start(place)

    half, sums, doubled = r["half"], r["sums"], r["doubled"]
    k0, k1, k2 = r["k0"], r["k1"], r["k2"]
    to_1, to_2 = r["to_1"], r["to_2"]
    restrict(lambda p: k0[p, 0 : l0.x, :], k1, l1.n, l0.h, l1.h, l0.x, to_1, half, sums)
    l1.k.start(place)
    restrict(lambda p: k1[p, 0 : l1.x, :], k2, l2.n, l1.h, l2.h, l1.x, to_2, half, sums)

    def small_block(read):
        tile = (8, 128)
        mine = iota(tile, 1) // 32 == iota(tile, 0) // 2
        pairs = [read(l2.h + 2 * j) + read(l2.h + 2 * j + 1) for j in range(2)]
        means = times(jnp.concatenate(pairs, axis=0), r["to_3"][...])
        found = jnp.zeros(tile, F32)
        for j in range(2):
            spread = jnp.where(mine, means[8 * j : 8 * j + 8], 0.0)
            line = jnp.sum(spread, axis=0, keepdims=True)
            found = jnp.where(iota(tile, 0) == 2 * chip_x + j, jnp.broadcast_to(line, tile), found)
        return found

    class Gather:
        def __init__(self, name, target, eager):
            self.first, self.target, self.eager = r[name + "_first"], target, eager
            self.send, self.recv = r[name + "_send"], r[name + "_recv"]
            self.tiles_sent, self.tiles_last = 0, 0

        def go(self, sems, source, target, where, steps):
            copies = []
            for d in steps:
                copies.append(
                    pltpu.make_async_remote_copy(
                        src_ref=source,
                        dst_ref=target,
                        send_sem=self.send.at[0],
                        recv_sem=self.recv.at[sems(d)],
                        device_id=where(d),
                        device_id_type=MESH,
                    )
                )
            for copy in copies:
                copy.start()
            self.tiles_sent += len(copies) * (source.shape[0] // 8)
            return copies

        def along_x(self, tile):
            self.first[chip_x] = tile
            slot = self.first.at[chip_x]
            self.near = self.go(lambda d: d, slot, slot, along_x, range(1, ring_x))

        def part(self, d):
            rows = pl.ds(pl.multiple_of(8 * ((chip_z + ring_z - d) % ring_z) + LOW, 8), 8)
            return self.target.at[gx + 1, rows]

        def pass_on(self, part):
            self.go(lambda d: 0, part, part, along_gx, range(1, count_x))
            self.tiles_last += (count_x - 1) * (part.shape[0] // 8)

        def along_z(self):
            for copy in self.near:
                copy.wait_recv()
            found = self.first[0]
            for slot in range(1, ring_x):
                found = found + self.first[slot]
            tile = self.part(0)
            tile[...] = found
            self.far = self.go(lambda d: ring_x - 1 + d, tile, tile, along_z, z_steps)
            if self.eager:
                self.pass_on(tile)

        def along_gx(self):
            for d, copy in sorted(zip(z_steps, self.far), key=lambda pair: min(pair[0], ring_z - pair[0])):
                copy.wait_recv()
                if self.eager:
                    self.pass_on(self.part(d))
            if not self.eager:
                self.pass_on(self.target.at[gx + 1, pl.ds(LOW, 8 * ring_z)])

        def arrive(self):
            whole = r["idle"].at[pl.ds(0, self.tiles_last)]
            pltpu.make_async_copy(whole, whole, self.recv.at[0]).wait()

        def sent(self):
            whole = r["idle"].at[pl.ds(0, self.tiles_sent)]
            pltpu.make_async_copy(whole, whole, self.send.at[0]).wait()

    gather_k, gather_b = Gather("gk", l3.k, False), Gather("gb", l3.b, True)
    gather_k.along_x(small_block(lambda p: k2[p, 0 : l2.x, :]))
    l3.blank()
    for d in range(1, ring_z):
        if d not in z_steps:
            unused = pl.ds(pl.multiple_of(8 * ((chip_z + d) % ring_z) + LOW, 8), 8)
            l3.k[gx + 1, unused, :] = jnp.ones((8, 128), F32)
            for g in range(1, count_x + 1):
                l3.b[g, unused, :] = jnp.zeros((8, 128), F32)
    z0_3, z1_3 = r["z0_3"], r["z1_3"]
    for held in (z0_3, z1_3):
        held[0] = jnp.zeros((24, 128), F32)
        held[4] = jnp.zeros((24, 128), F32)
    grown3 = r["grown3"]
    for c in range(3):
        grown3[c, 0:LOW, :] = jnp.zeros((LOW, 128), F32)
        grown3[c, LOW + 8 * ring_z :, :] = jnp.zeros((HIGH, 128), F32)

    def ready(level, between=None):
        h, n, depth = level.h, level.n, level.k.depth
        if level.k.wide:
            level.k.arrive(ALONG_GX)
            level.merge_k(h, h + n)
            level.faces(h, h + n)
            level.faces_y(h, h + n - 1)
        else:
            level.faces_inside()
            level.k.arrive(ALONG_GX)
            level.merge_k(h, h + n)
            level.faces_edge()
        level.totals(h + 1, h + n - 1)
        if between is not None:
            between()
        level.k.arrive(ALONG_GY)
        low, high = h - depth + 1, h + n + depth - 1
        level.merge_k(h - level.k.corner, h)
        level.merge_k(h + n, h + n + level.k.corner)
        level.mend_planes()
        level.faces(low, h)
        level.faces(h + n, high)
        level.faces_y(h - depth, h)
        level.faces_y(h + n - 1, high)
        level.totals(low, h + 1)
        level.totals(h + n - 1, high)

    def descend(level, source, depth):
        h, n = level.h, level.n
        if source is not None:
            source.arrive(range(8))
            source.merge(h - depth + 1, h + n + depth - 1)
        level.first(h - depth, h + n + depth)
        level.second(depth - 1)

    def source_below(level, target, margin, rows, matrix):
        below = levels[levels.index(level) + 1]
        read = lambda p: level.residual(level.x2, p)[0:rows, :]
        count, fine = below.n + 2 * margin, level.h - 2 * margin
        restrict(read, target, count, fine, below.h - margin, rows, matrix, half, sums)

    ready(l0)
    descend(l0, sources[0], 2)
    source_below(l0, r["b1"], 0, l0.x, to_1)
    sources[1].start(place)
    gather_k.along_z()
    l2.k.start(place)
    ready(l1)
    sources[1].arrive(range(8))
    gather_k.along_gx()
    descend(l1, None, 6)
    source_below(l1, r["b2"], 2, l1.x + 16, to_2)
    ready(l2)
    descend(l2, None, 2)
    gather_b.along_x(small_block(lambda p: l2.residual(l2.x2, p)[0 : l2.x, :]))
    def to_bottom(source, low):
        kept = 4 * ring_z
        pieces = []
        for g in range(count_x):
            even = source[g, pl.ds(low, kept, stride=2), :]
            odd = source[g, pl.ds(low + 1, kept, stride=2), :]
            pieces.append(even + odd)
        means = times(jnp.concatenate(pieces, axis=0), r["to_4"][...])
        group = iota((8, 128), 1) // 32
        tiles = []
        for g in range(count_x):
            found = means[g * kept : g * kept + 8]
            for q in range(1, 4):
                found = jnp.where(group == q, means[g * kept + 8 * q : g * kept + 8 * q + 8], found)
            tiles.append(found)
        return tiles

    gather_k.arrive()
    l3.weights()
    gather_b.along_z()
    l4.weights(to_bottom(l3.k.at[pl.ds(1, count_x)], LOW), r["w4"], r["inv4"])
    gather_b.along_gx()
    l2.xh.start(place)
    l0.xh.start(place)
    for field in [level.k for level in levels] + sources[:2]:
        field.sent(r["idle"])
    gather_k.sent()
    gather_b.arrive()
    l3.down(r["left3"])
    deepest = l4.solve(to_bottom(r["left3"], 0), r["w4"], r["inv4"])
    tiles4 = r["tiles4"]
    tiles4[0] = l4.zero
    tiles4[count_x + 1] = l4.zero
    for g in range(count_x):
        tiles4[g + 1] = deepest[g]

    group = iota((8, 128), 1) // 32
    spread = [jnp.where(group == q, tiles4[gx + c], 0.0) for c in range(3) for q in range(4)]
    wide = times(jnp.concatenate(spread, axis=0), r["from_4"][...])
    for c in range(3):
        piece = wide[32 * c : 32 * c + 32]
        grown3[c, pl.ds(LOW, 32, stride=2), :] = piece
        grown3[c, pl.ds(LOW + 1, 32, stride=2), :] = piece
    start = 8 * ((2 * gy + 4) // 8)
    answer = r["answer"]
    l3.up(gx, pl.multiple_of(start, 8), grown3, (z0_3, z1_3), answer)

    l2.xh.arrive(range(8))
    l2.xh.merge(0, 2 * l2.h + l2.n)
    tile = (8, 128)
    own_group = iota(tile, 1) // 32 == iota(tile, 0) // 2
    first_half = iota(tile, 0) < 4
    spread = []
    for j in range(6):
        at = 6 + 2 * gy + j - start
        lower, own, upper = [jnp.broadcast_to(answer[c, pl.ds(at, 1), :], tile) for c in range(3)]
        spread.append(jnp.where(own_group, own, 0.0))
        spread.append(jnp.where(own_group, jnp.where(first_half, upper, lower), 0.0))
    wide = times(jnp.concatenate(spread, axis=0), r["from_3"][...])
    l2.rows_ok = l2.row_ok()
    low_lanes = iota(l2.shape, 1) < 64
    for p in range(12):
        both = l2.xh.field[p]
        turned = roll(both, 64, 1)
        l2.x1[p] = jnp.where(l2.rows_ok & l2.plane_ok(p), jnp.where(low_lanes, turned, both), 0.0)
        l2.x2[p] = jnp.where(low_lanes, both, turned)
        l2.correct(p, wide[16 * (p // 2) : 16 * (p // 2) + 16])
    l2.third(1, 11)
    l2.fourth(2, 10, r["z2"])

    grow(r["z2"], (2, 10), 16, r["from_2"], doubled)
    l1.rows_ok = l1.row_ok()

    def lift_1(j):
        grown = doubled[j, 0, 0 : l1.x + 16, :]
        l1.correct(l1.h - 4 + 2 * j, grown)
        l1.correct(l1.h - 3 + 2 * j, grown)

    loop(0, 8, lift_1, 2)
    l1.third(l1.h - 3, l1.h + l1.n + 3)
    l1.fourth(l1.h - 2, l1.h + l1.n + 2, r["z1out"])

    grow(r["z1out"], (l1.h - 2, l1.h + l1.n + 2), 32, r["from_1"], doubled)
    l0.xh.arrive(range(8))
    l0.xh.merge(l0.h - 2, l0.h + l0.n + 2)
    l0.rows_ok = l0.row_ok()
    l0.correct(0, grown_plane(doubled, 0, 32, 2))

    def lift_0(j):
        grown = grown_plane(doubled, j, 32, 2)
        l0.correct(2 * j - 1, grown)
        l0.correct(2 * j, grown)

    loop(1, 11, lift_0)
    l0.correct(21, grown_plane(doubled, 11, 32, 2))
    l0.third(1, 21)
    l0.fourth(2, 20, l0.x2)

    def turn_back(staged, y, value):
        for part in range(2):
            lanes = slice(128 * part, 128 * (part + 1))
            staged[part, pl.ds(y, l0.x, stride=l0.n), :] = value[0 : l0.x, lanes]

    loop(0, l0.n, lambda y: turn_back(r["k_in"], y, l0.x2[l0.h + y]), 4)
    stores = halves(r["solution"], r["k_in"], 4, True)
    for copy in stores:
        copy.start()
    loop(0, l0.n, lambda y: turn_back(r["b_in"], y, l0.residual(l0.x2, l0.h + y)), 2)
    for copy in halves(r["residual"], r["b_in"], 6, True):
        copy.start()
        stores.append(copy)
    gather_b.sent()
    l2.xh.sent(r["idle"])
    l0.xh.sent(r["idle"])
    for copy in stores:
        copy.wait()


SHAPES = ((256, 3, 3, 2, 3), (128, 7, 7, 6, 0), (64, 4, 4, 0, 4))
LOCAL = ("x1_", "x2_", "wx", "wy", "wz", "w", "inv", "z0_", "z1_")
WHOLE = ("k", "b", "x1_", "x2_", "wx", "wy", "wz", "w", "inv")


def per_device(count_x, count_y, right_side, coefficient):
    nx, ny, nz = right_side.shape
    vmem = lambda *shape: pltpu.VMEM(shape, F32)
    rows3 = 2 * count_y
    scratch = {
        "k_in": vmem(2, nx * ny, 128),
        "b_in": vmem(2, nx * ny, 128),
        "load": pltpu.SemaphoreType.DMA((8,)),
        "half": vmem(2, 2, nx, 128),
        "idle": vmem(256, 8, 128),
        "to_1": pltpu.VMEM((256, 128), jnp.bfloat16),
        "from_1": pltpu.VMEM((128, 256), jnp.bfloat16),
        "sums": vmem(nx * ny // 4, nz),
        "doubled": vmem(ny // 2 + 4, 2, nx + 32, 128),
        "z0_3": vmem(5, 24, 128),
        "z1_3": vmem(5, 24, 128),
        "left3": vmem(count_x, rows3, 128),
        "w4": vmem(6, count_x, 8, 128),
        "inv4": vmem(count_x, 8, 128),
        "tiles4": vmem(count_x + 2, 8, 128),
        "grown3": vmem(3, LOW + rows3 + HIGH, 128),
        "answer": vmem(3, 24, 128),
        "z2": vmem((ny >> 2) + 8, (nx >> 2) + 8, 128),
        "z1out": vmem((ny >> 1) + 14, (nx >> 1) + 16, 128),
    }
    for name in ("to_2", "to_3", "to_4", "from_4", "from_3", "from_2"):
        scratch[name] = pltpu.VMEM((128, 128), jnp.bfloat16)
    for number, (lanes, halo, *depths) in enumerate(SHAPES):
        rows, planes, width = nx >> number, ny >> number, max(128, lanes)
        wide = number == 1
        full = (planes + 2 * halo, rows + (16 if wide else 8), width)
        scratch[f"b{number}"] = vmem(*full)
        for name, depth in zip(("k", "b", "xh"), depths):
            if not depth:
                continue
            tag = f"{name}{number}"
            scratch[tag] = vmem(*full)
            if not wide:
                scratch[tag + "_l"] = vmem(full[0], 8, width)
                scratch[tag + "_r"] = vmem(full[0], 8, width)
            scratch[tag + "_send"] = pltpu.SemaphoreType.DMA((1,))
            scratch[tag + "_recv"] = pltpu.SemaphoreType.DMA((8,))
        for name in LOCAL:
            scratch[f"{name}{number}"] = vmem(*full)
    for name in WHOLE:
        scratch[f"{name}3"] = vmem(count_x + 2, LOW + rows3 + HIGH, 128)
    for name in ("gk", "gb"):
        scratch[name + "_first"] = vmem(4, 8, 128)
        scratch[name + "_send"] = pltpu.SemaphoreType.DMA((1,))
        scratch[name + "_recv"] = pltpu.SemaphoreType.DMA((4 + count_y // 4,))

    names = ["right_side", "coefficient", "solution", "residual"] + list(scratch)
    shape = jax.ShapeDtypeStruct((nx * ny, nz), F32)
    found = pl.pallas_call(
        functools.partial(kernel, count_x, count_y, names),
        out_shape=(shape, shape),
        in_specs=[pl.BlockSpec(memory_space=pl.ANY)] * 2,
        out_specs=(pl.BlockSpec(memory_space=pl.ANY),) * 2,
        scratch_shapes=list(scratch.values()),
        compiler_params=pltpu.CompilerParams(
            collective_id=0, has_side_effects=True, vmem_limit_bytes=56 << 20
        ),
        name="vcycle",
    )(right_side.reshape(nx * ny, nz), coefficient.reshape(nx * ny, nz))
    return tuple(value.reshape(nx, ny, nz) for value in found)


def solution(mesh):
    spec = P("gx", "gy", None)
    step = functools.partial(per_device, mesh.shape["gx"], mesh.shape["gy"])
    return jax.shard_map(step, mesh=mesh, in_specs=(spec, spec), out_specs=(spec, spec), check_vma=False)
```

```python
import functools

import jax
import jax.numpy as jnp
from jax import lax
from jax.experimental import pallas as pl
from jax.experimental.pallas import tpu as pltpu
from jax.sharding import PartitionSpec as P

MESH = pl.DeviceIdType.MESH
F32 = jnp.float32

SMOOTH_LO, SMOOTH_HI = 0.5, 2.0
COARSE_LO, COARSE_HI = 0.05, 2.0
BOTTOM = 8

STEPS = ((1, 1), (1, -1), (-1, 1), (-1, -1), (0, 1), (0, -1), (1, 0), (-1, 0))
ALONG_GX, ALONG_GY = (6, 7), (0, 1, 2, 3, 4, 5)


def coefficients(low, high, sweeps):
    theta = (high + low) / 2.0
    delta = (high - low) / 2.0
    sigma = theta / delta
    rho = 1.0 / sigma
    pairs = []
    for _ in range(sweeps - 1):
        rho_next = 1.0 / (2.0 * sigma - rho)
        pairs.append((rho_next * rho, 2.0 * rho_next / delta))
        rho = rho_next
    return theta, pairs


THETA, ((MOMENTUM, STEP),) = coefficients(SMOOTH_LO, SMOOTH_HI, 2)


def harmonic(own, other):
    return 2.0 * own * other / (own + other)


def roll(value, shift, axis):
    size = value.shape[axis]
    return pltpu.roll(value, shift % size, axis)


def iota(shape, dim):
    return lax.broadcasted_iota(jnp.int32, shape, dim)


def times(rows, matrix):
    high = rows.astype(jnp.bfloat16)
    rest = rows - high.astype(F32)
    middle = rest.astype(jnp.bfloat16)
    low = (rest - middle.astype(F32)).astype(jnp.bfloat16)
    found = [jnp.dot(term, matrix, preferred_element_type=F32) for term in (low, middle, high)]
    return (found[0] + found[1]) + found[2]


def loop(start, stop, body, unroll=1):
    count = (stop - start) // unroll

    def step(index, carry):
        for k in range(unroll):
            body(start + index * unroll + k)
        return carry

    if count > 1:
        lax.fori_loop(0, count, step, 0)
        start += count * unroll
    for index in range(start, stop):
        body(index)


class Exchange:
    def __init__(self, field, landing, send, recv, halo, depth, corner, skip=0):
        self.skip = skip
        self.field, self.wide = field, landing is None
        self.left, self.right = (None, None) if self.wide else landing
        self.send, self.recv = send, recv
        self.halo, self.depth, self.corner = halo, depth, corner
        self.planes = field.shape[0] - 2 * halo
        self.rows = field.shape[1] - (16 if self.wide else 8)

    def copies(self, place):
        h, n, r, x = self.halo, self.planes, self.depth, self.rows
        found, self.tiles = [], 0
        for number, (dx, dy) in enumerate(STEPS):
            if dx == 0:
                count, skip = r - self.skip, self.skip
                source_plane = h + n - r if dy > 0 else h + skip
                target_plane = h - r if dy > 0 else h + n + skip
                source = self.field.at[pl.ds(source_plane, count), pl.ds(0, x)]
                target = self.field.at[pl.ds(target_plane, count), pl.ds(0, x)]
            else:
                count = n if dy == 0 else self.corner
                source_plane = h if dy <= 0 else h + n - count
                target_plane = h if dy == 0 else (h - count if dy > 0 else h + n)
                source = self.field.at[pl.ds(source_plane, count), pl.ds(x - 8 if dx > 0 else 0, 8)]
                if self.wide:
                    target = self.field.at[pl.ds(target_plane, count), pl.ds(x + 8 if dx > 0 else x, 8)]
                else:
                    landing = self.left if dx > 0 else self.right
                    target = landing.at[pl.ds(target_plane, count)]
            self.tiles += source.shape[0] * source.shape[1] * source.shape[2] // 1024
            found.append(
                pltpu.make_async_remote_copy(
                    src_ref=source,
                    dst_ref=target,
                    send_sem=self.send.at[0],
                    recv_sem=self.recv.at[number],
                    device_id=place(dx, dy),
                    device_id_type=MESH,
                )
            )
        return found

    def start(self, place):
        self.started = self.copies(place)
        for copy in self.started:
            copy.start()

    def arrive(self, which):
        for number in which:
            self.started[number].wait_recv()

    def merge(self, start, stop):
        if self.wide:
            return
        x = self.rows
        shape = (8, self.field.shape[2])

        def body(p):
            upper = iota(shape, 0) < 4
            self.field[p, x:, :] = jnp.where(upper, self.right[p], self.left[p])

        loop(start, stop, body, 4)

    def merge_mended(self, start, stop, at_low, at_high):
        x = self.rows
        shape = (8, self.field.shape[2])
        row = iota(shape, 0)
        take_high = jnp.where(row == 0, at_high, 0) == 1
        take_low = jnp.where(row == 7, at_low, 0) == 1
        upper = row < 4

        def ends(p):
            high, low = self.field[p, x : x + 8, :], self.field[p, x + 8 :, :]
            self.field[p, x : x + 8, :] = jnp.where(take_high, roll(self.field[p, x - 8 : x, :], 1, 0), high)
            self.field[p, x + 8 :, :] = jnp.where(take_low, roll(self.field[p, 0:8, :], 7, 0), low)

        if self.wide:
            loop(start, stop, ends, 4)
            return

        def body(p):
            tile = jnp.where(upper, self.right[p], self.left[p])
            tile = jnp.where(take_high, roll(self.field[p, x - 8 : x, :], 1, 0), tile)
            self.field[p, x:, :] = jnp.where(take_low, roll(self.field[p, 0:8, :], 7, 0), tile)

        loop(start, stop, body, 4)

    def sent(self, idle):
        whole = idle.at[pl.ds(0, self.tiles)]
        pltpu.make_async_copy(whole, whole, self.send.at[0]).wait()


class Level:
    def __init__(self, number, lanes, refs, gx, gy, counts):
        self.scale = 0.25**number
        self.lanes = lanes
        self.gx, self.gy = gx, gy
        self.count_x, self.count_y = counts
        (self.k, self.b, self.xh, self.x1, self.x2, self.wx, self.wy, self.wz, self.w, self.inv, self.z0, self.z1) = refs
        self.h = self.k.halo
        self.n = self.k.planes
        self.x = self.k.rows
        self.shape = self.k.field.shape[1:]
        self.period = lanes
        self.unroll = 2 if number == 0 else 4

    def merge_k(self, start, stop):
        at_low = jnp.where(self.gx == 0, 1, 0)
        at_high = jnp.where(self.gx == self.count_x - 1, 1, 0)
        self.k.merge_mended(start, stop, at_low, at_high)

    def row_ok(self):
        row = iota(self.shape, 0)
        below = jnp.where(self.gx == 0, 1, 0)
        above = jnp.where(self.gx == self.count_x - 1, 1, 0)
        middle = (self.x + self.shape[0]) // 2
        bad_low = jnp.where(row >= middle, below, 0)
        bad_high = jnp.where((row >= self.x) & (row < middle), above, 0)
        return (bad_low + bad_high) == 0

    def plane_ok(self, p):
        y = self.gy * self.n + p - self.h
        return (y >= 0) & (y < self.count_y * self.n)

    def mend_planes(self):
        field, h, n = self.k.field, self.h, self.n

        @pl.when(self.gy == 0)
        def _():
            field[h - 1] = field[h]

        @pl.when(self.gy == self.count_y - 1)
        def _():
            field[h + n] = field[h + n - 1]

    def lane(self):
        return iota(self.shape, 1) % self.period

    def faces(self, start, stop):
        k = self.k.field

        def body(p):
            own = k[p]
            self.wx[p] = harmonic(own, roll(own, -1, 0))
            along = harmonic(own, roll(own, -1, 1))
            self.wz[p] = jnp.where(self.lane() == self.period - 1, 0.0, along)

        loop(start, stop, body, self.unroll)

    def faces_inside(self):
        k, h, n, x = self.k.field, self.h, self.n, self.x
        last = self.lane()[0:x] == self.period - 1

        def body(p):
            own = k[p, 0:x, :]
            self.wx[p, 0:x, :] = harmonic(own, roll(own, -1, 0))
            self.wz[p, 0:x, :] = jnp.where(last, 0.0, harmonic(own, roll(own, -1, 1)))

        def along(p):
            self.wy[p, 0:x, :] = harmonic(k[p, 0:x, :], k[p + 1, 0:x, :])

        loop(h, h + n, body, self.unroll)
        loop(h, h + n - 1, along, self.unroll)

    def faces_edge(self):
        k, h, n, x = self.k.field, self.h, self.n, self.x
        last = self.lane()[0:8] == self.period - 1
        inner = iota((8, self.shape[1]), 0) < 7
        after = lambda own, following: jnp.where(inner, roll(own, -1, 0), roll(following, -1, 0))

        def body(p):
            first, end, halo = k[p, 0:8, :], k[p, x - 8 : x, :], k[p, x:, :]
            self.wx[p, x - 8 : x, :] = harmonic(end, after(end, halo))
            self.wx[p, x:, :] = harmonic(halo, after(halo, first))
            self.wz[p, x:, :] = jnp.where(last, 0.0, harmonic(halo, roll(halo, -1, 1)))

        def along(p):
            self.wy[p, x:, :] = harmonic(k[p, x:, :], k[p + 1, x:, :])

        loop(h, h + n, body, 4)
        loop(h, h + n - 1, along, 4)

    def faces_y(self, start, stop):
        k = self.k.field

        def body(p):
            self.wy[p] = harmonic(k[p], k[p + 1])

        loop(start, stop, body, self.unroll)

    def totals(self, start, stop):
        k = self.k.field
        rows_ok = self.row_ok()

        def body(p):
            wx, wz = self.wx[p], self.wz[p]
            lane = self.lane()
            edge = jnp.where((lane == 0) | (lane == self.period - 1), k[p], 0.0)
            total = wx + roll(wx, 1, 0) + self.wy[p] + self.wy[p - 1] + wz + roll(wz, 1, 1) + edge
            self.w[p] = total
            ok = rows_ok & self.plane_ok(p)
            self.inv[p] = jnp.where(ok, 1.0 / total, 0.0)

        loop(start, stop, body, self.unroll)

    def beside(self, field, p):
        own, wx, wz = field[p], self.wx[p], self.wz[p]
        found = wx * roll(own, -1, 0) + roll(wx * own, 1, 0)
        found = found + self.wy[p] * field[p + 1] + self.wy[p - 1] * field[p - 1]
        return found + wz * roll(own, -1, 1) + roll(wz * own, 1, 1)

    def first(self, start, stop):
        def body(p):
            self.x1[p] = self.b[p] * self.inv[p] * (1.0 / (THETA * self.scale))

        loop(start, stop, body, self.unroll)

    def second(self, margin):
        h, n, x = self.h, self.n, self.x

        def value(p):
            own = self.x1[p]
            factor = 1.0 + MOMENTUM + STEP * (THETA - 1.0)
            return factor * own + STEP * (self.inv[p] * self.beside(self.x1, p))

        def plain(p):
            self.x2[p] = value(p)

        def kept(p):
            found = value(p)
            self.x2[p] = found
            if self.lanes < 128:
                first = iota(found.shape, 1) < self.lanes
                found = jnp.where(first, found, self.x1[p])
            self.xh.field[p, 0:x, :] = found[0:x, :]

        if self.xh is None:
            loop(h - margin, h + n + margin, plain, self.unroll)
            return
        loop(h, h + n, kept, self.unroll)
        for p in list(range(h - margin, h)) + list(range(h + n, h + n + margin)):
            plain(p) if self.xh.skip == 0 else kept(p)

    def residual(self, field, p):
        return self.b[p] - self.scale * (self.w[p] * field[p] - self.beside(field, p))

    def correct(self, p, grown):
        ok = self.rows_ok & self.plane_ok(p)
        base = self.x2[p] if self.xh is None or self.lanes < 128 else self.xh.field[p]
        self.z0[p] = jnp.where(ok, base + grown, 0.0)

    def third(self, start, stop):
        def body(p):
            own = self.z0[p]
            flow = self.inv[p] * self.beside(self.z0, p)
            self.z1[p] = (1.0 - 1.0 / THETA) * own + self.x1[p] + (1.0 / THETA) * flow

        loop(start, stop, body, self.unroll)

    def fourth(self, start, stop, target):
        def body(p):
            own = self.z1[p]
            flow = self.inv[p] * self.beside(self.z1, p)
            found = (1.0 + MOMENTUM - STEP) * own - MOMENTUM * self.z0[p]
            target[p] = found + (STEP * THETA) * self.x1[p] + STEP * flow

        loop(start, stop, body, self.unroll)


LOW, HIGH = 8, 16


class Whole:
    def __init__(self, refs):
        self.scale = 0.25**3
        self.size_z = 32
        self.k, self.b, self.x1, self.x2, self.wx, self.wy, self.wz, self.w, self.inv = refs
        self.count = self.k.shape[0] - 2
        self.rows = self.k.shape[1] - LOW - HIGH
        self.shape = (self.rows, 128)

    def blank(self):
        for ref in (self.k, self.x1, self.x2, self.wx, self.wy, self.wz, self.inv):
            empty = jnp.zeros(ref.shape[1:], F32)
            ref[0] = empty
            ref[self.count + 1] = empty

            def body(g, ref=ref):
                ref[g, 0:LOW, :] = jnp.zeros((LOW, 128), F32)
                ref[g, LOW + self.rows :, :] = jnp.zeros((HIGH, 128), F32)

            loop(1, self.count + 1, body, 4)

    def at(self, ref, g):
        return ref[g, LOW : LOW + self.rows, :]

    def after(self, own, following):
        inner = iota(own.shape, 1) < 128 - self.size_z
        return jnp.where(inner, roll(own, -self.size_z, 1), roll(following, -self.size_z, 1))

    def before(self, own, previous):
        inner = iota(own.shape, 1) >= self.size_z
        return jnp.where(inner, roll(own, self.size_z, 1), roll(previous, self.size_z, 1))

    def weights(self):
        rows, inside = self.rows, slice(LOW, LOW + self.rows)

        def faces(g):
            own, following = self.at(self.k, g), self.at(self.k, g + 1)
            lane, row = iota(self.shape, 1), iota(self.shape, 0)
            end = jnp.where(lane >= 128 - self.size_z, jnp.where(g == self.count, 1, 0), 0)
            self.wx[g, inside, :] = jnp.where(end == 1, 0.0, harmonic(own, self.after(own, following)))
            self.wy[g, inside, :] = jnp.where(row == rows - 1, 0.0, harmonic(own, roll(own, -1, 0)))
            last = lane % self.size_z == self.size_z - 1
            self.wz[g, inside, :] = jnp.where(last, 0.0, harmonic(own, roll(own, -1, 1)))

        loop(1, self.count + 1, faces, 2)

        def totals(g):
            lane, row = iota(self.shape, 1), iota(self.shape, 0)
            high = jnp.where(lane >= 128 - self.size_z, jnp.where(g == self.count, 1.0, 0.0), 0.0)
            low = jnp.where(lane < self.size_z, jnp.where(g == 1, 1.0, 0.0), 0.0)
            edge = high + low
            edge = edge + jnp.where((row == 0) | (row == rows - 1), 1.0, 0.0)
            z = lane % self.size_z
            edge = edge + jnp.where((z == 0) | (z == self.size_z - 1), 1.0, 0.0)
            wx, wy, wz = self.at(self.wx, g), self.at(self.wy, g), self.at(self.wz, g)
            total = wx + self.before(wx, self.at(self.wx, g - 1)) + wy + roll(wy, 1, 0) + wz + roll(wz, 1, 1)
            total = total + edge * self.at(self.k, g)
            self.w[g, inside, :] = total
            self.inv[g, inside, :] = 1.0 / total

        loop(1, self.count + 1, totals, 2)

    def flow(self, fields, weights):
        previous, own, following = fields
        wx_previous, wx, wy, wz = weights
        found = wx * self.after(own, following) + self.before(wx * own, wx_previous * previous)
        found = found + wy * roll(own, -1, 0) + roll(wy * own, 1, 0)
        return found + wz * roll(own, -1, 1) + roll(wz * own, 1, 1)

    def beside(self, field, g):
        fields = [self.at(field, g + step) for step in (-1, 0, 1)]
        weights = [self.at(self.wx, g - 1)] + [self.at(ref, g) for ref in (self.wx, self.wy, self.wz)]
        return self.flow(fields, weights)

    def down(self, left):
        inside = slice(LOW, LOW + self.rows)

        def first(g):
            found = self.at(self.b, g) * self.at(self.inv, g) * (1.0 / (THETA * self.scale))
            self.x1[g, inside, :] = found

        loop(1, self.count + 1, first, 8)

        def second(g):
            factor = 1.0 + MOMENTUM + STEP * (THETA - 1.0)
            moved = self.at(self.inv, g) * self.beside(self.x1, g)
            self.x2[g, inside, :] = factor * self.at(self.x1, g) + STEP * moved

        loop(1, self.count + 1, second, 8)

        def residual(g):
            applied = self.at(self.w, g) * self.at(self.x2, g) - self.beside(self.x2, g)
            left[g - 1] = self.at(self.b, g) - self.scale * applied

        loop(1, self.count + 1, residual, 8)

    def up(self, gx, start, grown, held, answer):
        span = pl.ds(start, 24)
        z0, z1 = held
        planes = (0, 1, 2)
        part = lambda ref, c: ref[gx + c, span, :]
        for c in planes:
            z0[c + 1] = part(self.x2, c) + grown[c, span, :]

        def flow(field, c):
            fields = [field[c + step] for step in (0, 1, 2)]
            before = self.wx[jnp.maximum(gx + c - 1, 0), span, :]
            return part(self.inv, c) * self.flow(fields, [before, part(self.wx, c), part(self.wy, c), part(self.wz, c)])

        for c in planes:
            z1[c + 1] = (1.0 - 1.0 / THETA) * z0[c + 1] + part(self.x1, c) + (1.0 / THETA) * flow(z0, c)
        for c in planes:
            found = (1.0 + MOMENTUM - STEP) * z1[c + 1] - MOMENTUM * z0[c + 1]
            answer[c] = found + (STEP * THETA) * part(self.x1, c) + STEP * flow(z1, c)


class Deepest:
    def __init__(self, count):
        self.count = count
        self.scale = 0.25**4
        shape = (8, 128)
        self.lane, self.row = iota(shape, 1), iota(shape, 0)
        self.low_x = (self.lane % 32) < 16
        self.zero = jnp.zeros(shape, F32)

    def next_x(self, tiles):
        back, ahead = [roll(t, -16, 1) for t in tiles], [roll(t, 16, 1) for t in tiles] + [self.zero]
        return [jnp.where(self.low_x, back[g], ahead[g + 1]) for g in range(self.count)]

    def last_x(self, tiles):
        back, ahead = [self.zero] + [roll(t, -16, 1) for t in tiles], [roll(t, 16, 1) for t in tiles]
        return [jnp.where(self.low_x, back[g], ahead[g]) for g in range(self.count)]

    def next_y(self, tiles):
        moved = [roll(t, -1, 0) for t in tiles]
        return [jnp.where(self.row < 7, t, roll(t, -32, 1)) for t in moved]

    def last_y(self, tiles):
        moved = [roll(t, 1, 0) for t in tiles]
        return [jnp.where(self.row > 0, t, roll(t, 32, 1)) for t in moved]

    def next_z(self, tiles):
        return [roll(t, -1, 1) for t in tiles]

    def last_z(self, tiles):
        return [roll(t, 1, 1) for t in tiles]

    def weights(self, k, weight_refs, inv_ref):
        lane, row, span = self.lane, self.row, range(self.count)
        z = lane % 16
        end_y = (row == 7) & (lane >= 96)
        edge = jnp.where((z == 0) | (z == 15), 1.0, 0.0)
        edge = edge + jnp.where(end_y | ((row == 0) & (lane < 32)), 1.0, 0.0)
        faces_x = [harmonic(a, b) for a, b in zip(k, self.next_x(k))]
        faces_x[-1] = jnp.where(self.low_x, faces_x[-1], 0.0)
        faces_y = [jnp.where(end_y, 0.0, harmonic(a, b)) for a, b in zip(k, self.next_y(k))]
        faces_z = [jnp.where(z == 15, 0.0, harmonic(a, b)) for a, b in zip(k, self.next_z(k))]
        sets = [faces_x, self.last_x(faces_x), faces_y, self.last_y(faces_y), faces_z, self.last_z(faces_z)]
        for g in span:
            total = edge * k[g]
            if g == 0:
                total = total + jnp.where(self.low_x, k[g], 0.0)
            if g == self.count - 1:
                total = total + jnp.where(self.low_x, 0.0, k[g])
            for one in sets:
                total = total + one[g]
            inv = 1.0 / total
            inv_ref[g] = inv
            for number, one in enumerate(sets):
                weight_refs[number, g] = one[g] * inv

    def solve(self, b, weight_refs, inv_ref):
        theta, pairs = coefficients(COARSE_LO, COARSE_HI, BOTTOM)
        span = range(self.count)
        scaled = [b[g] * inv_ref[g] * (1.0 / self.scale) for g in span]
        update = [t * (1.0 / theta) for t in scaled]
        found = update
        for momentum, step in pairs:
            shifted = [
                self.next_x(found),
                self.last_x(found),
                self.next_y(found),
                self.last_y(found),
                self.next_z(found),
                self.last_z(found),
            ]
            following = []
            for g in span:
                flow = weight_refs[0, g] * shifted[0][g]
                for number in range(1, 6):
                    flow = flow + weight_refs[number, g] * shifted[number][g]
                following.append(momentum * update[g] + step * ((scaled[g] - found[g]) + flow))
            update = following
            found = [a + d for a, d in zip(found, update)]
        return found


def shrink_lanes(lanes, kept):
    row, col = iota((max(lanes, 128), 128), 0), iota((max(lanes, 128), 128), 1)
    return jnp.where((row // 2 == col % kept) & (row < lanes), 0.125, 0.0).astype(jnp.bfloat16)


def grow_lanes(kept, lanes):
    row, col = iota((128, lanes), 0), iota((128, lanes), 1)
    period = 2 * kept
    return jnp.where((col % period) // 2 == row, 1.0, 0.0).astype(jnp.bfloat16)


def restrict(read, target, count, fine_plane, coarse_plane, rows, matrix, half, sums):
    kept = rows // 2
    parts = matrix.shape[0] // 128

    def body(j):
        pair = read(fine_plane + 2 * j) + read(fine_plane + 2 * j + 1)
        slot = j % 2
        for part in range(parts):
            half[slot, part, 0:rows, :] = pair[:, part * 128 : (part + 1) * 128]
        for part in range(parts):
            even = half[slot, part, pl.ds(0, kept, stride=2), :]
            odd = half[slot, part, pl.ds(1, kept, stride=2), :]
            sums[pl.ds(pl.multiple_of(j * kept, 8), kept), 128 * part : 128 * (part + 1)] = even + odd

    loop(0, count, body, 2)
    means = times(sums[0 : count * kept, 0 : 128 * parts], matrix[...])
    target[coarse_plane : coarse_plane + count, 0:kept, :] = means.reshape(count, kept, 128)


def grow(source, planes, rows, matrix, doubled):
    start, stop = planes
    count, parts = stop - start, matrix.shape[1] // 128
    wide = times(source[start:stop].reshape(count * rows, 128), matrix[...])
    for j in range(count):
        for part in range(parts):
            piece = wide[j * rows : (j + 1) * rows, 128 * part : 128 * (part + 1)]
            doubled[j, part, pl.ds(0, rows, stride=2), :] = piece
            doubled[j, part, pl.ds(1, rows, stride=2), :] = piece


def grown_plane(doubled, j, rows, parts):
    own = 2 * (rows - 16)
    upper = iota((8, 128), 0) < 4
    found = []
    for part in range(parts):
        tail = jnp.where(upper, doubled[j, part, own : own + 8, :], doubled[j, part, own + 24 : own + 32, :])
        found.append(jnp.concatenate([doubled[j, part, 0:own, :], tail], axis=0))
    return found[0] if parts == 1 else jnp.concatenate(found, axis=1)


def kernel(count_x, count_y, names, *refs):
    r = dict(zip(names, refs))
    gx, gy = lax.axis_index("gx"), lax.axis_index("gy")
    ring_x = 4
    ring_z = count_y // ring_x
    chip_x, chip_z = gy % ring_x, gy // ring_x

    def place(dx, dy):
        return ((gx + dx + count_x) % count_x, (gy + dy + count_y) % count_y)

    def along_x(d):
        return (gx, chip_z * ring_x + (chip_x + d) % ring_x)

    def along_z(d):
        return (gx, ((chip_z + d) % ring_z) * ring_x + chip_x)

    def along_gx(d):
        return ((gx + d) % count_x, gy)

    z_steps = [d for d in range(1, ring_z) if min(d, ring_z - d) <= 3]
    partners = [place(dx, dy) for dx, dy in STEPS]
    partners += [along_x(d) for d in range(1, ring_x)]
    partners += [along_z(d) for d in z_steps]
    partners += [along_gx(d) for d in range(1, count_x)]

    def halves(whole, staged, first, store):
        copies = []
        for part in range(2):
            wide = whole.at[:, pl.ds(128 * part, 128)]
            pair = (staged.at[part], wide) if store else (wide, staged.at[part])
            copies.append(pltpu.make_async_copy(*pair, r["load"].at[first + part]))
        return copies

    loads_k = halves(r["coefficient"], r["k_in"], 0, False)
    loads_b = halves(r["right_side"], r["b_in"], 2, False)
    for copy in loads_k + loads_b:
        copy.start()
    barrier = pltpu.get_barrier_semaphore()
    for partner in partners:
        pl.semaphore_signal(barrier, inc=1, device_id=partner, device_id_type=MESH)

    def exchange(name, number, halo, depth):
        tag = f"{name}{number}"
        if not depth:
            return None
        landing = (r[tag + "_l"], r[tag + "_r"]) if tag + "_l" in r else None
        corner = depth if number == 2 else depth - 1
        return Exchange(r[tag], landing, r[tag + "_send"], r[tag + "_recv"], halo, depth, corner, 1 if tag == "xh0" else 0)

    levels, sources = [], []
    for number, (lanes, halo, depth_k, depth_b, depth_x) in enumerate(SHAPES):
        sources.append(exchange("b", number, halo, depth_b))
        fields = [exchange("k", number, halo, depth_k), r[f"b{number}"], exchange("xh", number, halo, depth_x)]
        fields += [r[f"{name}{number}"] for name in LOCAL]
        levels.append(Level(number, lanes, fields, gx, gy, (count_x, count_y)))
    l0, l1, l2 = levels
    l3 = Whole([r[f"{name}3"] for name in WHOLE])
    l4 = Deepest(count_x)

    def turn(staged, target):
        for y in range(l0.n):
            for part in range(2):
                lanes = pl.ds(128 * part, 128)
                target[l0.h + y, 0 : l0.x, lanes] = staged[part, pl.ds(y, l0.x, stride=l0.n), :]

    square = (128, 128)
    row, col = iota(square, 0), iota(square, 1)
    same_x, same_z = (row // 32) // 2 == (col % 32) // 16, (row % 32) // 2 == col % 16
    back = ((row % 32) // 16 == (col // 32) // 2) & (row % 16 == (col % 32) // 2)
    one = lambda where, value: jnp.where(where, value, 0.0).astype(jnp.bfloat16)
    r["to_1"][...] = shrink_lanes(256, 128)
    r["to_2"][...] = shrink_lanes(128, 64)
    r["to_3"][...] = one((row < 64) & (row // 2 == col % 32), 0.125)
    r["to_4"][...] = one(same_x & same_z, 0.125)
    r["from_4"][...] = one(back, 1.0)
    r["from_3"][...] = one(row % 32 == (col % 64) // 2, 1.0)
    r["from_2"][...] = grow_lanes(64, 128)
    r["from_1"][...] = grow_lanes(128, 256)

    for copy in loads_k:
        copy.wait()
    turn(r["k_in"], r["k0"])
    pl.semaphore_wait(barrier, len(partners))
    l0.k.start(place)
    for copy in loads_b:
        copy.wait()
    turn(r["b_in"], r["b0"])
    sources[0].start(place)

    half, sums, doubled = r["half"], r["sums"], r["doubled"]
    k0, k1, k2 = r["k0"], r["k1"], r["k2"]
    to_1, to_2 = r["to_1"], r["to_2"]
    restrict(lambda p: k0[p, 0 : l0.x, :], k1, l1.n, l0.h, l1.h, l0.x, to_1, half, sums)
    l1.k.start(place)
    restrict(lambda p: k1[p, 0 : l1.x, :], k2, l2.n, l1.h, l2.h, l1.x, to_2, half, sums)

    def small_block(read):
        tile = (8, 128)
        mine = iota(tile, 1) // 32 == iota(tile, 0) // 2
        pairs = [read(l2.h + 2 * j) + read(l2.h + 2 * j + 1) for j in range(2)]
        means = times(jnp.concatenate(pairs, axis=0), r["to_3"][...])
        found = jnp.zeros(tile, F32)
        for j in range(2):
            spread = jnp.where(mine, means[8 * j : 8 * j + 8], 0.0)
            line = jnp.sum(spread, axis=0, keepdims=True)
            found = jnp.where(iota(tile, 0) == 2 * chip_x + j, jnp.broadcast_to(line, tile), found)
        return found

    class Gather:
        def __init__(self, name, target, eager):
            self.first, self.target, self.eager = r[name + "_first"], target, eager
            self.send, self.recv = r[name + "_send"], r[name + "_recv"]
            self.tiles_sent, self.tiles_last = 0, 0

        def go(self, sems, source, target, where, steps):
            copies = []
            for d in steps:
                copies.append(
                    pltpu.make_async_remote_copy(
                        src_ref=source,
                        dst_ref=target,
                        send_sem=self.send.at[0],
                        recv_sem=self.recv.at[sems(d)],
                        device_id=where(d),
                        device_id_type=MESH,
                    )
                )
            for copy in copies:
                copy.start()
            self.tiles_sent += len(copies) * (source.shape[0] // 8)
            return copies

        def along_x(self, tile):
            self.first[chip_x] = tile
            slot = self.first.at[chip_x]
            self.near = self.go(lambda d: d, slot, slot, along_x, range(1, ring_x))

        def part(self, d):
            rows = pl.ds(pl.multiple_of(8 * ((chip_z + ring_z - d) % ring_z) + LOW, 8), 8)
            return self.target.at[gx + 1, rows]

        def pass_on(self, part):
            self.go(lambda d: 0, part, part, along_gx, range(1, count_x))
            self.tiles_last += (count_x - 1) * (part.shape[0] // 8)

        def along_z(self):
            for copy in self.near:
                copy.wait_recv()
            found = self.first[0]
            for slot in range(1, ring_x):
                found = found + self.first[slot]
            tile = self.part(0)
            tile[...] = found
            self.far = self.go(lambda d: ring_x - 1 + d, tile, tile, along_z, z_steps)
            if self.eager:
                self.pass_on(tile)

        def along_gx(self):
            for d, copy in sorted(zip(z_steps, self.far), key=lambda pair: min(pair[0], ring_z - pair[0])):
                copy.wait_recv()
                if self.eager:
                    self.pass_on(self.part(d))
            if not self.eager:
                self.pass_on(self.target.at[gx + 1, pl.ds(LOW, 8 * ring_z)])

        def arrive(self):
            whole = r["idle"].at[pl.ds(0, self.tiles_last)]
            pltpu.make_async_copy(whole, whole, self.recv.at[0]).wait()

        def sent(self):
            whole = r["idle"].at[pl.ds(0, self.tiles_sent)]
            pltpu.make_async_copy(whole, whole, self.send.at[0]).wait()

    gather_k, gather_b = Gather("gk", l3.k, False), Gather("gb", l3.b, True)
    gather_k.along_x(small_block(lambda p: k2[p, 0 : l2.x, :]))
    l3.blank()
    for d in range(1, ring_z):
        if d not in z_steps:
            unused = pl.ds(pl.multiple_of(8 * ((chip_z + d) % ring_z) + LOW, 8), 8)
            l3.k[gx + 1, unused, :] = jnp.ones((8, 128), F32)
            for g in range(1, count_x + 1):
                l3.b[g, unused, :] = jnp.zeros((8, 128), F32)
    z0_3, z1_3 = r["z0_3"], r["z1_3"]
    for held in (z0_3, z1_3):
        held[0] = jnp.zeros((24, 128), F32)
        held[4] = jnp.zeros((24, 128), F32)
    grown3 = r["grown3"]
    for c in range(3):
        grown3[c, 0:LOW, :] = jnp.zeros((LOW, 128), F32)
        grown3[c, LOW + 8 * ring_z :, :] = jnp.zeros((HIGH, 128), F32)

    def ready(level, between=None):
        h, n, depth = level.h, level.n, level.k.depth
        if level.k.wide:
            level.k.arrive(ALONG_GX)
            level.merge_k(h, h + n)
            level.faces(h, h + n)
            level.faces_y(h, h + n - 1)
        else:
            level.faces_inside()
            level.k.arrive(ALONG_GX)
            level.merge_k(h, h + n)
            level.faces_edge()
        level.totals(h + 1, h + n - 1)
        if between is not None:
            between()
        level.k.arrive(ALONG_GY)
        low, high = h - depth + 1, h + n + depth - 1
        level.merge_k(h - level.k.corner, h)
        level.merge_k(h + n, h + n + level.k.corner)
        level.mend_planes()
        level.faces(low, h)
        level.faces(h + n, high)
        level.faces_y(h - depth, h)
        level.faces_y(h + n - 1, high)
        level.totals(low, h + 1)
        level.totals(h + n - 1, high)

    def descend(level, source, depth):
        h, n = level.h, level.n
        if source is not None:
            source.arrive(range(8))
            source.merge(h - depth + 1, h + n + depth - 1)
        level.first(h - depth, h + n + depth)
        level.second(depth - 1)

    def source_below(level, target, margin, rows, matrix):
        below = levels[levels.index(level) + 1]
        read = lambda p: level.residual(level.x2, p)[0:rows, :]
        count, fine = below.n + 2 * margin, level.h - 2 * margin
        restrict(read, target, count, fine, below.h - margin, rows, matrix, half, sums)

    ready(l0)
    descend(l0, sources[0], 2)
    source_below(l0, r["b1"], 0, l0.x, to_1)
    sources[1].start(place)
    gather_k.along_z()
    l2.k.start(place)
    ready(l1)
    sources[1].arrive(range(8))
    gather_k.along_gx()
    descend(l1, None, 6)
    source_below(l1, r["b2"], 2, l1.x + 16, to_2)
    ready(l2)
    descend(l2, None, 2)
    gather_b.along_x(small_block(lambda p: l2.residual(l2.x2, p)[0 : l2.x, :]))
    def to_bottom(source, low):
        kept = 4 * ring_z
        pieces = []
        for g in range(count_x):
            even = source[g, pl.ds(low, kept, stride=2), :]
            odd = source[g, pl.ds(low + 1, kept, stride=2), :]
            pieces.append(even + odd)
        means = times(jnp.concatenate(pieces, axis=0), r["to_4"][...])
        group = iota((8, 128), 1) // 32
        tiles = []
        for g in range(count_x):
            found = means[g * kept : g * kept + 8]
            for q in range(1, 4):
                found = jnp.where(group == q, means[g * kept + 8 * q : g * kept + 8 * q + 8], found)
            tiles.append(found)
        return tiles

    gather_k.arrive()
    l3.weights()
    gather_b.along_z()
    l4.weights(to_bottom(l3.k.at[pl.ds(1, count_x)], LOW), r["w4"], r["inv4"])
    gather_b.along_gx()
    l2.xh.start(place)
    l0.xh.start(place)
    for field in [level.k for level in levels] + sources[:2]:
        field.sent(r["idle"])
    gather_k.sent()
    gather_b.arrive()
    l3.down(r["left3"])
    deepest = l4.solve(to_bottom(r["left3"], 0), r["w4"], r["inv4"])
    tiles4 = r["tiles4"]
    tiles4[0] = l4.zero
    tiles4[count_x + 1] = l4.zero
    for g in range(count_x):
        tiles4[g + 1] = deepest[g]

    group = iota((8, 128), 1) // 32
    spread = [jnp.where(group == q, tiles4[gx + c], 0.0) for c in range(3) for q in range(4)]
    wide = times(jnp.concatenate(spread, axis=0), r["from_4"][...])
    for c in range(3):
        piece = wide[32 * c : 32 * c + 32]
        grown3[c, pl.ds(LOW, 32, stride=2), :] = piece
        grown3[c, pl.ds(LOW + 1, 32, stride=2), :] = piece
    start = 8 * ((2 * gy + 4) // 8)
    answer = r["answer"]
    l3.up(gx, pl.multiple_of(start, 8), grown3, (z0_3, z1_3), answer)

    l2.xh.arrive(range(8))
    l2.xh.merge(0, 2 * l2.h + l2.n)
    tile = (8, 128)
    own_group = iota(tile, 1) // 32 == iota(tile, 0) // 2
    first_half = iota(tile, 0) < 4
    spread = []
    for j in range(6):
        at = 6 + 2 * gy + j - start
        lower, own, upper = [jnp.broadcast_to(answer[c, pl.ds(at, 1), :], tile) for c in range(3)]
        spread.append(jnp.where(own_group, own, 0.0))
        spread.append(jnp.where(own_group, jnp.where(first_half, upper, lower), 0.0))
    wide = times(jnp.concatenate(spread, axis=0), r["from_3"][...])
    l2.rows_ok = l2.row_ok()
    low_lanes = iota(l2.shape, 1) < 64
    for p in range(12):
        both = l2.xh.field[p]
        turned = roll(both, 64, 1)
        l2.x1[p] = jnp.where(l2.rows_ok & l2.plane_ok(p), jnp.where(low_lanes, turned, both), 0.0)
        l2.x2[p] = jnp.where(low_lanes, both, turned)
        l2.correct(p, wide[16 * (p // 2) : 16 * (p // 2) + 16])
    l2.third(1, 11)
    l2.fourth(2, 10, r["z2"])

    grow(r["z2"], (2, 10), 16, r["from_2"], doubled)
    l1.rows_ok = l1.row_ok()

    def lift_1(j):
        grown = doubled[j, 0, 0 : l1.x + 16, :]
        l1.correct(l1.h - 4 + 2 * j, grown)
        l1.correct(l1.h - 3 + 2 * j, grown)

    loop(0, 8, lift_1, 2)
    l1.third(l1.h - 3, l1.h + l1.n + 3)
    l1.fourth(l1.h - 2, l1.h + l1.n + 2, r["z1out"])

    grow(r["z1out"], (l1.h - 2, l1.h + l1.n + 2), 32, r["from_1"], doubled)
    l0.xh.arrive(range(8))
    l0.xh.merge(l0.h - 2, l0.h + l0.n + 2)
    l0.rows_ok = l0.row_ok()
    l0.correct(0, grown_plane(doubled, 0, 32, 2))

    def lift_0(j):
        grown = grown_plane(doubled, j, 32, 2)
        l0.correct(2 * j - 1, grown)
        l0.correct(2 * j, grown)

    loop(1, 11, lift_0)
    l0.correct(21, grown_plane(doubled, 11, 32, 2))
    l0.third(1, 21)
    l0.fourth(2, 20, l0.x2)

    def turn_back(staged, y, value):
        for part in range(2):
            lanes = slice(128 * part, 128 * (part + 1))
            staged[part, pl.ds(y, l0.x, stride=l0.n), :] = value[0 : l0.x, lanes]

    loop(0, l0.n, lambda y: turn_back(r["k_in"], y, l0.x2[l0.h + y]), 4)
    stores = halves(r["solution"], r["k_in"], 4, True)
    for copy in stores:
        copy.start()
    loop(0, l0.n, lambda y: turn_back(r["b_in"], y, l0.residual(l0.x2, l0.h + y)), 2)
    for copy in halves(r["residual"], r["b_in"], 6, True):
        copy.start()
        stores.append(copy)
    gather_b.sent()
    l2.xh.sent(r["idle"])
    l0.xh.sent(r["idle"])
    for copy in stores:
        copy.wait()


SHAPES = ((256, 3, 3, 2, 3), (128, 7, 7, 6, 0), (64, 4, 4, 0, 4))
LOCAL = ("x1_", "x2_", "wx", "wy", "wz", "w", "inv", "z0_", "z1_")
WHOLE = ("k", "b", "x1_", "x2_", "wx", "wy", "wz", "w", "inv")


def per_device(count_x, count_y, right_side, coefficient):
    nx, ny, nz = right_side.shape
    vmem = lambda *shape: pltpu.VMEM(shape, F32)
    rows3 = 2 * count_y
    scratch = {
        "k_in": vmem(2, nx * ny, 128),
        "b_in": vmem(2, nx * ny, 128),
        "load": pltpu.SemaphoreType.DMA((8,)),
        "half": vmem(2, 2, nx, 128),
        "idle": vmem(256, 8, 128),
        "to_1": pltpu.VMEM((256, 128), jnp.bfloat16),
        "from_1": pltpu.VMEM((128, 256), jnp.bfloat16),
        "sums": vmem(nx * ny // 4, nz),
        "doubled": vmem(ny // 2 + 4, 2, nx + 32, 128),
        "z0_3": vmem(5, 24, 128),
        "z1_3": vmem(5, 24, 128),
        "left3": vmem(count_x, rows3, 128),
        "w4": vmem(6, count_x, 8, 128),
        "inv4": vmem(count_x, 8, 128),
        "tiles4": vmem(count_x + 2, 8, 128),
        "grown3": vmem(3, LOW + rows3 + HIGH, 128),
        "answer": vmem(3, 24, 128),
        "z2": vmem((ny >> 2) + 8, (nx >> 2) + 8, 128),
        "z1out": vmem((ny >> 1) + 14, (nx >> 1) + 16, 128),
    }
    for name in ("to_2", "to_3", "to_4", "from_4", "from_3", "from_2"):
        scratch[name] = pltpu.VMEM((128, 128), jnp.bfloat16)
    for number, (lanes, halo, *depths) in enumerate(SHAPES):
        rows, planes, width = nx >> number, ny >> number, max(128, lanes)
        wide = number == 1
        full = (planes + 2 * halo, rows + (16 if wide else 8), width)
        scratch[f"b{number}"] = vmem(*full)
        for name, depth in zip(("k", "b", "xh"), depths):
            if not depth:
                continue
            tag = f"{name}{number}"
            scratch[tag] = vmem(*full)
            if not wide:
                scratch[tag + "_l"] = vmem(full[0], 8, width)
                scratch[tag + "_r"] = vmem(full[0], 8, width)
            scratch[tag + "_send"] = pltpu.SemaphoreType.DMA((1,))
            scratch[tag + "_recv"] = pltpu.SemaphoreType.DMA((8,))
        for name in LOCAL:
            scratch[f"{name}{number}"] = vmem(*full)
    for name in WHOLE:
        scratch[f"{name}3"] = vmem(count_x + 2, LOW + rows3 + HIGH, 128)
    for name in ("gk", "gb"):
        scratch[name + "_first"] = vmem(4, 8, 128)
        scratch[name + "_send"] = pltpu.SemaphoreType.DMA((1,))
        scratch[name + "_recv"] = pltpu.SemaphoreType.DMA((4 + count_y // 4,))

    names = ["right_side", "coefficient", "solution", "residual"] + list(scratch)
    shape = jax.ShapeDtypeStruct((nx * ny, nz), F32)
    found = pl.pallas_call(
        functools.partial(kernel, count_x, count_y, names),
        out_shape=(shape, shape),
        in_specs=[pl.BlockSpec(memory_space=pl.ANY)] * 2,
        out_specs=(pl.BlockSpec(memory_space=pl.ANY),) * 2,
        scratch_shapes=list(scratch.values()),
        compiler_params=pltpu.CompilerParams(
            collective_id=0, has_side_effects=True, vmem_limit_bytes=56 << 20
        ),
        name="vcycle",
    )(right_side.reshape(nx * ny, nz), coefficient.reshape(nx * ny, nz))
    return tuple(value.reshape(nx, ny, nz) for value in found)


def solution(mesh):
    spec = P("gx", "gy", None)
    step = functools.partial(per_device, mesh.shape["gx"], mesh.shape["gy"])
    return jax.shard_map(step, mesh=mesh, in_specs=(spec, spec), out_specs=(spec, spec), check_vma=False)
```

```python
import functools

import jax
import jax.numpy as jnp
from jax import lax
from jax.experimental import pallas as pl
from jax.experimental.pallas import tpu as pltpu
from jax.sharding import PartitionSpec as P

MESH = pl.DeviceIdType.MESH
F32 = jnp.float32

SMOOTH_LO, SMOOTH_HI = 0.5, 2.0
COARSE_LO, COARSE_HI = 0.05, 2.0
BOTTOM = 8

STEPS = ((1, 1), (1, -1), (-1, 1), (-1, -1), (0, 1), (0, -1), (1, 0), (-1, 0))
ALONG_GX, ALONG_GY = (6, 7), (0, 1, 2, 3, 4, 5)


def coefficients(low, high, sweeps):
    theta = (high + low) / 2.0
    delta = (high - low) / 2.0
    sigma = theta / delta
    rho = 1.0 / sigma
    pairs = []
    for _ in range(sweeps - 1):
        rho_next = 1.0 / (2.0 * sigma - rho)
        pairs.append((rho_next * rho, 2.0 * rho_next / delta))
        rho = rho_next
    return theta, pairs


THETA, ((MOMENTUM, STEP),) = coefficients(SMOOTH_LO, SMOOTH_HI, 2)


def harmonic(own, other):
    return 2.0 * own * other / (own + other)


def roll(value, shift, axis):
    size = value.shape[axis]
    return pltpu.roll(value, shift % size, axis)


def iota(shape, dim):
    return lax.broadcasted_iota(jnp.int32, shape, dim)


def times(rows, matrix):
    high = rows.astype(jnp.bfloat16)
    rest = rows - high.astype(F32)
    middle = rest.astype(jnp.bfloat16)
    low = (rest - middle.astype(F32)).astype(jnp.bfloat16)
    found = [jnp.dot(term, matrix, preferred_element_type=F32) for term in (low, middle, high)]
    return (found[0] + found[1]) + found[2]


def loop(start, stop, body, unroll=1):
    count = (stop - start) // unroll

    def step(index, carry):
        for k in range(unroll):
            body(start + index * unroll + k)
        return carry

    if count > 1:
        lax.fori_loop(0, count, step, 0)
        start += count * unroll
    for index in range(start, stop):
        body(index)


class Exchange:
    def __init__(self, field, landing, send, recv, halo, depth, corner, skip=0):
        self.skip = skip
        self.field, self.wide = field, landing is None
        self.left, self.right = (None, None) if self.wide else landing
        self.send, self.recv = send, recv
        self.halo, self.depth, self.corner = halo, depth, corner
        self.planes = field.shape[0] - 2 * halo
        self.rows = field.shape[1] - (16 if self.wide else 8)

    def copies(self, place):
        h, n, r, x = self.halo, self.planes, self.depth, self.rows
        found, self.tiles = [], 0
        for number, (dx, dy) in enumerate(STEPS):
            if dx == 0:
                count, skip = r - self.skip, self.skip
                source_plane = h + n - r if dy > 0 else h + skip
                target_plane = h - r if dy > 0 else h + n + skip
                source = self.field.at[pl.ds(source_plane, count), pl.ds(0, x)]
                target = self.field.at[pl.ds(target_plane, count), pl.ds(0, x)]
            else:
                count = n if dy == 0 else self.corner
                source_plane = h if dy <= 0 else h + n - count
                target_plane = h if dy == 0 else (h - count if dy > 0 else h + n)
                source = self.field.at[pl.ds(source_plane, count), pl.ds(x - 8 if dx > 0 else 0, 8)]
                if self.wide:
                    target = self.field.at[pl.ds(target_plane, count), pl.ds(x + 8 if dx > 0 else x, 8)]
                else:
                    landing = self.left if dx > 0 else self.right
                    target = landing.at[pl.ds(target_plane, count)]
            self.tiles += source.shape[0] * source.shape[1] * source.shape[2] // 1024
            found.append(
                pltpu.make_async_remote_copy(
                    src_ref=source,
                    dst_ref=target,
                    send_sem=self.send.at[0],
                    recv_sem=self.recv.at[number],
                    device_id=place(dx, dy),
                    device_id_type=MESH,
                )
            )
        return found

    def start(self, place):
        self.started = self.copies(place)
        for copy in self.started:
            copy.start()

    def arrive(self, which):
        for number in which:
            self.started[number].wait_recv()

    def merge(self, start, stop):
        if self.wide:
            return
        x = self.rows
        shape = (8, self.field.shape[2])

        def body(p):
            upper = iota(shape, 0) < 4
            self.field[p, x:, :] = jnp.where(upper, self.right[p], self.left[p])

        loop(start, stop, body, 4)

    def merge_mended(self, start, stop, at_low, at_high):
        x = self.rows
        shape = (8, self.field.shape[2])
        row = iota(shape, 0)
        take_high = jnp.where(row == 0, at_high, 0) == 1
        take_low = jnp.where(row == 7, at_low, 0) == 1
        upper = row < 4

        def ends(p):
            high, low = self.field[p, x : x + 8, :], self.field[p, x + 8 :, :]
            self.field[p, x : x + 8, :] = jnp.where(take_high, roll(self.field[p, x - 8 : x, :], 1, 0), high)
            self.field[p, x + 8 :, :] = jnp.where(take_low, roll(self.field[p, 0:8, :], 7, 0), low)

        if self.wide:
            loop(start, stop, ends, 4)
            return

        def body(p):
            tile = jnp.where(upper, self.right[p], self.left[p])
            tile = jnp.where(take_high, roll(self.field[p, x - 8 : x, :], 1, 0), tile)
            self.field[p, x:, :] = jnp.where(take_low, roll(self.field[p, 0:8, :], 7, 0), tile)

        loop(start, stop, body, 4)

    def sent(self, idle):
        whole = idle.at[pl.ds(0, self.tiles)]
        pltpu.make_async_copy(whole, whole, self.send.at[0]).wait()


class Level:
    def __init__(self, number, lanes, refs, gx, gy, counts):
        self.scale = 0.25**number
        self.lanes = lanes
        self.gx, self.gy = gx, gy
        self.count_x, self.count_y = counts
        (self.k, self.b, self.xh, self.x1, self.x2, self.wx, self.wy, self.wz, self.w, self.inv, self.z0, self.z1) = refs
        self.h = self.k.halo
        self.n = self.k.planes
        self.x = self.k.rows
        self.shape = self.k.field.shape[1:]
        self.period = lanes
        self.unroll = 2 if number == 0 else 8

    def merge_k(self, start, stop):
        at_low = jnp.where(self.gx == 0, 1, 0)
        at_high = jnp.where(self.gx == self.count_x - 1, 1, 0)
        self.k.merge_mended(start, stop, at_low, at_high)

    def row_ok(self):
        row = iota(self.shape, 0)
        below = jnp.where(self.gx == 0, 1, 0)
        above = jnp.where(self.gx == self.count_x - 1, 1, 0)
        middle = (self.x + self.shape[0]) // 2
        bad_low = jnp.where(row >= middle, below, 0)
        bad_high = jnp.where((row >= self.x) & (row < middle), above, 0)
        return (bad_low + bad_high) == 0

    def plane_ok(self, p):
        y = self.gy * self.n + p - self.h
        return (y >= 0) & (y < self.count_y * self.n)

    def mend_planes(self):
        field, h, n = self.k.field, self.h, self.n

        @pl.when(self.gy == 0)
        def _():
            field[h - 1] = field[h]

        @pl.when(self.gy == self.count_y - 1)
        def _():
            field[h + n] = field[h + n - 1]

    def lane(self):
        return iota(self.shape, 1) % self.period

    def faces(self, start, stop):
        k = self.k.field

        def body(p):
            own = k[p]
            self.wx[p] = harmonic(own, roll(own, -1, 0))
            along = harmonic(own, roll(own, -1, 1))
            self.wz[p] = jnp.where(self.lane() == self.period - 1, 0.0, along)

        loop(start, stop, body, self.unroll)

    def faces_inside(self):
        k, h, n, x = self.k.field, self.h, self.n, self.x
        last = self.lane()[0:x] == self.period - 1

        def body(p):
            own = k[p, 0:x, :]
            self.wx[p, 0:x, :] = harmonic(own, roll(own, -1, 0))
            self.wz[p, 0:x, :] = jnp.where(last, 0.0, harmonic(own, roll(own, -1, 1)))

        def along(p):
            self.wy[p, 0:x, :] = harmonic(k[p, 0:x, :], k[p + 1, 0:x, :])

        loop(h, h + n, body, self.unroll)
        loop(h, h + n - 1, along, self.unroll)

    def faces_edge(self):
        k, h, n, x = self.k.field, self.h, self.n, self.x
        last = self.lane()[0:8] == self.period - 1
        inner = iota((8, self.shape[1]), 0) < 7
        after = lambda own, following: jnp.where(inner, roll(own, -1, 0), roll(following, -1, 0))

        def body(p):
            first, end, halo = k[p, 0:8, :], k[p, x - 8 : x, :], k[p, x:, :]
            self.wx[p, x - 8 : x, :] = harmonic(end, after(end, halo))
            self.wx[p, x:, :] = harmonic(halo, after(halo, first))
            self.wz[p, x:, :] = jnp.where(last, 0.0, harmonic(halo, roll(halo, -1, 1)))

        def along(p):
            self.wy[p, x:, :] = harmonic(k[p, x:, :], k[p + 1, x:, :])

        loop(h, h + n, body, 4)
        loop(h, h + n - 1, along, 4)

    def faces_y(self, start, stop):
        k = self.k.field

        def body(p):
            self.wy[p] = harmonic(k[p], k[p + 1])

        loop(start, stop, body, self.unroll)

    def totals(self, start, stop):
        k = self.k.field
        rows_ok = self.row_ok()

        def body(p):
            wx, wz = self.wx[p], self.wz[p]
            lane = self.lane()
            edge = jnp.where((lane == 0) | (lane == self.period - 1), k[p], 0.0)
            total = wx + roll(wx, 1, 0) + self.wy[p] + self.wy[p - 1] + wz + roll(wz, 1, 1) + edge
            self.w[p] = total
            ok = rows_ok & self.plane_ok(p)
            self.inv[p] = jnp.where(ok, 1.0 / total, 0.0)

        loop(start, stop, body, self.unroll)

    def beside(self, field, p):
        own, wx, wz = field[p], self.wx[p], self.wz[p]
        found = wx * roll(own, -1, 0) + roll(wx * own, 1, 0)
        found = found + self.wy[p] * field[p + 1] + self.wy[p - 1] * field[p - 1]
        return found + wz * roll(own, -1, 1) + roll(wz * own, 1, 1)

    def first(self, start, stop):
        def body(p):
            self.x1[p] = self.b[p] * self.inv[p] * (1.0 / (THETA * self.scale))

        loop(start, stop, body, self.unroll)

    def second(self, margin):
        h, n, x = self.h, self.n, self.x

        def value(p):
            own = self.x1[p]
            factor = 1.0 + MOMENTUM + STEP * (THETA - 1.0)
            return factor * own + STEP * (self.inv[p] * self.beside(self.x1, p))

        def plain(p):
            self.x2[p] = value(p)

        def kept(p):
            found = value(p)
            self.x2[p] = found
            if self.lanes < 128:
                first = iota(found.shape, 1) < self.lanes
                found = jnp.where(first, found, self.x1[p])
            self.xh.field[p, 0:x, :] = found[0:x, :]

        if self.xh is None:
            loop(h - margin, h + n + margin, plain, self.unroll)
            return
        loop(h, h + n, kept, self.unroll)
        for p in list(range(h - margin, h)) + list(range(h + n, h + n + margin)):
            plain(p) if self.xh.skip == 0 else kept(p)

    def residual(self, field, p):
        return self.b[p] - self.scale * (self.w[p] * field[p] - self.beside(field, p))

    def correct(self, p, grown):
        ok = self.rows_ok & self.plane_ok(p)
        base = self.x2[p] if self.xh is None or self.lanes < 128 else self.xh.field[p]
        self.z0[p] = jnp.where(ok, base + grown, 0.0)

    def third(self, start, stop):
        def body(p):
            own = self.z0[p]
            flow = self.inv[p] * self.beside(self.z0, p)
            self.z1[p] = (1.0 - 1.0 / THETA) * own + self.x1[p] + (1.0 / THETA) * flow

        loop(start, stop, body, self.unroll)

    def fourth(self, start, stop, target):
        def body(p):
            own = self.z1[p]
            flow = self.inv[p] * self.beside(self.z1, p)
            found = (1.0 + MOMENTUM - STEP) * own - MOMENTUM * self.z0[p]
            target[p] = found + (STEP * THETA) * self.x1[p] + STEP * flow

        loop(start, stop, body, self.unroll)


LOW, HIGH = 8, 16


class Whole:
    def __init__(self, refs):
        self.scale = 0.25**3
        self.size_z = 32
        self.k, self.b, self.x1, self.x2, self.wx, self.wy, self.wz, self.w, self.inv = refs
        self.count = self.k.shape[0] - 2
        self.rows = self.k.shape[1] - LOW - HIGH
        self.shape = (self.rows, 128)

    def blank(self):
        for ref in (self.k, self.x1, self.x2, self.wx, self.wy, self.wz, self.inv):
            empty = jnp.zeros(ref.shape[1:], F32)
            ref[0] = empty
            ref[self.count + 1] = empty

            def body(g, ref=ref):
                ref[g, 0:LOW, :] = jnp.zeros((LOW, 128), F32)
                ref[g, LOW + self.rows :, :] = jnp.zeros((HIGH, 128), F32)

            loop(1, self.count + 1, body, 4)

    def at(self, ref, g):
        return ref[g, LOW : LOW + self.rows, :]

    def after(self, own, following):
        inner = iota(own.shape, 1) < 128 - self.size_z
        return jnp.where(inner, roll(own, -self.size_z, 1), roll(following, -self.size_z, 1))

    def before(self, own, previous):
        inner = iota(own.shape, 1) >= self.size_z
        return jnp.where(inner, roll(own, self.size_z, 1), roll(previous, self.size_z, 1))

    def weights(self):
        rows, inside = self.rows, slice(LOW, LOW + self.rows)

        def faces(g):
            own, following = self.at(self.k, g), self.at(self.k, g + 1)
            lane, row = iota(self.shape, 1), iota(self.shape, 0)
            end = jnp.where(lane >= 128 - self.size_z, jnp.where(g == self.count, 1, 0), 0)
            self.wx[g, inside, :] = jnp.where(end == 1, 0.0, harmonic(own, self.after(own, following)))
            self.wy[g, inside, :] = jnp.where(row == rows - 1, 0.0, harmonic(own, roll(own, -1, 0)))
            last = lane % self.size_z == self.size_z - 1
            self.wz[g, inside, :] = jnp.where(last, 0.0, harmonic(own, roll(own, -1, 1)))

        loop(1, self.count + 1, faces, 2)

        def totals(g):
            lane, row = iota(self.shape, 1), iota(self.shape, 0)
            high = jnp.where(lane >= 128 - self.size_z, jnp.where(g == self.count, 1.0, 0.0), 0.0)
            low = jnp.where(lane < self.size_z, jnp.where(g == 1, 1.0, 0.0), 0.0)
            edge = high + low
            edge = edge + jnp.where((row == 0) | (row == rows - 1), 1.0, 0.0)
            z = lane % self.size_z
            edge = edge + jnp.where((z == 0) | (z == self.size_z - 1), 1.0, 0.0)
            wx, wy, wz = self.at(self.wx, g), self.at(self.wy, g), self.at(self.wz, g)
            total = wx + self.before(wx, self.at(self.wx, g - 1)) + wy + roll(wy, 1, 0) + wz + roll(wz, 1, 1)
            total = total + edge * self.at(self.k, g)
            self.w[g, inside, :] = total
            self.inv[g, inside, :] = 1.0 / total

        loop(1, self.count + 1, totals, 2)

    def flow(self, fields, weights):
        previous, own, following = fields
        wx_previous, wx, wy, wz = weights
        found = wx * self.after(own, following) + self.before(wx * own, wx_previous * previous)
        found = found + wy * roll(own, -1, 0) + roll(wy * own, 1, 0)
        return found + wz * roll(own, -1, 1) + roll(wz * own, 1, 1)

    def beside(self, field, g):
        fields = [self.at(field, g + step) for step in (-1, 0, 1)]
        weights = [self.at(self.wx, g - 1)] + [self.at(ref, g) for ref in (self.wx, self.wy, self.wz)]
        return self.flow(fields, weights)

    def down(self, left):
        inside = slice(LOW, LOW + self.rows)

        def first(g):
            found = self.at(self.b, g) * self.at(self.inv, g) * (1.0 / (THETA * self.scale))
            self.x1[g, inside, :] = found

        loop(1, self.count + 1, first, 8)

        def second(g):
            factor = 1.0 + MOMENTUM + STEP * (THETA - 1.0)
            moved = self.at(self.inv, g) * self.beside(self.x1, g)
            self.x2[g, inside, :] = factor * self.at(self.x1, g) + STEP * moved

        loop(1, self.count + 1, second, 8)

        def residual(g):
            applied = self.at(self.w, g) * self.at(self.x2, g) - self.beside(self.x2, g)
            left[g - 1] = self.at(self.b, g) - self.scale * applied

        loop(1, self.count + 1, residual, 8)

    def up(self, gx, start, grown, held, answer):
        span = pl.ds(start, 24)
        z0, z1 = held
        planes = (0, 1, 2)
        part = lambda ref, c: ref[gx + c, span, :]
        for c in planes:
            z0[c + 1] = part(self.x2, c) + grown[c, span, :]

        def flow(field, c):
            fields = [field[c + step] for step in (0, 1, 2)]
            before = self.wx[jnp.maximum(gx + c - 1, 0), span, :]
            return part(self.inv, c) * self.flow(fields, [before, part(self.wx, c), part(self.wy, c), part(self.wz, c)])

        for c in planes:
            z1[c + 1] = (1.0 - 1.0 / THETA) * z0[c + 1] + part(self.x1, c) + (1.0 / THETA) * flow(z0, c)
        for c in planes:
            found = (1.0 + MOMENTUM - STEP) * z1[c + 1] - MOMENTUM * z0[c + 1]
            answer[c] = found + (STEP * THETA) * part(self.x1, c) + STEP * flow(z1, c)


class Deepest:
    def __init__(self, count):
        self.count = count
        self.scale = 0.25**4
        shape = (8, 128)
        self.lane, self.row = iota(shape, 1), iota(shape, 0)
        self.low_x = (self.lane % 32) < 16
        self.zero = jnp.zeros(shape, F32)

    def next_x(self, tiles):
        back, ahead = [roll(t, -16, 1) for t in tiles], [roll(t, 16, 1) for t in tiles] + [self.zero]
        return [jnp.where(self.low_x, back[g], ahead[g + 1]) for g in range(self.count)]

    def last_x(self, tiles):
        back, ahead = [self.zero] + [roll(t, -16, 1) for t in tiles], [roll(t, 16, 1) for t in tiles]
        return [jnp.where(self.low_x, back[g], ahead[g]) for g in range(self.count)]

    def next_y(self, tiles):
        moved = [roll(t, -1, 0) for t in tiles]
        return [jnp.where(self.row < 7, t, roll(t, -32, 1)) for t in moved]

    def last_y(self, tiles):
        moved = [roll(t, 1, 0) for t in tiles]
        return [jnp.where(self.row > 0, t, roll(t, 32, 1)) for t in moved]

    def next_z(self, tiles):
        return [roll(t, -1, 1) for t in tiles]

    def last_z(self, tiles):
        return [roll(t, 1, 1) for t in tiles]

    def weights(self, k, weight_refs, inv_ref):
        lane, row, span = self.lane, self.row, range(self.count)
        z = lane % 16
        end_y = (row == 7) & (lane >= 96)
        edge = jnp.where((z == 0) | (z == 15), 1.0, 0.0)
        edge = edge + jnp.where(end_y | ((row == 0) & (lane < 32)), 1.0, 0.0)
        faces_x = [harmonic(a, b) for a, b in zip(k, self.next_x(k))]
        faces_x[-1] = jnp.where(self.low_x, faces_x[-1], 0.0)
        faces_y = [jnp.where(end_y, 0.0, harmonic(a, b)) for a, b in zip(k, self.next_y(k))]
        faces_z = [jnp.where(z == 15, 0.0, harmonic(a, b)) for a, b in zip(k, self.next_z(k))]
        sets = [faces_x, self.last_x(faces_x), faces_y, self.last_y(faces_y), faces_z, self.last_z(faces_z)]
        for g in span:
            total = edge * k[g]
            if g == 0:
                total = total + jnp.where(self.low_x, k[g], 0.0)
            if g == self.count - 1:
                total = total + jnp.where(self.low_x, 0.0, k[g])
            for one in sets:
                total = total + one[g]
            inv = 1.0 / total
            inv_ref[g] = inv
            for number, one in enumerate(sets):
                weight_refs[number, g] = one[g] * inv

    def solve(self, b, weight_refs, inv_ref):
        theta, pairs = coefficients(COARSE_LO, COARSE_HI, BOTTOM)
        span = range(self.count)
        scaled = [b[g] * inv_ref[g] * (1.0 / self.scale) for g in span]
        update = [t * (1.0 / theta) for t in scaled]
        found = update
        for momentum, step in pairs:
            shifted = [
                self.next_x(found),
                self.last_x(found),
                self.next_y(found),
                self.last_y(found),
                self.next_z(found),
                self.last_z(found),
            ]
            following = []
            for g in span:
                flow = weight_refs[0, g] * shifted[0][g]
                for number in range(1, 6):
                    flow = flow + weight_refs[number, g] * shifted[number][g]
                following.append(momentum * update[g] + step * ((scaled[g] - found[g]) + flow))
            update = following
            found = [a + d for a, d in zip(found, update)]
        return found


def shrink_lanes(lanes, kept):
    row, col = iota((max(lanes, 128), 128), 0), iota((max(lanes, 128), 128), 1)
    return jnp.where((row // 2 == col % kept) & (row < lanes), 0.125, 0.0).astype(jnp.bfloat16)


def grow_lanes(kept, lanes):
    row, col = iota((128, lanes), 0), iota((128, lanes), 1)
    period = 2 * kept
    return jnp.where((col % period) // 2 == row, 1.0, 0.0).astype(jnp.bfloat16)


def restrict(read, target, count, fine_plane, coarse_plane, rows, matrix, half, sums):
    kept = rows // 2
    parts = matrix.shape[0] // 128

    def body(j):
        pair = read(fine_plane + 2 * j) + read(fine_plane + 2 * j + 1)
        slot = j % 2
        for part in range(parts):
            half[slot, part, 0:rows, :] = pair[:, part * 128 : (part + 1) * 128]
        for part in range(parts):
            even = half[slot, part, pl.ds(0, kept, stride=2), :]
            odd = half[slot, part, pl.ds(1, kept, stride=2), :]
            sums[pl.ds(pl.multiple_of(j * kept, 8), kept), 128 * part : 128 * (part + 1)] = even + odd

    loop(0, count, body, 2)
    means = times(sums[0 : count * kept, 0 : 128 * parts], matrix[...])
    target[coarse_plane : coarse_plane + count, 0:kept, :] = means.reshape(count, kept, 128)


def grow(source, planes, rows, matrix, doubled):
    start, stop = planes
    count, parts = stop - start, matrix.shape[1] // 128
    wide = times(source[start:stop].reshape(count * rows, 128), matrix[...])
    for j in range(count):
        for part in range(parts):
            piece = wide[j * rows : (j + 1) * rows, 128 * part : 128 * (part + 1)]
            doubled[j, part, pl.ds(0, rows, stride=2), :] = piece
            doubled[j, part, pl.ds(1, rows, stride=2), :] = piece


def grown_plane(doubled, j, rows, parts):
    own = 2 * (rows - 16)
    upper = iota((8, 128), 0) < 4
    found = []
    for part in range(parts):
        tail = jnp.where(upper, doubled[j, part, own : own + 8, :], doubled[j, part, own + 24 : own + 32, :])
        found.append(jnp.concatenate([doubled[j, part, 0:own, :], tail], axis=0))
    return found[0] if parts == 1 else jnp.concatenate(found, axis=1)


def kernel(count_x, count_y, names, *refs):
    r = dict(zip(names, refs))
    gx, gy = lax.axis_index("gx"), lax.axis_index("gy")
    ring_x = 4
    ring_z = count_y // ring_x
    chip_x, chip_z = gy % ring_x, gy // ring_x

    def place(dx, dy):
        return ((gx + dx + count_x) % count_x, (gy + dy + count_y) % count_y)

    def along_x(d):
        return (gx, chip_z * ring_x + (chip_x + d) % ring_x)

    def along_z(d):
        return (gx, ((chip_z + d) % ring_z) * ring_x + chip_x)

    def along_gx(d):
        return ((gx + d) % count_x, gy)

    z_steps = [d for d in range(1, ring_z) if min(d, ring_z - d) <= 3]
    partners = [place(dx, dy) for dx, dy in STEPS]
    partners += [along_x(d) for d in range(1, ring_x)]
    partners += [along_z(d) for d in z_steps]
    partners += [along_gx(d) for d in range(1, count_x)]

    def halves(whole, staged, first, store):
        copies = []
        for part in range(2):
            wide = whole.at[:, pl.ds(128 * part, 128)]
            pair = (staged.at[part], wide) if store else (wide, staged.at[part])
            copies.append(pltpu.make_async_copy(*pair, r["load"].at[first + part]))
        return copies

    loads_k = halves(r["coefficient"], r["k_in"], 0, False)
    loads_b = halves(r["right_side"], r["b_in"], 2, False)
    for copy in loads_k + loads_b:
        copy.start()
    barrier = pltpu.get_barrier_semaphore()
    for partner in partners:
        pl.semaphore_signal(barrier, inc=1, device_id=partner, device_id_type=MESH)

    def exchange(name, number, halo, depth):
        tag = f"{name}{number}"
        if not depth:
            return None
        landing = (r[tag + "_l"], r[tag + "_r"]) if tag + "_l" in r else None
        corner = depth if number == 2 else depth - 1
        return Exchange(r[tag], landing, r[tag + "_send"], r[tag + "_recv"], halo, depth, corner, 1 if tag == "xh0" else 0)

    levels, sources = [], []
    for number, (lanes, halo, depth_k, depth_b, depth_x) in enumerate(SHAPES):
        sources.append(exchange("b", number, halo, depth_b))
        fields = [exchange("k", number, halo, depth_k), r[f"b{number}"], exchange("xh", number, halo, depth_x)]
        fields += [r[f"{name}{number}"] for name in LOCAL]
        levels.append(Level(number, lanes, fields, gx, gy, (count_x, count_y)))
    l0, l1, l2 = levels
    l3 = Whole([r[f"{name}3"] for name in WHOLE])
    l4 = Deepest(count_x)

    def turn(staged, target):
        for y in range(l0.n):
            for part in range(2):
                lanes = pl.ds(128 * part, 128)
                target[l0.h + y, 0 : l0.x, lanes] = staged[part, pl.ds(y, l0.x, stride=l0.n), :]

    square = (128, 128)
    row, col = iota(square, 0), iota(square, 1)
    same_x, same_z = (row // 32) // 2 == (col % 32) // 16, (row % 32) // 2 == col % 16
    back = ((row % 32) // 16 == (col // 32) // 2) & (row % 16 == (col % 32) // 2)
    one = lambda where, value: jnp.where(where, value, 0.0).astype(jnp.bfloat16)
    r["to_1"][...] = shrink_lanes(256, 128)
    r["to_2"][...] = shrink_lanes(128, 64)
    r["to_3"][...] = one((row < 64) & (row // 2 == col % 32), 0.125)
    r["to_4"][...] = one(same_x & same_z, 0.125)
    r["from_4"][...] = one(back, 1.0)
    r["from_3"][...] = one(row % 32 == (col % 64) // 2, 1.0)
    r["from_2"][...] = grow_lanes(64, 128)
    r["from_1"][...] = grow_lanes(128, 256)

    for copy in loads_k:
        copy.wait()
    turn(r["k_in"], r["k0"])
    pl.semaphore_wait(barrier, len(partners))
    l0.k.start(place)
    for copy in loads_b:
        copy.wait()
    turn(r["b_in"], r["b0"])
    sources[0].start(place)

    half, sums, doubled = r["half"], r["sums"], r["doubled"]
    k0, k1, k2 = r["k0"], r["k1"], r["k2"]
    to_1, to_2 = r["to_1"], r["to_2"]
    restrict(lambda p: k0[p, 0 : l0.x, :], k1, l1.n, l0.h, l1.h, l0.x, to_1, half, sums)
    l1.k.start(place)
    restrict(lambda p: k1[p, 0 : l1.x, :], k2, l2.n, l1.h, l2.h, l1.x, to_2, half, sums)

    def small_block(read):
        tile = (8, 128)
        mine = iota(tile, 1) // 32 == iota(tile, 0) // 2
        pairs = [read(l2.h + 2 * j) + read(l2.h + 2 * j + 1) for j in range(2)]
        means = times(jnp.concatenate(pairs, axis=0), r["to_3"][...])
        found = jnp.zeros(tile, F32)
        for j in range(2):
            spread = jnp.where(mine, means[8 * j : 8 * j + 8], 0.0)
            line = jnp.sum(spread, axis=0, keepdims=True)
            found = jnp.where(iota(tile, 0) == 2 * chip_x + j, jnp.broadcast_to(line, tile), found)
        return found

    class Gather:
        def __init__(self, name, target, eager):
            self.first, self.target, self.eager = r[name + "_first"], target, eager
            self.send, self.recv = r[name + "_send"], r[name + "_recv"]
            self.tiles_sent, self.tiles_last = 0, 0

        def go(self, sems, source, target, where, steps):
            copies = []
            for d in steps:
                copies.append(
                    pltpu.make_async_remote_copy(
                        src_ref=source,
                        dst_ref=target,
                        send_sem=self.send.at[0],
                        recv_sem=self.recv.at[sems(d)],
                        device_id=where(d),
                        device_id_type=MESH,
                    )
                )
            for copy in copies:
                copy.start()
            self.tiles_sent += len(copies) * (source.shape[0] // 8)
            return copies

        def along_x(self, tile):
            self.first[chip_x] = tile
            slot = self.first.at[chip_x]
            self.near = self.go(lambda d: d, slot, slot, along_x, range(1, ring_x))

        def part(self, d):
            rows = pl.ds(pl.multiple_of(8 * ((chip_z + ring_z - d) % ring_z) + LOW, 8), 8)
            return self.target.at[gx + 1, rows]

        def pass_on(self, part):
            self.go(lambda d: 0, part, part, along_gx, range(1, count_x))
            self.tiles_last += (count_x - 1) * (part.shape[0] // 8)

        def along_z(self):
            for copy in self.near:
                copy.wait_recv()
            found = self.first[0]
            for slot in range(1, ring_x):
                found = found + self.first[slot]
            tile = self.part(0)
            tile[...] = found
            self.far = self.go(lambda d: ring_x - 1 + d, tile, tile, along_z, z_steps)
            if self.eager:
                self.pass_on(tile)

        def along_gx(self):
            for d, copy in sorted(zip(z_steps, self.far), key=lambda pair: min(pair[0], ring_z - pair[0])):
                copy.wait_recv()
                if self.eager:
                    self.pass_on(self.part(d))
            if not self.eager:
                self.pass_on(self.target.at[gx + 1, pl.ds(LOW, 8 * ring_z)])

        def arrive(self):
            whole = r["idle"].at[pl.ds(0, self.tiles_last)]
            pltpu.make_async_copy(whole, whole, self.recv.at[0]).wait()

        def sent(self):
            whole = r["idle"].at[pl.ds(0, self.tiles_sent)]
            pltpu.make_async_copy(whole, whole, self.send.at[0]).wait()

    gather_k, gather_b = Gather("gk", l3.k, False), Gather("gb", l3.b, True)
    gather_k.along_x(small_block(lambda p: k2[p, 0 : l2.x, :]))
    l3.blank()
    for d in range(1, ring_z):
        if d not in z_steps:
            unused = pl.ds(pl.multiple_of(8 * ((chip_z + d) % ring_z) + LOW, 8), 8)
            l3.k[gx + 1, unused, :] = jnp.ones((8, 128), F32)
            for g in range(1, count_x + 1):
                l3.b[g, unused, :] = jnp.zeros((8, 128), F32)
    z0_3, z1_3 = r["z0_3"], r["z1_3"]
    for held in (z0_3, z1_3):
        held[0] = jnp.zeros((24, 128), F32)
        held[4] = jnp.zeros((24, 128), F32)
    grown3 = r["grown3"]
    for c in range(3):
        grown3[c, 0:LOW, :] = jnp.zeros((LOW, 128), F32)
        grown3[c, LOW + 8 * ring_z :, :] = jnp.zeros((HIGH, 128), F32)

    def ready(level, between=None):
        h, n, depth = level.h, level.n, level.k.depth
        if level.k.wide:
            level.k.arrive(ALONG_GX)
            level.merge_k(h, h + n)
            level.faces(h, h + n)
            level.faces_y(h, h + n - 1)
        else:
            level.faces_inside()
            level.k.arrive(ALONG_GX)
            level.merge_k(h, h + n)
            level.faces_edge()
        level.totals(h + 1, h + n - 1)
        if between is not None:
            between()
        level.k.arrive(ALONG_GY)
        low, high = h - depth + 1, h + n + depth - 1
        level.merge_k(h - level.k.corner, h)
        level.merge_k(h + n, h + n + level.k.corner)
        level.mend_planes()
        level.faces(low, h)
        level.faces(h + n, high)
        level.faces_y(h - depth, h)
        level.faces_y(h + n - 1, high)
        level.totals(low, h + 1)
        level.totals(h + n - 1, high)

    def descend(level, source, depth):
        h, n = level.h, level.n
        if source is not None:
            source.arrive(range(8))
            source.merge(h - depth + 1, h + n + depth - 1)
        level.first(h - depth, h + n + depth)
        level.second(depth - 1)

    def source_below(level, target, margin, rows, matrix):
        below = levels[levels.index(level) + 1]
        read = lambda p: level.residual(level.x2, p)[0:rows, :]
        count, fine = below.n + 2 * margin, level.h - 2 * margin
        restrict(read, target, count, fine, below.h - margin, rows, matrix, half, sums)

    ready(l0)
    descend(l0, sources[0], 2)
    source_below(l0, r["b1"], 0, l0.x, to_1)
    sources[1].start(place)
    gather_k.along_z()
    l2.k.start(place)
    ready(l1)
    sources[1].arrive(range(8))
    gather_k.along_gx()
    descend(l1, None, 6)
    source_below(l1, r["b2"], 2, l1.x + 16, to_2)
    ready(l2)
    descend(l2, None, 2)
    gather_b.along_x(small_block(lambda p: l2.residual(l2.x2, p)[0 : l2.x, :]))
    def to_bottom(source, low):
        kept = 4 * ring_z
        pieces = []
        for g in range(count_x):
            even = source[g, pl.ds(low, kept, stride=2), :]
            odd = source[g, pl.ds(low + 1, kept, stride=2), :]
            pieces.append(even + odd)
        means = times(jnp.concatenate(pieces, axis=0), r["to_4"][...])
        group = iota((8, 128), 1) // 32
        tiles = []
        for g in range(count_x):
            found = means[g * kept : g * kept + 8]
            for q in range(1, 4):
                found = jnp.where(group == q, means[g * kept + 8 * q : g * kept + 8 * q + 8], found)
            tiles.append(found)
        return tiles

    gather_k.arrive()
    l3.weights()
    gather_b.along_z()
    l4.weights(to_bottom(l3.k.at[pl.ds(1, count_x)], LOW), r["w4"], r["inv4"])
    gather_b.along_gx()
    l2.xh.start(place)
    l0.xh.start(place)
    for field in [level.k for level in levels] + sources[:2]:
        field.sent(r["idle"])
    gather_k.sent()
    gather_b.arrive()
    l3.down(r["left3"])
    deepest = l4.solve(to_bottom(r["left3"], 0), r["w4"], r["inv4"])
    tiles4 = r["tiles4"]
    tiles4[0] = l4.zero
    tiles4[count_x + 1] = l4.zero
    for g in range(count_x):
        tiles4[g + 1] = deepest[g]

    group = iota((8, 128), 1) // 32
    spread = [jnp.where(group == q, tiles4[gx + c], 0.0) for c in range(3) for q in range(4)]
    wide = times(jnp.concatenate(spread, axis=0), r["from_4"][...])
    for c in range(3):
        piece = wide[32 * c : 32 * c + 32]
        grown3[c, pl.ds(LOW, 32, stride=2), :] = piece
        grown3[c, pl.ds(LOW + 1, 32, stride=2), :] = piece
    start = 8 * ((2 * gy + 4) // 8)
    answer = r["answer"]
    l3.up(gx, pl.multiple_of(start, 8), grown3, (z0_3, z1_3), answer)

    l2.xh.arrive(range(8))
    l2.xh.merge(0, 2 * l2.h + l2.n)
    tile = (8, 128)
    own_group = iota(tile, 1) // 32 == iota(tile, 0) // 2
    first_half = iota(tile, 0) < 4
    spread = []
    for j in range(6):
        at = 6 + 2 * gy + j - start
        lower, own, upper = [jnp.broadcast_to(answer[c, pl.ds(at, 1), :], tile) for c in range(3)]
        spread.append(jnp.where(own_group, own, 0.0))
        spread.append(jnp.where(own_group, jnp.where(first_half, upper, lower), 0.0))
    wide = times(jnp.concatenate(spread, axis=0), r["from_3"][...])
    l2.rows_ok = l2.row_ok()
    low_lanes = iota(l2.shape, 1) < 64
    for p in range(12):
        both = l2.xh.field[p]
        turned = roll(both, 64, 1)
        l2.x1[p] = jnp.where(l2.rows_ok & l2.plane_ok(p), jnp.where(low_lanes, turned, both), 0.0)
        l2.x2[p] = jnp.where(low_lanes, both, turned)
        l2.correct(p, wide[16 * (p // 2) : 16 * (p // 2) + 16])
    l2.third(1, 11)
    l2.fourth(2, 10, r["z2"])

    grow(r["z2"], (2, 10), 16, r["from_2"], doubled)
    l1.rows_ok = l1.row_ok()

    def lift_1(j):
        grown = doubled[j, 0, 0 : l1.x + 16, :]
        l1.correct(l1.h - 4 + 2 * j, grown)
        l1.correct(l1.h - 3 + 2 * j, grown)

    loop(0, 8, lift_1, 2)
    l1.third(l1.h - 3, l1.h + l1.n + 3)
    l1.fourth(l1.h - 2, l1.h + l1.n + 2, r["z1out"])

    grow(r["z1out"], (l1.h - 2, l1.h + l1.n + 2), 32, r["from_1"], doubled)
    l0.xh.arrive(range(8))
    l0.xh.merge(l0.h - 2, l0.h + l0.n + 2)
    l0.rows_ok = l0.row_ok()
    l0.correct(0, grown_plane(doubled, 0, 32, 2))

    def lift_0(j):
        grown = grown_plane(doubled, j, 32, 2)
        l0.correct(2 * j - 1, grown)
        l0.correct(2 * j, grown)

    loop(1, 11, lift_0)
    l0.correct(21, grown_plane(doubled, 11, 32, 2))
    l0.third(1, 21)
    l0.fourth(2, 20, l0.x2)

    def turn_back(staged, y, value):
        for part in range(2):
            lanes = slice(128 * part, 128 * (part + 1))
            staged[part, pl.ds(y, l0.x, stride=l0.n), :] = value[0 : l0.x, lanes]

    loop(0, l0.n, lambda y: turn_back(r["k_in"], y, l0.x2[l0.h + y]), 4)
    stores = halves(r["solution"], r["k_in"], 4, True)
    for copy in stores:
        copy.start()
    loop(0, l0.n, lambda y: turn_back(r["b_in"], y, l0.residual(l0.x2, l0.h + y)), 2)
    for copy in halves(r["residual"], r["b_in"], 6, True):
        copy.start()
        stores.append(copy)
    gather_b.sent()
    l2.xh.sent(r["idle"])
    l0.xh.sent(r["idle"])
    for copy in stores:
        copy.wait()


SHAPES = ((256, 3, 3, 2, 3), (128, 7, 7, 6, 0), (64, 4, 4, 0, 4))
LOCAL = ("x1_", "x2_", "wx", "wy", "wz", "w", "inv", "z0_", "z1_")
WHOLE = ("k", "b", "x1_", "x2_", "wx", "wy", "wz", "w", "inv")


def per_device(count_x, count_y, right_side, coefficient):
    nx, ny, nz = right_side.shape
    vmem = lambda *shape: pltpu.VMEM(shape, F32)
    rows3 = 2 * count_y
    scratch = {
        "k_in": vmem(2, nx * ny, 128),
        "b_in": vmem(2, nx * ny, 128),
        "load": pltpu.SemaphoreType.DMA((8,)),
        "half": vmem(2, 2, nx, 128),
        "idle": vmem(256, 8, 128),
        "to_1": pltpu.VMEM((256, 128), jnp.bfloat16),
        "from_1": pltpu.VMEM((128, 256), jnp.bfloat16),
        "sums": vmem(nx * ny // 4, nz),
        "doubled": vmem(ny // 2 + 4, 2, nx + 32, 128),
        "z0_3": vmem(5, 24, 128),
        "z1_3": vmem(5, 24, 128),
        "left3": vmem(count_x, rows3, 128),
        "w4": vmem(6, count_x, 8, 128),
        "inv4": vmem(count_x, 8, 128),
        "tiles4": vmem(count_x + 2, 8, 128),
        "grown3": vmem(3, LOW + rows3 + HIGH, 128),
        "answer": vmem(3, 24, 128),
        "z2": vmem((ny >> 2) + 8, (nx >> 2) + 8, 128),
        "z1out": vmem((ny >> 1) + 14, (nx >> 1) + 16, 128),
    }
    for name in ("to_2", "to_3", "to_4", "from_4", "from_3", "from_2"):
        scratch[name] = pltpu.VMEM((128, 128), jnp.bfloat16)
    for number, (lanes, halo, *depths) in enumerate(SHAPES):
        rows, planes, width = nx >> number, ny >> number, max(128, lanes)
        wide = number == 1
        full = (planes + 2 * halo, rows + (16 if wide else 8), width)
        scratch[f"b{number}"] = vmem(*full)
        for name, depth in zip(("k", "b", "xh"), depths):
            if not depth:
                continue
            tag = f"{name}{number}"
            scratch[tag] = vmem(*full)
            if not wide:
                scratch[tag + "_l"] = vmem(full[0], 8, width)
                scratch[tag + "_r"] = vmem(full[0], 8, width)
            scratch[tag + "_send"] = pltpu.SemaphoreType.DMA((1,))
            scratch[tag + "_recv"] = pltpu.SemaphoreType.DMA((8,))
        for name in LOCAL:
            scratch[f"{name}{number}"] = vmem(*full)
    for name in WHOLE:
        scratch[f"{name}3"] = vmem(count_x + 2, LOW + rows3 + HIGH, 128)
    for name in ("gk", "gb"):
        scratch[name + "_first"] = vmem(4, 8, 128)
        scratch[name + "_send"] = pltpu.SemaphoreType.DMA((1,))
        scratch[name + "_recv"] = pltpu.SemaphoreType.DMA((4 + count_y // 4,))

    names = ["right_side", "coefficient", "solution", "residual"] + list(scratch)
    shape = jax.ShapeDtypeStruct((nx * ny, nz), F32)
    found = pl.pallas_call(
        functools.partial(kernel, count_x, count_y, names),
        out_shape=(shape, shape),
        in_specs=[pl.BlockSpec(memory_space=pl.ANY)] * 2,
        out_specs=(pl.BlockSpec(memory_space=pl.ANY),) * 2,
        scratch_shapes=list(scratch.values()),
        compiler_params=pltpu.CompilerParams(
            collective_id=0, has_side_effects=True, vmem_limit_bytes=56 << 20
        ),
        name="vcycle",
    )(right_side.reshape(nx * ny, nz), coefficient.reshape(nx * ny, nz))
    return tuple(value.reshape(nx, ny, nz) for value in found)


def solution(mesh):
    spec = P("gx", "gy", None)
    step = functools.partial(per_device, mesh.shape["gx"], mesh.shape["gy"])
    return jax.shard_map(step, mesh=mesh, in_specs=(spec, spec), out_specs=(spec, spec), check_vma=False)
```
